32 devices in a mesh: ctx: 8 (over y, x, core), fsdp: 4 (over z).
Axes of the slice: x: 2, y: 2, z: 4, core: 2. Of those that a mesh axis runs over, the one named last changes fastest.
Arguments:
- tokens: bfloat16 [4, 1024, 2048], P('fsdp', 'ctx'), may hold values from -6 to 6
- cotangent: bfloat16 [4, 1024, 2048], P('fsdp', 'ctx'), may hold values from -6 to 6
- pairing: int32 [8, 2], replicated, may hold values from 0 to 15, as said below
- norm_attn: float32 [2048], P('fsdp'), may hold values from 0.5 to 1.5
- w_query: bfloat16 [2048, 2048], P('fsdp'), may hold values from -0.125 to 0.125
- w_key: bfloat16 [2048, 512], P('fsdp'), may hold values from -0.125 to 0.125
- w_value: bfloat16 [2048, 512], P('fsdp'), may hold values from -0.125 to 0.125
- w_out: bfloat16 [2048, 2048], P('fsdp'), may hold values from -0.5 to 0.5
- norm_mlp: float32 [2048], P('fsdp'), may hold values from 0.5 to 1.5
- w_gate: bfloat16 [2048, 8192], P('fsdp'), may hold values from -0.125 to 0.125
- w_up: bfloat16 [2048, 8192], P('fsdp'), may hold values from -0.125 to 0.125
- w_down: bfloat16 [8192, 2048], P('fsdp'), may hold values from -0.0625 to 0.0625
Outputs:
- output: bfloat16 [4, 1024, 2048], P('fsdp', 'ctx')
- d_tokens: bfloat16 [4, 1024, 2048], P('fsdp', 'ctx')
- grad_norm_attn: float32 [2048], P('fsdp')
- grad_query: float32 [2048, 2048], P('fsdp')
- grad_key: float32 [2048, 512], P('fsdp')
- grad_value: float32 [2048, 512], P('fsdp')
- grad_out: float32 [2048, 2048], P('fsdp')
- grad_norm_mlp: float32 [2048], P('fsdp')
- grad_gate: float32 [2048, 8192], P('fsdp')
- grad_up: float32 [2048, 8192], P('fsdp')
- grad_down: float32 [8192, 2048], P('fsdp')
The draws below stay inside these ranges and needn't reach their ends.
Inputs may be any that keep to these rules, and one draw needn't show every extreme that they name: `pairing`: each of the 16 block numbers appears exactly once; each row holds a block number b and its mirror 16 - 1 - b, in either order.
All inputs are finite; a program needn't handle non-finite values.
Results may differ from the reference program's by a relative error of at most 0.035.
Values may be sent and summed in bfloat16 or wider, within the bound.
A program may use at most 448 MiB of HBM per device.

```python
import math
import jax
import jax.numpy as jnp
from jax import lax

D = 2048
HEADS = 32
KV_HEADS = 8
HEAD_DIM = 64
FF = 8192
TOK_DEV = 128
KBLK = 512
LENGTH = 1024
SEQS = 4
BLOCKS = 16


def draw_pairing(key, part):
    count = BLOCKS // 2
    order = jax.random.permutation(jax.random.fold_in(key, 11), count).astype(jnp.int32)
    flipped = jax.random.randint(jax.random.fold_in(key, 12), (count,), 0, 2).astype(jnp.int32)
    mirror = (BLOCKS - 1 - order).astype(jnp.int32)
    first = jnp.where(flipped == 1, mirror, order)
    second = jnp.where(flipped == 1, order, mirror)
    return jnp.stack([first, second], axis=1).astype(jnp.int32)


def steps_of(key, dims, pieces, low, high):
    level, own = 1.0, jax.random.fold_in(key, 6)
    for axis_at, parts in pieces:
        draws = jnp.exp(jax.random.uniform(jax.random.fold_in(own, axis_at), (parts,), jnp.float32, low / len(pieces), high / len(pieces)))
        level = level * jnp.repeat(draws, dims[axis_at] // parts).reshape([-1 if axis == axis_at else 1 for axis in range(len(dims))])
    return level


def centred(key, dims, width, reach, cuts=(), kind=jnp.bfloat16):
    entries = jax.random.normal(key, dims, jnp.float32) * width
    if len(cuts) > 0:
        entries = steps_of(key, dims, cuts, -0.22, 0.18) * entries
    return jnp.clip(entries, min=-reach, max=reach).astype(kind)


def setup_inputs(seed: int = 0) -> dict:
    key_list = jax.random.split(jax.random.key(seed), 13)
    return {
        "tokens": centred(key_list[0], (SEQS, LENGTH, D), 1.0, 6.0, ((0, 4), (1, 8))),
        "cotangent": centred(key_list[1], (SEQS, LENGTH, D), 1.0, 6.0, ((0, 4), (1, 8))),
        "pairing": draw_pairing(jax.random.fold_in(key_list[12], 71), 0),
        "norm_attn": jnp.clip(1.0 + 0.1 * jax.random.normal(key_list[3], (D,), jnp.float32), 0.5, 1.5),
        "w_query": centred(key_list[4], (D, HEADS * HEAD_DIM), D ** -0.5, 0.125, ((0, 4),)),
        "w_key": centred(key_list[5], (D, KV_HEADS * HEAD_DIM), D ** -0.5, 0.125, ((0, 4),)),
        "w_value": centred(key_list[6], (D, KV_HEADS * HEAD_DIM), D ** -0.5, 0.125, ((0, 4),)),
        "w_out": centred(key_list[7], (HEADS * HEAD_DIM, D), (HEADS * HEAD_DIM // 16) ** -0.5, 0.5, ((0, 4),)),
        "norm_mlp": jnp.clip(1.0 + 0.1 * jax.random.normal(key_list[8], (D,), jnp.float32), 0.5, 1.5),
        "w_gate": centred(key_list[9], (D, FF), D ** -0.5, 0.125, ((0, 4),)),
        "w_up": centred(key_list[10], (D, FF), D ** -0.5, 0.125, ((0, 4),)),
        "w_down": centred(key_list[11], (FF, D), FF ** -0.5, 0.0625, ((0, 4),)),
    }


EPS = 1e-05
THETA = 500000.0

@jax.custom_vjp
def low(v):
    return lax.optimization_barrier(v.astype(jnp.bfloat16)).astype(jnp.float32)

@jax.custom_vjp
def low_back(v):
    return v

def low_keep(v):
    return (low(v), None)

def low_pass(kept, grad):
    return (grad,)

def back_keep(v):
    return (v, None)

def back_low(kept, grad):
    return (low(grad),)
low.defvjp(low_keep, low_pass)
low_back.defvjp(back_keep, back_low)

def frequencies(head_width):
    evens = jnp.arange(0, head_width, 2, dtype=jnp.float32)
    inverse = 1.0 / THETA ** (evens / head_width)
    wavelen = 2.0 * math.pi / inverse
    smooth = (8192.0 / wavelen - 1.0) / 3.0
    middle = (1.0 - smooth) * inverse / 32.0 + smooth * inverse
    return jnp.where(wavelen < 2048.0, inverse, jnp.where(wavelen > 8192.0, inverse / 32.0, middle))

def rotation(positions, head_width):
    angles = positions.astype(jnp.float32)[:, None] * frequencies(head_width)[None, :]
    cosine = jnp.concatenate([jnp.cos(angles), jnp.cos(angles)], axis=1)[:, None, :]
    sine = jnp.concatenate([jnp.sin(angles), jnp.sin(angles)], axis=1)[:, None, :]
    return (cosine, sine)

def rotate(tensor, cosine, sine):
    middle = tensor.shape[-1] // 2
    turned = jnp.concatenate([-tensor[..., middle:], tensor[..., :middle]], axis=-1)
    return tensor * cosine + turned * sine

def slot_positions(pairing, seq_length, block_len):
    flattened = pairing.reshape(-1).astype(jnp.int32)
    slots = jnp.arange(seq_length, dtype=jnp.int32)
    owning = slots // block_len
    labels = jnp.arange(flattened.shape[0], dtype=jnp.int32)
    anchor = lax.optimization_barrier(jnp.sum(jnp.where(owning[:, None] == labels[None, :], flattened[None, :], 0), axis=1))
    return (anchor * block_len + slots % block_len).astype(jnp.int32)

def matmul(left, right):
    return jnp.dot(left, right, precision=lax.Precision.HIGHEST)

def rms_norm(hidden_in, gain):
    return hidden_in * lax.rsqrt(lax.optimization_barrier(jnp.mean(hidden_in * hidden_in, axis=-1, keepdims=True)) + EPS) * gain

def layer(inputs, gain_attn, query_w, key_w, value_w, out_w, gain_mlp, gate_w, up_w, down_w, positions, cosine, sine):
    seq_length = inputs.shape[0]
    group_size = HEADS // KV_HEADS
    normed = low(rms_norm(inputs, gain_attn))
    query_pre = low_back(matmul(normed, query_w)).reshape(seq_length, HEADS, HEAD_DIM)
    key_pre = low_back(matmul(normed, key_w)).reshape(seq_length, KV_HEADS, HEAD_DIM)
    values = low(low_back(matmul(normed, value_w))).reshape(seq_length, KV_HEADS, HEAD_DIM)
    queries = low(rotate(query_pre, cosine, sine)).reshape(seq_length, KV_HEADS, group_size, HEAD_DIM)
    keys = low(rotate(key_pre, cosine, sine))

    def block(item):
        query_blk, pos_blk = item
        logits = low_back(jnp.einsum('qhgd,khd->hgqk', query_blk, keys, precision=lax.Precision.HIGHEST))
        allowed = positions[None, :] <= pos_blk[:, None]
        scores = jnp.where(allowed, logits * HEAD_DIM ** (-0.5), -1e+30)
        largest = lax.optimization_barrier(jnp.max(scores, axis=-1, keepdims=True))
        expo = jnp.where(allowed, jnp.exp(scores - largest), 0.0)
        probs = low(expo / lax.optimization_barrier(jnp.sum(expo, axis=-1, keepdims=True)))
        return jnp.einsum('hgqk,khd->qhgd', probs, values, precision=lax.Precision.HIGHEST)
    count = seq_length // KBLK
    attended = lax.map(jax.checkpoint(block), (queries.reshape(count, KBLK, KV_HEADS, group_size, HEAD_DIM), positions.reshape(count, KBLK)))
    attended = low(low_back(attended.reshape(seq_length, HEADS * HEAD_DIM)))
    resid = inputs + low_back(matmul(attended, out_w))
    normed_mlp = low(rms_norm(resid, gain_mlp))
    gate = low_back(matmul(normed_mlp, gate_w))
    up_val = low_back(matmul(normed_mlp, up_w))
    hidden = low(jax.nn.silu(gate) * up_val)
    return resid + low_back(matmul(hidden, down_w))

def reference(tokens, cotangent, pairing, norm_attn, w_query, w_key, w_value, w_out, norm_mlp, w_gate, w_up, w_down):
    seq_length = tokens.shape[1]
    positions = slot_positions(pairing, seq_length, TOK_DEV // 2)
    cosine, sine = rotation(positions, HEAD_DIM)
    params = tuple((w.astype(jnp.float32) for w in (norm_attn, w_query, w_key, w_value, w_out, norm_mlp, w_gate, w_up, w_down)))

    def one(totals, item):
        sequence, grad_output = item

        def run(inputs, *weights):
            return layer(inputs, *weights, positions, cosine, sine)
        result, pull = jax.vjp(run, sequence.astype(jnp.float32), *params)
        grads = pull(grad_output.astype(jnp.float32))
        totals = tuple((acc + new for acc, new in zip(totals, grads[1:])))
        return (totals, (result.astype(jnp.bfloat16), grads[0].astype(jnp.bfloat16)))
    zeros = tuple((jnp.zeros_like(p) for p in params))
    totals, (outputs, d_inputs) = lax.scan(one, zeros, (tokens, cotangent))
    return (outputs, d_inputs, totals[0], totals[1], totals[2], totals[3], totals[4], totals[5], totals[6], totals[7], totals[8])
```

```python
import math

import jax
import jax.numpy as jnp
from jax import lax
from jax.sharding import PartitionSpec as P

HEAD_DIM = 64


EPS = 1e-05
THETA = 500000.0


def frequencies(head_width):
    evens = jnp.arange(0, head_width, 2, dtype=jnp.float32)
    inverse = 1.0 / THETA ** (evens / head_width)
    wavelen = 2.0 * math.pi / inverse
    smooth = (8192.0 / wavelen - 1.0) / 3.0
    middle = (1.0 - smooth) * inverse / 32.0 + smooth * inverse
    return jnp.where(wavelen < 2048.0, inverse, jnp.where(wavelen > 8192.0, inverse / 32.0, middle))


def rotation(positions, head_width):
    angles = positions.astype(jnp.float32)[:, None] * frequencies(head_width)[None, :]
    cosine = jnp.concatenate([jnp.cos(angles), jnp.cos(angles)], axis=1)[:, None, :]
    sine = jnp.concatenate([jnp.sin(angles), jnp.sin(angles)], axis=1)[:, None, :]
    return (cosine, sine)


def rotate(tensor, cosine, sine):
    middle = tensor.shape[-1] // 2
    turned = jnp.concatenate([-tensor[..., middle:], tensor[..., :middle]], axis=-1)
    return tensor * cosine + turned * sine


def unrotate(gradient, cosine, sine):
    middle = gradient.shape[-1] // 2
    moved = gradient * sine
    back_turn = jnp.concatenate([moved[..., middle:], -moved[..., :middle]], axis=-1)
    return gradient * cosine + back_turn


def slot_positions(pairing, seq_length, block_len):
    flattened = pairing.reshape(-1)
    slots = jnp.arange(seq_length, dtype=jnp.int32)
    owning = slots // block_len
    labels = jnp.arange(flattened.shape[0], dtype=jnp.int32)
    anchor = jnp.sum(jnp.where(owning[:, None] == labels[None, :], flattened[None, :], 0), axis=1)
    return anchor * block_len + slots % block_len


def product(left, right):
    return jnp.dot(left, right, preferred_element_type=jnp.float32)


def product_t(left, right):
    return lax.dot_general(
        left, right, (((1,), (1,)), ((), ())), preferred_element_type=jnp.float32
    )


def tokens_t(left, right):
    return lax.dot_general(
        left, right, (((0,), (0,)), ((), ())), preferred_element_type=jnp.float32
    )


def norm_back(upstream, gain, unit, scale):
    weighted = upstream * gain
    return scale * (weighted - unit * jnp.mean(weighted * unit, axis=1, keepdims=True))


def gather(array, axis):
    return lax.all_gather(array, axis, axis=0, tiled=True)


def scatter_sum(array, axis):
    return lax.psum_scatter(array, axis, scatter_dimension=0, tiled=True)


def einsum(spec, left, right):
    return jnp.einsum(spec, left, right, preferred_element_type=jnp.float32)


def exchange(pieces, axis):
    count = pieces.shape[0]
    me = lax.axis_index(axis)
    parts = [pieces[0]] * count
    own = lax.dynamic_index_in_dim(pieces, me, 0, keepdims=True)
    received = [own]
    for shift in range(1, count):
        target = lax.rem(me + shift, count)
        piece = lax.dynamic_index_in_dim(pieces, target, 0, keepdims=True)
        received.append(lax.ppermute(piece, axis, [(i, (i + shift) % count) for i in range(count)]))
    out = jnp.zeros_like(pieces)
    for shift, piece in enumerate(received):
        source = lax.rem(me + count - shift, count)
        out = lax.dynamic_update_slice_in_dim(out, piece, source, 0)
    return out


def on_device(
    tokens,
    cotangent,
    pairing,
    norm_attn,
    w_query,
    w_key,
    w_value,
    w_out,
    norm_mlp,
    w_gate,
    w_up,
    w_down,
):
    n_ctx, n_fsdp = lax.axis_size("ctx"), lax.axis_size("fsdp")
    ctx = lax.axis_index("ctx")
    own_tokens = tokens[0]
    tok_rows, width = own_tokens.shape
    length = tok_rows * n_ctx
    rows_model = w_gate.shape[0]
    low = jnp.bfloat16

    query_width = w_query.shape[1] // n_ctx
    heads_kv = w_key.shape[1] // HEAD_DIM
    kv_here = max(1, heads_kv // n_ctx)
    sharers = max(1, n_ctx // heads_kv)
    kv_width = kv_here * HEAD_DIM
    group = query_width // kv_width
    kv_start = (ctx // sharers) * kv_width

    def columns(matrix, start, size):
        return lax.dynamic_slice_in_dim(matrix, start, size, 1)

    joined = jnp.concatenate(
        [
            columns(w_query, ctx * query_width, query_width),
            columns(w_key, kv_start, kv_width),
            columns(w_value, kv_start, kv_width),
        ],
        axis=1,
    )
    w_joined = gather(joined, "fsdp")
    sequence = gather(own_tokens, "ctx")
    gains = lax.all_gather(jnp.stack([norm_attn, norm_mlp]), "fsdp", axis=1, tiled=True)
    gain_attn, gain_mlp = gains[0], gains[1]
    out_width = width // n_ctx
    w_out_cols = gather(columns(w_out, ctx * out_width, out_width), "fsdp")
    w_out_rows = lax.all_to_all(w_out_cols, "ctx", 0, 1, tiled=True)

    ff_rows = w_down.shape[0]
    chunk = ff_rows // n_ctx
    pieces = jnp.stack(
        [w.reshape(rows_model, n_fsdp, n_ctx, chunk) for w in (w_gate, w_up)], axis=0
    )
    pieces = lax.dynamic_index_in_dim(pieces, ctx, 3, keepdims=False)
    pieces = exchange(pieces.transpose(2, 0, 1, 3), "fsdp")
    pieces = pieces.transpose(1, 0, 2, 3).reshape(1, 2, width, chunk)
    w_pair = gather(pieces, "ctx")
    down_cut = w_down.reshape(n_ctx, chunk, width)
    upstream = cotangent[0]
    upstream_all = gather(upstream, "fsdp")

    all_pos = slot_positions(pairing, length, tok_rows // 2)
    cosine, sine = rotation(all_pos, HEAD_DIM)
    factor = HEAD_DIM ** (-0.5)
    wide = sequence.astype(jnp.float32)
    scale_attn = lax.rsqrt(jnp.mean(wide * wide, axis=1, keepdims=True) + EPS)
    normed_attn = (wide * scale_attn * gain_attn).astype(low)
    projected = product(normed_attn, w_joined)
    query_pre = projected[:, :query_width].reshape(length, -1, HEAD_DIM)
    key_pre = projected[:, query_width : query_width + kv_width].reshape(length, -1, HEAD_DIM)
    values = projected[:, query_width + kv_width :].reshape(length, -1, HEAD_DIM).astype(low)
    queries = rotate(query_pre, cosine, sine).astype(low).reshape(length, kv_here, group, HEAD_DIM)
    keys = rotate(key_pre, cosine, sine).astype(low)
    logits = einsum("qhgd,khd->hgqk", queries, keys)
    allowed = all_pos[None, :] <= all_pos[:, None]
    scores = jnp.where(allowed, logits * factor, -1e30)
    largest = jnp.max(scores, axis=-1, keepdims=True)
    expo = jnp.where(allowed, jnp.exp(scores - largest), 0.0)
    probs = expo / jnp.sum(expo, axis=-1, keepdims=True)
    probs_low = probs.astype(low)
    attended = einsum("hgqk,khd->qhgd", probs_low, values)
    attended_low = attended.reshape(length, query_width).astype(low)
    projected_out = scatter_sum(product(attended_low, w_out_rows).astype(low), "ctx")
    inputs = own_tokens.astype(jnp.float32)
    resid = inputs + projected_out.astype(jnp.float32)

    scale_mlp = lax.rsqrt(jnp.mean(resid * resid, axis=1, keepdims=True) + EPS)
    unit_mlp = resid * scale_mlp
    normed_mlp = gather((unit_mlp * gain_mlp).astype(low), "fsdp")
    both = einsum("td,cgdf->gctf", normed_mlp, w_pair)
    gate_pre, up_pre = both[0], both[1]
    sigma = jax.nn.sigmoid(gate_pre)
    swish = gate_pre * sigma
    hidden = (swish * up_pre).astype(low)
    d_hidden = einsum("td,cfd->ctf", upstream_all, down_cut)
    d_gate = (d_hidden * up_pre * sigma * (1.0 + gate_pre * (1.0 - sigma))).astype(low)
    d_up = (d_hidden * swish).astype(low)
    d_pair = jnp.stack([d_gate, d_up])
    d_normed_part = einsum("gctf,cgdf->td", d_pair, w_pair).astype(low)
    d_normed_mlp = scatter_sum(d_normed_part, "fsdp").astype(jnp.float32)
    down_part = einsum("ctf,cfd->td", hidden, down_cut).astype(low)
    output = resid + scatter_sum(down_part, "fsdp").astype(jnp.float32)
    grad_down = lax.psum(einsum("ctf,td->cfd", hidden, upstream_all).astype(low), "ctx")
    grad_pair = einsum("td,gctf->cgdf", normed_mlp, d_pair).astype(low)
    grad_pair = scatter_sum(grad_pair, "ctx").reshape(2, n_fsdp, rows_model, chunk)
    grad_pair = exchange(grad_pair.transpose(1, 0, 2, 3), "fsdp")
    grad_pair = lax.all_gather(grad_pair, "ctx", axis=0)
    grad_pair = grad_pair.transpose(2, 3, 1, 0, 4).reshape(2, rows_model, -1).astype(jnp.float32)

    gain_mlp_term = jnp.sum(d_normed_mlp * unit_mlp, axis=0)
    d_resid = upstream.astype(jnp.float32) + norm_back(d_normed_mlp, gain_mlp, unit_mlp, scale_mlp)
    d_resid_low = gather(d_resid.astype(low), "ctx")

    d_attended = product_t(d_resid_low, w_out_rows).astype(low)
    d_attended = d_attended.reshape(length, kv_here, group, HEAD_DIM)
    d_probs = einsum("qhgd,khd->hgqk", d_attended, values)
    delta = jnp.sum(probs * d_probs, axis=-1, keepdims=True)
    d_score = (probs * (d_probs - delta) * factor).astype(low)
    d_query_rot = einsum("hgqk,khd->qhgd", d_score, keys)
    d_key_rot = einsum("hgqk,qhgd->khd", d_score, queries)
    d_value = einsum("hgqk,qhgd->khd", probs_low, d_attended)
    d_query = unrotate(d_query_rot.reshape(length, -1, HEAD_DIM), cosine, sine)
    d_key = unrotate(d_key_rot, cosine, sine)
    d_joined = jnp.concatenate(
        [part.reshape(length, -1).astype(low) for part in (d_query, d_key, d_value)], axis=1
    )
    d_normed_part = product_t(d_joined, w_joined).astype(low)
    d_normed_attn = scatter_sum(d_normed_part, "ctx").astype(jnp.float32)
    grad_out = tokens_t(attended_low, d_resid_low).astype(low)
    grad_out = lax.all_to_all(grad_out, "ctx", 1, 0, tiled=True)
    grad_joined = tokens_t(normed_attn, d_joined).astype(low)
    grad_attn = scatter_sum(jnp.concatenate([grad_joined, grad_out], axis=1), "fsdp")
    grad_attn = lax.all_gather(grad_attn, "ctx", axis=0).astype(jnp.float32)

    def spread(part):
        return part.transpose(1, 0, 2).reshape(part.shape[1], -1)

    def shared(part):
        return jnp.sum(part.reshape(n_ctx // sharers, sharers, *part.shape[1:]), axis=1)

    at = query_width
    grad_query = spread(grad_attn[:, :, :at])
    grad_key = spread(shared(grad_attn[:, :, at : at + kv_width]))
    grad_value = spread(shared(grad_attn[:, :, at + kv_width : at + 2 * kv_width]))
    grad_out = spread(grad_attn[:, :, at + 2 * kv_width :])

    unit_attn = inputs * lax.rsqrt(jnp.mean(inputs * inputs, axis=1, keepdims=True) + EPS)
    scale_own = lax.rsqrt(jnp.mean(inputs * inputs, axis=1, keepdims=True) + EPS)
    gain_attn_term = jnp.sum(d_normed_attn * unit_attn, axis=0)
    d_inputs = d_resid + norm_back(d_normed_attn, gain_attn, unit_attn, scale_own)
    terms = lax.psum(jnp.stack([gain_attn_term, gain_mlp_term]), ("ctx", "fsdp"))
    terms = lax.dynamic_slice_in_dim(terms, lax.axis_index("fsdp") * rows_model, rows_model, 1)
    return (
        output.astype(low)[None],
        d_inputs.astype(low)[None],
        terms[0],
        grad_query,
        grad_key,
        grad_value,
        grad_out,
        terms[1],
        grad_pair[0],
        grad_pair[1],
        grad_down.reshape(ff_rows, width).astype(jnp.float32),
    )


def solution(mesh):
    return jax.shard_map(
        on_device,
        mesh=mesh,
        in_specs=(
            P("fsdp", "ctx", None),
            P("fsdp", "ctx", None),
            P(),
            P("fsdp"),
            P("fsdp", None),
            P("fsdp", None),
            P("fsdp", None),
            P("fsdp", None),
            P("fsdp"),
            P("fsdp", None),
            P("fsdp", None),
            P("fsdp", None),
        ),
        out_specs=(
            P("fsdp", "ctx", None),
            P("fsdp", "ctx", None),
            P("fsdp"),
            P("fsdp", None),
            P("fsdp", None),
            P("fsdp", None),
            P("fsdp", None),
            P("fsdp"),
            P("fsdp", None),
            P("fsdp", None),
            P("fsdp", None),
        ),
        check_vma=False,
    )
```

```python
import functools
import math

import jax
import jax.numpy as jnp
from jax import lax
from jax.experimental import pallas as pl
from jax.experimental.pallas import tpu as pltpu
from jax.sharding import PartitionSpec as P

HEAD_DIM = 64


EPS = 1e-05
THETA = 500000.0


def frequencies(head_width):
    evens = jnp.arange(0, head_width, 2, dtype=jnp.float32)
    inverse = 1.0 / THETA ** (evens / head_width)
    wavelen = 2.0 * math.pi / inverse
    smooth = (8192.0 / wavelen - 1.0) / 3.0
    middle = (1.0 - smooth) * inverse / 32.0 + smooth * inverse
    return jnp.where(wavelen < 2048.0, inverse, jnp.where(wavelen > 8192.0, inverse / 32.0, middle))


def rotation(positions, head_width):
    angles = positions.astype(jnp.float32)[:, None] * frequencies(head_width)[None, :]
    cosine = jnp.concatenate([jnp.cos(angles), jnp.cos(angles)], axis=1)[:, None, :]
    sine = jnp.concatenate([jnp.sin(angles), jnp.sin(angles)], axis=1)[:, None, :]
    return (cosine, sine)


def rotate(tensor, cosine, sine):
    middle = tensor.shape[-1] // 2
    turned = jnp.concatenate([-tensor[..., middle:], tensor[..., :middle]], axis=-1)
    return tensor * cosine + turned * sine


def unrotate(gradient, cosine, sine):
    middle = gradient.shape[-1] // 2
    moved = gradient * sine
    back_turn = jnp.concatenate([moved[..., middle:], -moved[..., :middle]], axis=-1)
    return gradient * cosine + back_turn


def slot_positions(pairing, seq_length, block_len):
    flattened = pairing.reshape(-1)
    slots = jnp.arange(seq_length, dtype=jnp.int32)
    owning = slots // block_len
    labels = jnp.arange(flattened.shape[0], dtype=jnp.int32)
    anchor = jnp.sum(jnp.where(owning[:, None] == labels[None, :], flattened[None, :], 0), axis=1)
    return anchor * block_len + slots % block_len


def product(left, right):
    return jnp.dot(left, right, preferred_element_type=jnp.float32)


def product_t(left, right):
    return lax.dot_general(
        left, right, (((1,), (1,)), ((), ())), preferred_element_type=jnp.float32
    )


def tokens_t(left, right):
    return lax.dot_general(
        left, right, (((0,), (0,)), ((), ())), preferred_element_type=jnp.float32
    )


LOW = jnp.bfloat16
MESH = pl.DeviceIdType.MESH
ANY = pl.BlockSpec(memory_space=pl.ANY)
VMEM = pl.BlockSpec(memory_space=pltpu.VMEM)


def norm_back(upstream, gain, unit, scale):
    weighted = upstream * gain
    return scale * (weighted - unit * jnp.mean(weighted * unit, axis=1, keepdims=True))


def gather(array, axis):
    return lax.all_gather(array, axis, axis=0, tiled=True)


def scatter_sum(array, axis):
    return lax.psum_scatter(array, axis, scatter_dimension=0, tiled=True)


def einsum(spec, left, right):
    return jnp.einsum(spec, left, right, preferred_element_type=jnp.float32)


def by_permutes(piece_for, axis):
    count, me = lax.axis_size(axis), lax.axis_index(axis)
    own = piece_for(me)
    rows = own.shape[0]
    out = jnp.zeros((count * rows, *own.shape[1:]), own.dtype)
    out = lax.dynamic_update_slice_in_dim(out, own, me * rows, 0)
    for shift in range(1, count):
        piece = piece_for(lax.rem(me + shift, count))
        piece = lax.ppermute(piece, axis, [(i, (i + shift) % count) for i in range(count)])
        out = lax.dynamic_update_slice_in_dim(out, piece, lax.rem(me + count - shift, count) * rows, 0)
    return out


def swap_order(array, first, second):
    size = array.shape[1] // (first * second)
    parts = []
    for b in range(second):
        for a in range(first):
            at = (a * second + b) * size
            parts.append(array[:, at : at + size])
    return jnp.concatenate(parts, axis=1)


class Links:
    def __init__(self, n_ctx, n_fsdp, send_sems, recv_sems):
        self.n_ctx, self.n_fsdp = n_ctx, n_fsdp
        self.ctx, self.fsdp = lax.axis_index("ctx"), lax.axis_index("fsdp")
        self.send_sems, self.recv_sems = send_sems, recv_sems
        self.used = 0
        core = self.ctx % 2
        flips = [self.flip(d) for d in range(1, n_ctx.bit_length() - 1)]
        backward = flips[::-1]
        self.order = [(1 - core) * a + core * b for a, b in zip(flips, backward)]
        self.sibling = self.flip(0)

    def flip(self, digit):
        return 2**digit * (1 - 2 * ((self.ctx // 2**digit) % 2))

    def greet(self, cube=False, plane=False, line=False, whole_line=False):
        barrier = pltpu.get_barrier_semaphore()
        count = 0

        def hail(ctx, fsdp):
            pl.semaphore_signal(barrier, inc=1, device_id=(ctx, fsdp), device_id_type=MESH)

        if plane:
            for shift in range(1, self.n_ctx):
                hail(lax.rem(self.ctx + shift, self.n_ctx), self.fsdp)
            count += self.n_ctx - 1
        elif cube:
            for step in self.order + [self.sibling]:
                hail(self.ctx + step, self.fsdp)
            count += len(self.order) + 1
        if whole_line:
            for shift in range(1, self.n_fsdp):
                hail(self.ctx, lax.rem(self.fsdp + shift, self.n_fsdp))
            count += self.n_fsdp - 1
        if line and not whole_line:
            for step in (-1, 1):
                inside = jnp.logical_and(self.fsdp + step >= 0, self.fsdp + step < self.n_fsdp)

                @pl.when(inside)
                def _():
                    hail(self.ctx, self.fsdp + step)

            ends = jnp.logical_or(self.fsdp == 0, self.fsdp == self.n_fsdp - 1)
            pl.when(ends)(lambda: pl.semaphore_wait(barrier, count + 1))
            pl.when(jnp.logical_not(ends))(lambda: pl.semaphore_wait(barrier, count + 2))
        else:
            pl.semaphore_wait(barrier, count)

    def copy(self, source, target, ctx, fsdp):
        slot = self.used
        self.used += 1
        return pltpu.make_async_remote_copy(
            src_ref=source,
            dst_ref=target,
            send_sem=self.send_sems.at[slot],
            recv_sem=self.recv_sems.at[slot],
            device_id=(ctx, fsdp),
            device_id_type=MESH,
        )


def rows_of(ref, index, rows):
    return ref.at[pl.ds(pl.multiple_of(index * rows, rows), rows)]


def cube_gather(links, ref, rows, between=None):
    held, sent = [0], []
    to_sibling = []

    def share(offset):
        block = rows_of(ref, links.ctx + offset, rows)
        copy = links.copy(block, block, links.ctx + links.sibling, links.fsdp)
        copy.start()
        to_sibling.append(copy)

    for stage, step in enumerate(links.order):
        copies = []
        for offset in held:
            block = rows_of(ref, links.ctx + offset, rows)
            copy = links.copy(block, block, links.ctx + step, links.fsdp)
            copy.start()
            copies.append(copy)
        for offset in held if stage == 0 else held[len(held) // 2 :]:
            share(offset)
        if stage == 0 and between is not None:
            between()
        for copy in copies:
            copy.wait_recv()
        sent += copies
        held = held + [offset + step for offset in held]
    for offset in held[len(held) // 2 :] if links.order else held:
        share(offset)
    for copy in to_sibling:
        copy.wait_recv()
    for copy in sent + to_sibling:
        copy.wait_send()


def cube_slots(n_ctx):
    return n_ctx - 1


def cube_sum(links, part, stage_ref, land, rows):
    offsets = [0]
    theirs = [0]
    for step, other in zip(links.order, links.order[::-1]):
        offsets = offsets + [offset + step for offset in offsets]
        theirs = theirs + [offset + other for offset in theirs]
    sent = []
    copies = []
    for at, offset in enumerate(theirs):
        source = rows_of(part, links.ctx + links.sibling + offset, rows)
        copy = links.copy(source, land.at[pl.ds(at * rows, rows)], links.ctx + links.sibling, links.fsdp)
        copy.start()
        copies.append(copy)
    sums = {}
    stage_at, land_at = 0, len(offsets)
    pending = copies
    first = True
    for level in range(len(links.order) + 1):
        last = level == len(links.order)
        count = len(offsets)
        half = count // 2
        step = None if last else links.order[len(links.order) - 1 - level]
        onward = []
        for at in list(range(half, count)) + list(range(half)) if not last else [0]:
            pending[at].wait_recv()
            if first:
                base = rows_of(part, links.ctx + offsets[at], rows)[...].astype(jnp.float32)
            else:
                base = sums[at]
            start = pending_land + at * rows if not first else at * rows
            total = base + land[pl.ds(start, rows), :].astype(jnp.float32)
            if not last and at >= half:
                slot = stage_ref.at[pl.ds(stage_at * rows, rows)]
                slot[...] = total.astype(LOW)
                copy = links.copy(
                    slot, land.at[pl.ds((land_at + at - half) * rows, rows)], links.ctx + step, links.fsdp
                )
                copy.start()
                onward.append(copy)
                stage_at += 1
            else:
                sums[at] = total
        sent += pending
        pending = onward
        pending_land = land_at * rows
        land_at += half
        offsets = offsets[:half] if not last else offsets
        first = False
    for copy in sent:
        copy.wait_send()
    return sums[0]


def line_gather(links, refs, rows):
    count, me = links.n_fsdp, links.fsdp
    sends = []
    for hop in range(count - 1):
        receives = []
        for ref, size in zip(refs, rows):
            up_block = rows_of(ref, me - hop, size)
            down_block = rows_of(ref, me + hop, size)
            up = links.copy(up_block, up_block, links.ctx, me + 1)
            down = links.copy(down_block, down_block, links.ctx, me - 1)
            up_ok = jnp.logical_and(me >= hop, me < count - 1)
            down_ok = jnp.logical_and(me <= count - 1 - hop, me > 0)
            pl.when(up_ok)(up.start)
            pl.when(down_ok)(down.start)
            sends += [(up_ok, up), (down_ok, down)]
            receives += [(me >= hop + 1, up), (me <= count - 2 - hop, down)]
        for ok, copy in receives:
            pl.when(ok)(copy.wait_recv)

    def finish():
        for ok, copy in sends:
            pl.when(ok)(copy.wait_send)

    return finish


def line_sum(links, part, stage_ref, land, total, rows):
    count, me = links.n_fsdp, links.fsdp
    flows = []
    for hop in range(count - 1):
        for side in (0, 1):
            goal = count - 1 - hop if side == 0 else hop
            slot = (side * (count - 1) + hop) * rows
            landing = land.at[pl.ds(slot, rows)]
            staging = stage_ref.at[pl.ds(slot, rows)]
            onward = links.copy(staging, landing, links.ctx, me + 1 if side == 0 else me - 1)
            fed = me > 0 if side == 0 else me < count - 1
            passes = me < goal if side == 0 else me > goal
            flows.append((side, goal, landing, staging, onward, fed, passes))
    for side, goal, landing, staging, onward, fed, passes in flows:

        @pl.when(jnp.logical_and(passes, jnp.logical_not(fed)))
        def _():
            staging[...] = part[pl.ds(goal * rows, rows), :]
            onward.start()

    def steps():
        total[...] = rows_of(part, me, rows)[...].astype(jnp.float32)
        lower = me < count // 2
        for near in (0, 1):

            @pl.when(lower if near == 0 else jnp.logical_not(lower))
            def _():
                for hop in range(count - 1):
                    for way in (near, 1 - near):
                        side, goal, landing, staging, onward, fed, passes = flows[2 * hop + way]

                        @pl.when(jnp.logical_and(passes, fed))
                        def _():
                            onward.wait_recv()
                            own = part[pl.ds(goal * rows, rows), :].astype(jnp.float32)
                            staging[...] = (own + landing[...].astype(jnp.float32)).astype(LOW)
                            onward.start()

        for side, goal, landing, staging, onward, fed, passes in flows:

            @pl.when(jnp.logical_and(me == goal, fed))
            def _():
                onward.wait_recv()
                total[...] += landing[...].astype(jnp.float32)

        for side, goal, landing, staging, onward, fed, passes in flows:
            pl.when(passes)(onward.wait_send)

    return steps


def communicate(kernel, collective_id, name, operands, in_specs, outs, out_specs, scratch, copies, busy):
    return pl.pallas_call(
        kernel,
        out_shape=outs,
        in_specs=in_specs,
        out_specs=out_specs,
        scratch_shapes=scratch
        + [pltpu.SemaphoreType.DMA((copies,)), pltpu.SemaphoreType.DMA((copies,))],
        compiler_params=pltpu.CompilerParams(
            collective_id=collective_id, has_side_effects=True, vmem_limit_bytes=48 << 20
        ),
        cost_estimate=pl.CostEstimate(flops=0, bytes_accessed=busy * 3_000_000, transcendentals=0),
        name=name,
    )(*operands)


def front_kernel(
    n_ctx,
    n_fsdp,
    own,
    w_query,
    kv,
    w_out,
    gains,
    seq,
    q_all,
    kv_all,
    gains_all,
    cols_all,
    out_rows,
    local_sems,
    send_sems,
    recv_sems,
):
    links = Links(n_ctx, n_fsdp, send_sems, recv_sems)
    rows, weight_rows, query_width = own.shape[0], kv.shape[0], q_all.shape[1]
    head_rows, out_width = out_rows.shape[0], cols_all.shape[1]

    def cut(ref, size):
        return ref.at[:, pl.ds(pl.multiple_of(links.ctx * size, size), size)]

    local = [
        (own, rows_of(seq, links.ctx, rows)),
        (cut(w_query, query_width), rows_of(q_all, links.fsdp, weight_rows)),
        (kv, rows_of(kv_all, links.fsdp, weight_rows)),
        (gains, rows_of(gains_all, links.fsdp, gains.shape[0])),
        (cut(w_out, out_width), rows_of(cols_all, links.fsdp, weight_rows)),
    ]
    local = [pltpu.make_async_copy(a, b, local_sems.at[i]) for i, (a, b) in enumerate(local)]
    for copy in local:
        copy.start()
    links.greet(plane=True, line=True)
    for copy in local:
        copy.wait()
    ends = []

    def between():
        refs = [gains_all, q_all, kv_all, cols_all]
        ends.append(line_gather(links, refs, [gains.shape[0]] + [weight_rows] * 3))

    cube_gather(links, seq, rows, between)
    column = cut(out_rows, out_width)
    mine = pltpu.make_async_copy(rows_of(cols_all, links.ctx, head_rows), column, local_sems.at[0])
    mine.start()
    copies = []
    for shift in range(1, n_ctx):
        target = lax.rem(links.ctx + shift, n_ctx)
        copy = links.copy(rows_of(cols_all, target, head_rows), column, target, links.fsdp)
        copy.start()
        copies.append(copy)
    for copy in copies:
        copy.wait()
    mine.wait()
    for end in ends:
        end()


def front(n_ctx, n_fsdp, own, w_query, kv, w_out, gains):
    rows, width = own.shape
    weight_rows = kv.shape[0]
    total = weight_rows * n_fsdp
    query_width, out_width = w_query.shape[1] // n_ctx, width // n_ctx
    shape = lambda *dims: jax.ShapeDtypeStruct(dims, LOW)
    return communicate(
        functools.partial(front_kernel, n_ctx, n_fsdp),
        1,
        "front",
        (own, w_query, kv, w_out, gains),
        [ANY] * 5,
        [
            shape(rows * n_ctx, width),
            shape(total, query_width),
            shape(total, kv.shape[1]),
            jax.ShapeDtypeStruct((gains.shape[0] * n_fsdp, gains.shape[1]), jnp.float32),
            shape(total, out_width),
            shape(total // n_ctx, width),
        ],
        [ANY] * 6,
        [pltpu.SemaphoreType.DMA((5,))],
        2 * (n_ctx - 1) + 8 * (n_fsdp - 1),
        50,
    )


def middle_kernel(
    n_ctx, n_fsdp, part, own, gain, resid, normed, staged, land, send_sems, recv_sems
):
    links = Links(n_ctx, n_fsdp, send_sems, recv_sems)
    rows = own.shape[0]
    links.greet(cube=True, line=True)
    value = cube_sum(links, part, staged, land, rows) + own[...].astype(jnp.float32)
    resid[...] = value
    scale = lax.rsqrt(jnp.mean(value * value, axis=1, keepdims=True) + EPS)
    block = swap_order((value * scale * gain[...]).astype(LOW), n_fsdp, n_ctx)
    rows_of(normed, links.fsdp, rows)[...] = block
    line_gather(links, [normed], [rows])()


def middle(n_ctx, n_fsdp, part, own, gain):
    rows, width = own.shape
    return communicate(
        functools.partial(middle_kernel, n_ctx, n_fsdp),
        2,
        "middle",
        (part, own, gain),
        [VMEM] * 3,
        [
            jax.ShapeDtypeStruct((rows, width), jnp.float32),
            jax.ShapeDtypeStruct((rows * n_fsdp, width), LOW),
        ],
        [VMEM] * 2,
        [
            pltpu.VMEM(((n_ctx // 2 - 1) * rows, width), LOW),
            pltpu.VMEM(((n_ctx - 1) * rows, width), LOW),
        ],
        n_ctx - 1 + 2 * (n_fsdp - 1),
        60,
    )


def turn_kernel(
    n_ctx, n_fsdp, part, upstream, resid, gain, d_resid, seq, term, staged, land, total, send_sems, recv_sems
):
    links = Links(n_ctx, n_fsdp, send_sems, recv_sems)
    rows = upstream.shape[0]
    links.greet(cube=True, line=True)
    line_sum(links, part, staged, land, total, rows)()
    d_normed = swap_order(total[...], n_ctx, n_fsdp)
    value = resid[...]
    scale = lax.rsqrt(jnp.mean(value * value, axis=1, keepdims=True) + EPS)
    unit = value * scale
    term[...] = jnp.sum(d_normed * unit, axis=0, keepdims=True)
    value = upstream[...].astype(jnp.float32) + norm_back(d_normed, gain[...], unit, scale)
    d_resid[...] = value
    rows_of(seq, links.ctx, rows)[...] = value.astype(LOW)
    cube_gather(links, seq, rows)


def turn(n_ctx, n_fsdp, part, upstream, resid, gain):
    rows, width = upstream.shape
    return communicate(
        functools.partial(turn_kernel, n_ctx, n_fsdp),
        3,
        "turn",
        (part, upstream, resid, gain),
        [VMEM] * 4,
        [
            jax.ShapeDtypeStruct((rows, width), jnp.float32),
            jax.ShapeDtypeStruct((rows * n_ctx, width), LOW),
            jax.ShapeDtypeStruct((1, width), jnp.float32),
        ],
        [VMEM] * 3,
        [
            pltpu.VMEM((2 * (n_fsdp - 1) * rows, width), LOW),
            pltpu.VMEM((2 * (n_fsdp - 1) * rows, width), LOW),
            pltpu.VMEM((rows, width), jnp.float32),
        ],
        n_ctx - 1 + 2 * (n_fsdp - 1),
        65,
    )


def last_kernel(
    n_ctx,
    n_fsdp,
    part,
    down_part,
    own,
    resid,
    d_resid,
    gain,
    d_own,
    output,
    term,
    staged,
    land,
    down_staged,
    down_land,
    total,
    send_sems,
    recv_sems,
):
    links = Links(n_ctx, n_fsdp, send_sems, recv_sems)
    rows = own.shape[0]
    links.greet(cube=True, line=True)
    finish = line_sum(links, down_part, down_staged, down_land, total, rows)
    d_normed = cube_sum(links, part, staged, land, rows)
    value = own[...].astype(jnp.float32)
    scale = lax.rsqrt(jnp.mean(value * value, axis=1, keepdims=True) + EPS)
    unit = value * scale
    term[...] = jnp.sum(d_normed * unit, axis=0, keepdims=True)
    d_own[...] = (d_resid[...] + norm_back(d_normed, gain[...], unit, scale)).astype(LOW)
    finish()
    output[...] = (resid[...] + total[...]).astype(LOW)


def last(n_ctx, n_fsdp, part, down_part, own, resid, d_resid, gain):
    rows, width = own.shape
    return communicate(
        functools.partial(last_kernel, n_ctx, n_fsdp),
        4,
        "last",
        (part, down_part, own, resid, d_resid, gain),
        [VMEM] * 6,
        [
            jax.ShapeDtypeStruct((rows, width), LOW),
            jax.ShapeDtypeStruct((rows, width), LOW),
            jax.ShapeDtypeStruct((1, width), jnp.float32),
        ],
        [VMEM] * 3,
        [
            pltpu.VMEM(((n_ctx // 2 - 1) * rows, width), LOW),
            pltpu.VMEM(((n_ctx - 1) * rows, width), LOW),
            pltpu.VMEM((2 * (n_fsdp - 1) * rows, width), LOW),
            pltpu.VMEM((2 * (n_fsdp - 1) * rows, width), LOW),
            pltpu.VMEM((rows, width), jnp.float32),
        ],
        n_ctx - 1 + 2 * (n_fsdp - 1),
        45,
    )


def tail_kernel(
    n_ctx,
    n_fsdp,
    gate,
    up,
    down,
    joined,
    out_part,
    gate_all,
    up_all,
    down_all,
    attn_all,
    attn_part,
    staged,
    land,
    total,
    attn_low,
    local_sems,
    send_sems,
    recv_sems,
):
    links = Links(n_ctx, n_fsdp, send_sems, recv_sems)
    strip, ff_rows = gate.shape[0] // n_fsdp, gate.shape[1]
    down_rows, rows = down.shape[0], joined.shape[0] // n_fsdp
    head_rows, joined_width = out_part.shape[0], joined.shape[1]
    out_width = attn_part.shape[1] - joined_width

    def place(ref, ctx, fsdp):
        return ref.at[
            pl.ds(pl.multiple_of(ctx * strip, strip), strip),
            pl.ds(pl.multiple_of(fsdp * ff_rows, ff_rows), ff_rows),
        ]

    def out_column(ctx):
        return out_part.at[:, pl.ds(pl.multiple_of(ctx * out_width, out_width), out_width)]

    def out_place(ctx):
        return attn_part.at[
            pl.ds(pl.multiple_of(ctx * head_rows, head_rows), head_rows), pl.ds(joined_width, out_width)
        ]

    local = [
        (down, rows_of(down_all, links.ctx, down_rows)),
        (rows_of(gate, links.fsdp, strip), place(gate_all, links.ctx, links.fsdp)),
        (rows_of(up, links.fsdp, strip), place(up_all, links.ctx, links.fsdp)),
        (joined, attn_part.at[:, pl.ds(0, joined_width)]),
        (out_column(links.ctx), out_place(links.ctx)),
    ]
    local = [pltpu.make_async_copy(a, b, local_sems.at[i]) for i, (a, b) in enumerate(local)]
    for copy in local:
        copy.start()
    links.greet(plane=True, line=True, whole_line=True)
    to_shards, to_plane = [], []
    for shift in range(1, n_fsdp):
        target = lax.rem(links.fsdp + shift, n_fsdp)
        for source, goal in ((gate, gate_all), (up, up_all)):
            copy = links.copy(
                rows_of(source, target, strip), place(goal, links.ctx, links.fsdp), links.ctx, target
            )
            copy.start()
            to_shards.append(copy)
    for shift in range(1, n_ctx):
        target = lax.rem(links.ctx + shift, n_ctx)
        copy = links.copy(out_column(target), out_place(links.ctx), target, links.fsdp)
        copy.start()
        to_plane.append(copy)
    for copy in local:
        copy.wait()
    cube_gather(links, down_all, down_rows)
    for copy in to_plane + to_shards:
        copy.wait()
    finish = line_sum(links, attn_part, staged, land, total, rows)
    cube_gather(links, gate_all, strip, finish)
    cube_gather(links, up_all, strip)
    attn_low[...] = total[...].astype(LOW)
    mine = pltpu.make_async_copy(attn_low, rows_of(attn_all, links.ctx, rows), local_sems.at[0])
    mine.start()
    mine.wait()
    cube_gather(links, attn_all, rows)


def tail(n_ctx, n_fsdp, gate, up, down, joined, out_part):
    strip, ff_rows = gate.shape[0] // n_fsdp, gate.shape[1]
    rows = joined.shape[0] // n_fsdp
    attn_width = joined.shape[1] + out_part.shape[1] // n_ctx
    shape = lambda *dims: jax.ShapeDtypeStruct(dims, LOW)
    return communicate(
        functools.partial(tail_kernel, n_ctx, n_fsdp),
        5,
        "tail",
        (gate, up, down, joined, out_part),
        [ANY] * 5,
        [
            shape(strip * n_ctx, ff_rows * n_fsdp),
            shape(strip * n_ctx, ff_rows * n_fsdp),
            shape(down.shape[0] * n_ctx, down.shape[1]),
            shape(rows * n_ctx, attn_width),
        ],
        [ANY] * 4,
        [
            pltpu.VMEM((rows * n_fsdp, attn_width), LOW),
            pltpu.VMEM((2 * (n_fsdp - 1) * rows, attn_width), LOW),
            pltpu.VMEM((2 * (n_fsdp - 1) * rows, attn_width), LOW),
            pltpu.VMEM((rows, attn_width), jnp.float32),
            pltpu.VMEM((rows, attn_width), LOW),
            pltpu.SemaphoreType.DMA((5,)),
        ],
        5 * (n_ctx - 1) + 4 * (n_fsdp - 1),
        150,
    )


def spread_kernel(parts, widths, gathered, *outs):
    at = 0
    for out, width, sharers in zip(outs, widths, parts):
        pieces = []
        for i in range(0, gathered.shape[0], sharers):
            piece = gathered[i, :, at : at + width].astype(jnp.float32)
            for j in range(1, sharers):
                piece = piece + gathered[i + j, :, at : at + width].astype(jnp.float32)
            pieces.append(piece)
        out[...] = jnp.concatenate(pieces, axis=1)
        at += width


def spread(gathered, widths, sharers):
    n_ctx, rows, joined = gathered.shape
    step = 2 * max(sharers)
    tile = min(rows, 256)
    return pl.pallas_call(
        functools.partial(spread_kernel, sharers, widths),
        grid=(n_ctx // step, rows // tile),
        in_specs=[pl.BlockSpec((step, tile, joined), lambda i, j: (i, j, 0))],
        out_specs=[
            pl.BlockSpec((tile, step // s * w), lambda i, j: (j, i)) for w, s in zip(widths, sharers)
        ],
        out_shape=[
            jax.ShapeDtypeStruct((rows, n_ctx // s * w), jnp.float32) for w, s in zip(widths, sharers)
        ],
        compiler_params=pltpu.CompilerParams(vmem_limit_bytes=32 << 20),
        name="spread",
    )(gathered)


def on_device(
    tokens,
    cotangent,
    pairing,
    norm_attn,
    w_query,
    w_key,
    w_value,
    w_out,
    norm_mlp,
    w_gate,
    w_up,
    w_down,
):
    n_ctx, n_fsdp = lax.axis_size("ctx"), lax.axis_size("fsdp")
    ctx = lax.axis_index("ctx")
    own_tokens = tokens[0]
    tok_rows, width = own_tokens.shape
    length = tok_rows * n_ctx
    rows_model = w_gate.shape[0]
    low = LOW

    query_width = w_query.shape[1] // n_ctx
    heads_kv = w_key.shape[1] // HEAD_DIM
    kv_here = max(1, heads_kv // n_ctx)
    sharers = max(1, n_ctx // heads_kv)
    kv_width = kv_here * HEAD_DIM
    group = query_width // kv_width
    kv_start = (ctx // sharers) * kv_width

    def columns(matrix, start, size):
        return lax.dynamic_slice_in_dim(matrix, start, size, 1)

    kv = jnp.concatenate([columns(w_key, kv_start, kv_width), columns(w_value, kv_start, kv_width)], axis=1)
    gains = jnp.zeros((8, rows_model), jnp.float32).at[0].set(norm_attn).at[1].set(norm_mlp)
    sequence, w_q, w_kv, gains, _, w_out_rows = front(
        n_ctx, n_fsdp, own_tokens, w_query, kv, w_out, gains
    )
    gains = gains.reshape(n_fsdp, 8, rows_model)
    gain_attn, gain_mlp = gains[:, 0].reshape(1, -1), gains[:, 1].reshape(1, -1)
    out_width = width // n_ctx

    ff_rows = w_down.shape[0]
    strip = rows_model // n_ctx
    upstream = cotangent[0]
    w_gate, w_up, upstream, sequence = lax.optimization_barrier((w_gate, w_up, upstream, sequence))

    def strips(matrix):
        piece = lambda fsdp: lax.dynamic_slice(matrix, (ctx * strip, fsdp * ff_rows), (strip, ff_rows))
        return by_permutes(piece, "fsdp")

    gate_full = gather(strips(w_gate), "ctx")
    up_full = gather(strips(w_up), "ctx")
    upstream_all = by_permutes(lambda fsdp: upstream, "fsdp")

    all_pos = slot_positions(pairing, length, tok_rows // 2)
    cosine, sine = rotation(all_pos, HEAD_DIM)
    factor = HEAD_DIM ** (-0.5)
    wide = sequence.astype(jnp.float32)
    scale_attn = lax.rsqrt(jnp.mean(wide * wide, axis=1, keepdims=True) + EPS)
    normed_attn = (wide * scale_attn * gain_attn).astype(low)
    w_joined = jnp.concatenate([w_q, w_kv], axis=1)
    projected = product(normed_attn, w_joined)
    query_pre = projected[:, :query_width].reshape(length, -1, HEAD_DIM)
    key_pre = projected[:, query_width : query_width + kv_width].reshape(length, -1, HEAD_DIM)
    values = projected[:, query_width + kv_width :].reshape(length, -1, HEAD_DIM).astype(low)
    queries = rotate(query_pre, cosine, sine).astype(low).reshape(length, kv_here, group, HEAD_DIM)
    keys = rotate(key_pre, cosine, sine).astype(low)
    logits = einsum("qhgd,khd->hgqk", queries, keys)
    allowed = all_pos[None, :] <= all_pos[:, None]
    scores = jnp.where(allowed, logits * factor, -1e30)
    largest = jnp.max(scores, axis=-1, keepdims=True)
    expo = jnp.where(allowed, jnp.exp(scores - largest), 0.0)
    probs = expo / jnp.sum(expo, axis=-1, keepdims=True)
    probs_low = probs.astype(low)
    attended = einsum("hgqk,khd->qhgd", probs_low, values)
    attended_low = attended.reshape(length, query_width).astype(low)
    resid, normed_mlp = middle(
        n_ctx, n_fsdp, product(attended_low, w_out_rows).astype(low), own_tokens, gain_mlp
    )

    gate_pre = product(normed_mlp, gate_full)
    up_pre = product(normed_mlp, up_full)
    sigma = jax.nn.sigmoid(gate_pre)
    swish = gate_pre * sigma
    hidden = (swish * up_pre).astype(low)
    d_hidden = product_t(upstream_all, w_down)
    d_gate = (d_hidden * up_pre * sigma * (1.0 + gate_pre * (1.0 - sigma))).astype(low)
    d_up = (d_hidden * swish).astype(low)
    d_part = (product_t(d_gate, gate_full) + product_t(d_up, up_full)).astype(low)
    grad_gate = tokens_t(normed_mlp, d_gate).astype(low)
    grad_up = tokens_t(normed_mlp, d_up).astype(low)
    d_part, grad_gate, grad_up = lax.optimization_barrier((d_part, grad_gate, grad_up))
    d_resid, d_resid_low, gain_mlp_term = turn(n_ctx, n_fsdp, d_part, upstream, resid, gain_mlp)
    grad_gate, grad_up = scatter_sum(grad_gate, "ctx"), scatter_sum(grad_up, "ctx")
    grad_down = scatter_sum(tokens_t(hidden, upstream_all).astype(low), "ctx")

    d_attended = product_t(d_resid_low, w_out_rows).astype(low)
    d_attended = d_attended.reshape(length, kv_here, group, HEAD_DIM)
    d_probs = einsum("qhgd,khd->hgqk", d_attended, values)
    delta = jnp.sum(probs * d_probs, axis=-1, keepdims=True)
    d_score = (probs * (d_probs - delta) * factor).astype(low)
    d_query_rot = einsum("hgqk,khd->qhgd", d_score, keys)
    d_key_rot = einsum("hgqk,qhgd->khd", d_score, queries)
    d_value = einsum("hgqk,qhgd->khd", probs_low, d_attended)
    d_query = unrotate(d_query_rot.reshape(length, -1, HEAD_DIM), cosine, sine)
    d_key = unrotate(d_key_rot, cosine, sine)
    d_joined = jnp.concatenate(
        [part.reshape(length, -1).astype(low) for part in (d_query, d_key, d_value)], axis=1
    )
    d_inputs, output, gain_attn_term = last(
        n_ctx,
        n_fsdp,
        product_t(d_joined, w_joined).astype(low),
        product(hidden, w_down).astype(low),
        own_tokens,
        resid,
        d_resid,
        gain_attn,
    )
    grad_out = tokens_t(attended_low, d_resid_low).astype(low)
    grad_joined = tokens_t(normed_attn, d_joined).astype(low)
    grad_gate, grad_up, grad_down, grad_attn = tail(
        n_ctx, n_fsdp, grad_gate, grad_up, grad_down, grad_joined, grad_out
    )
    grad_attn = grad_attn.reshape(n_ctx, rows_model, -1)
    grad_query, grad_key, grad_value, grad_out = spread(
        grad_attn, (query_width, kv_width, kv_width, out_width), (1, sharers, sharers, 1)
    )

    terms = lax.psum(jnp.concatenate([gain_attn_term, gain_mlp_term]), ("ctx", "fsdp"))
    terms = lax.dynamic_slice_in_dim(terms, lax.axis_index("fsdp") * rows_model, rows_model, 1)
    return (
        output[None],
        d_inputs[None],
        terms[0],
        grad_query,
        grad_key,
        grad_value,
        grad_out,
        terms[1],
        grad_gate.astype(jnp.float32),
        grad_up.astype(jnp.float32),
        grad_down.astype(jnp.float32),
    )


def solution(mesh):
    return jax.shard_map(
        on_device,
        mesh=mesh,
        in_specs=(
            P("fsdp", "ctx", None),
            P("fsdp", "ctx", None),
            P(),
            P("fsdp"),
            P("fsdp", None),
            P("fsdp", None),
            P("fsdp", None),
            P("fsdp", None),
            P("fsdp"),
            P("fsdp", None),
            P("fsdp", None),
            P("fsdp", None),
        ),
        out_specs=(
            P("fsdp", "ctx", None),
            P("fsdp", "ctx", None),
            P("fsdp"),
            P("fsdp", None),
            P("fsdp", None),
            P("fsdp", None),
            P("fsdp", None),
            P("fsdp"),
            P("fsdp", None),
            P("fsdp", None),
            P("fsdp", None),
        ),
        check_vma=False,
    )
```

```python
import functools
import math

import jax
import jax.numpy as jnp
from jax import lax
from jax.experimental import pallas as pl
from jax.experimental.pallas import tpu as pltpu
from jax.sharding import PartitionSpec as P

HEAD_DIM = 64


EPS = 1e-05
THETA = 500000.0


def frequencies(head_width):
    evens = jnp.arange(0, head_width, 2, dtype=jnp.float32)
    inverse = 1.0 / THETA ** (evens / head_width)
    wavelen = 2.0 * math.pi / inverse
    smooth = (8192.0 / wavelen - 1.0) / 3.0
    middle = (1.0 - smooth) * inverse / 32.0 + smooth * inverse
    return jnp.where(wavelen < 2048.0, inverse, jnp.where(wavelen > 8192.0, inverse / 32.0, middle))


def rotation(positions, head_width):
    angles = positions.astype(jnp.float32)[:, None] * frequencies(head_width)[None, :]
    cosine = jnp.concatenate([jnp.cos(angles), jnp.cos(angles)], axis=1)[:, None, :]
    sine = jnp.concatenate([jnp.sin(angles), jnp.sin(angles)], axis=1)[:, None, :]
    return (cosine, sine)


def rotate(tensor, cosine, sine):
    middle = tensor.shape[-1] // 2
    turned = jnp.concatenate([-tensor[..., middle:], tensor[..., :middle]], axis=-1)
    return tensor * cosine + turned * sine


def unrotate(gradient, cosine, sine):
    middle = gradient.shape[-1] // 2
    moved = gradient * sine
    back_turn = jnp.concatenate([moved[..., middle:], -moved[..., :middle]], axis=-1)
    return gradient * cosine + back_turn


def slot_positions(pairing, seq_length, block_len):
    flattened = pairing.reshape(-1)
    slots = jnp.arange(seq_length, dtype=jnp.int32)
    owning = slots // block_len
    labels = jnp.arange(flattened.shape[0], dtype=jnp.int32)
    anchor = jnp.sum(jnp.where(owning[:, None] == labels[None, :], flattened[None, :], 0), axis=1)
    return anchor * block_len + slots % block_len


def product(left, right):
    return jnp.dot(left, right, preferred_element_type=jnp.float32)


def product_t(left, right):
    return lax.dot_general(
        left, right, (((1,), (1,)), ((), ())), preferred_element_type=jnp.float32
    )


def tokens_t(left, right):
    return lax.dot_general(
        left, right, (((0,), (0,)), ((), ())), preferred_element_type=jnp.float32
    )


LOW = jnp.bfloat16
MESH = pl.DeviceIdType.MESH
ANY = pl.BlockSpec(memory_space=pl.ANY)
VMEM = pl.BlockSpec(memory_space=pltpu.VMEM)


def norm_back(upstream, gain, unit, scale):
    weighted = upstream * gain
    return scale * (weighted - unit * jnp.mean(weighted * unit, axis=1, keepdims=True))


def gather(array, axis):
    return lax.all_gather(array, axis, axis=0, tiled=True)


def scatter_sum(array, axis):
    return lax.psum_scatter(array, axis, scatter_dimension=0, tiled=True)


def einsum(spec, left, right):
    return jnp.einsum(spec, left, right, preferred_element_type=jnp.float32)


def by_permutes(piece_for, axis):
    count, me = lax.axis_size(axis), lax.axis_index(axis)
    own = piece_for(me)
    rows = own.shape[0]
    out = jnp.zeros((count * rows, *own.shape[1:]), own.dtype)
    out = lax.dynamic_update_slice_in_dim(out, own, me * rows, 0)
    for shift in range(1, count):
        piece = piece_for(lax.rem(me + shift, count))
        piece = lax.ppermute(piece, axis, [(i, (i + shift) % count) for i in range(count)])
        out = lax.dynamic_update_slice_in_dim(out, piece, lax.rem(me + count - shift, count) * rows, 0)
    return out


def swap_order(array, first, second):
    size = array.shape[1] // (first * second)
    parts = []
    for b in range(second):
        for a in range(first):
            at = (a * second + b) * size
            parts.append(array[:, at : at + size])
    return jnp.concatenate(parts, axis=1)


class Links:
    def __init__(self, n_ctx, n_fsdp, send_sems, recv_sems):
        self.n_ctx, self.n_fsdp = n_ctx, n_fsdp
        self.ctx, self.fsdp = lax.axis_index("ctx"), lax.axis_index("fsdp")
        self.send_sems, self.recv_sems = send_sems, recv_sems
        self.used = 0
        core = self.ctx % 2
        flips = [self.flip(d) for d in range(1, n_ctx.bit_length() - 1)]
        backward = flips[::-1]
        self.order = [(1 - core) * a + core * b for a, b in zip(flips, backward)]
        self.sibling = self.flip(0)

    def flip(self, digit):
        return 2**digit * (1 - 2 * ((self.ctx // 2**digit) % 2))

    def greet(self, cube=False, plane=False, line=False, whole_line=False):
        barrier = pltpu.get_barrier_semaphore()
        count = 0

        def hail(ctx, fsdp):
            pl.semaphore_signal(barrier, inc=1, device_id=(ctx, fsdp), device_id_type=MESH)

        if plane:
            for shift in range(1, self.n_ctx):
                hail(lax.rem(self.ctx + shift, self.n_ctx), self.fsdp)
            count += self.n_ctx - 1
        elif cube:
            for step in self.order + [self.sibling]:
                hail(self.ctx + step, self.fsdp)
            count += len(self.order) + 1
        if whole_line:
            for shift in range(1, self.n_fsdp):
                hail(self.ctx, lax.rem(self.fsdp + shift, self.n_fsdp))
            count += self.n_fsdp - 1
        if line and not whole_line:
            for step in (-1, 1):
                inside = jnp.logical_and(self.fsdp + step >= 0, self.fsdp + step < self.n_fsdp)

                @pl.when(inside)
                def _():
                    hail(self.ctx, self.fsdp + step)

            ends = jnp.logical_or(self.fsdp == 0, self.fsdp == self.n_fsdp - 1)
            pl.when(ends)(lambda: pl.semaphore_wait(barrier, count + 1))
            pl.when(jnp.logical_not(ends))(lambda: pl.semaphore_wait(barrier, count + 2))
        else:
            pl.semaphore_wait(barrier, count)

    def copy(self, source, target, ctx, fsdp):
        slot = self.used
        self.used += 1
        return pltpu.make_async_remote_copy(
            src_ref=source,
            dst_ref=target,
            send_sem=self.send_sems.at[slot],
            recv_sem=self.recv_sems.at[slot],
            device_id=(ctx, fsdp),
            device_id_type=MESH,
        )


def rows_of(ref, index, rows):
    return ref.at[pl.ds(pl.multiple_of(index * rows, rows), rows)]


def in_turns(*walks):
    for walk in walks:
        next(walk, None)


def finish(*walks):
    for walk in walks:
        for _ in walk:
            pass


def cube_gather(links, ref, rows):
    held, sent, shared = [0], [], []

    def send(offset, step):
        block = rows_of(ref, links.ctx + offset, rows)
        copy = links.copy(block, block, links.ctx + step, links.fsdp)
        copy.start()
        return copy

    fresh = held
    for step in links.order:
        copies = [send(offset, step) for offset in held]
        shared += [send(offset, links.sibling) for offset in fresh]
        yield
        for copy in copies:
            copy.wait_recv()
        sent += copies
        fresh = [offset + step for offset in held]
        held = held + fresh
    shared += [send(offset, links.sibling) for offset in fresh]
    yield
    for copy in shared:
        copy.wait_recv()
    for copy in sent + shared:
        copy.wait_send()


def in_rows(rows, body):
    size = math.gcd(rows, 64)

    def step(at, carry):
        body(pl.multiple_of(at * size, size), size)
        return carry

    lax.fori_loop(0, rows // size, step, 0)


def cube_sum(links, part, staged, land, acc, rows):
    offsets, theirs = [0], [0]
    for step, other in zip(links.order, links.order[::-1]):
        offsets = offsets + [offset + step for offset in offsets]
        theirs = theirs + [offset + other for offset in theirs]
    wide = jnp.float32
    sent, pending = [], []
    for at, offset in enumerate(theirs):
        source = rows_of(part, links.ctx + links.sibling + offset, rows)
        target = land.at[pl.ds(at * rows, rows)]
        copy = links.copy(source, target, links.ctx + links.sibling, links.fsdp)
        copy.start()
        pending.append(copy)
    yield
    stage_at, land_from, land_at = 0, 0, len(offsets)
    for level in range(len(links.order) + 1):
        count = len(offsets)
        half = count // 2
        onward = []
        for at in list(range(half, count)) + list(range(half)):
            pending[at].wait_recv()
            first, place = level == 0, (land_from + at) * rows
            goes = at >= half and count > 1

            def add(start, size, at=at, place=place, first=first, goes=goes, slot=stage_at * rows):
                landed = land[pl.ds(place + start, size), :].astype(wide)
                if first:
                    base = (links.ctx + offsets[at]) * rows
                    mine = part[pl.ds(pl.multiple_of(base + start, size), size), :].astype(wide)
                else:
                    mine = acc[pl.ds(at * rows + start, size), :]
                if goes:
                    staged[pl.ds(slot + start, size), :] = (mine + landed).astype(LOW)
                else:
                    acc[pl.ds(at * rows + start, size), :] = mine + landed

            in_rows(rows, add)
            if goes:
                source = staged.at[pl.ds(stage_at * rows, rows)]
                target = land.at[pl.ds((land_at + at - half) * rows, rows)]
                step = links.order[len(links.order) - 1 - level]
                copy = links.copy(source, target, links.ctx + step, links.fsdp)
                copy.start()
                onward.append(copy)
                stage_at += 1
        sent += pending
        pending, land_from = onward, land_at
        land_at += half
        offsets = offsets[: max(half, 1)]
        if level < len(links.order):
            yield
    for copy in sent:
        copy.wait_send()


def cube_scratch(n_ctx, rows, width):
    return [
        pltpu.VMEM((max(1, n_ctx // 2 - 1) * rows, width), LOW),
        pltpu.VMEM(((n_ctx - 1) * rows, width), LOW),
        pltpu.VMEM((max(1, n_ctx // 4) * rows, width), jnp.float32),
    ]


def line_gather(links, refs, rows):
    count, me = links.n_fsdp, links.fsdp
    sends = []
    for hop in range(count - 1):
        receives = []
        for ref, size in zip(refs, rows):
            up_block = rows_of(ref, me - hop, size)
            down_block = rows_of(ref, me + hop, size)
            up = links.copy(up_block, up_block, links.ctx, me + 1)
            down = links.copy(down_block, down_block, links.ctx, me - 1)
            up_ok = jnp.logical_and(me >= hop, me < count - 1)
            down_ok = jnp.logical_and(me <= count - 1 - hop, me > 0)
            pl.when(up_ok)(up.start)
            pl.when(down_ok)(down.start)
            sends += [(up_ok, up), (down_ok, down)]
            receives += [(me >= hop + 1, up), (me <= count - 2 - hop, down)]
        yield
        for ok, copy in receives:
            pl.when(ok)(copy.wait_recv)
    for ok, copy in sends:
        pl.when(ok)(copy.wait_send)


def line_sum(links, part, staged, land, total, rows):
    count, me = links.n_fsdp, links.fsdp
    flows = []
    for hop in range(count - 1):
        for side in (0, 1):
            goal = count - 1 - hop if side == 0 else hop
            slot = (side * (count - 1) + hop) * rows
            landing = land.at[pl.ds(slot, rows)]
            staging = staged.at[pl.ds(slot, rows)]
            onward = links.copy(staging, landing, links.ctx, me + 1 if side == 0 else me - 1)
            fed = me > 0 if side == 0 else me < count - 1
            passes = me < goal if side == 0 else me > goal
            flows.append((goal * rows, slot, onward, fed, passes, me == goal))
    for base, slot, onward, fed, passes, _ in flows:

        @pl.when(jnp.logical_and(passes, jnp.logical_not(fed)))
        def _():
            staged[pl.ds(slot, rows), :] = part[pl.ds(base, rows), :]
            onward.start()

    total[...] = rows_of(part, me, rows)[...].astype(jnp.float32)
    lower = me < count // 2
    for hop in range(count - 1):
        yield
        for near in (0, 1):

            @pl.when(lower if near == 0 else jnp.logical_not(lower))
            def _():
                for way in (near, 1 - near):
                    base, slot, onward, fed, passes, _ = flows[2 * hop + way]

                    @pl.when(jnp.logical_and(passes, fed))
                    def _():
                        onward.wait_recv()

                        def add(start, size):
                            own = part[pl.ds(base + start, size), :].astype(jnp.float32)
                            landed = land[pl.ds(slot + start, size), :].astype(jnp.float32)
                            staged[pl.ds(slot + start, size), :] = (own + landed).astype(LOW)

                        in_rows(rows, add)
                        onward.start()

    yield
    for base, slot, onward, fed, passes, mine in flows:

        @pl.when(jnp.logical_and(mine, fed))
        def _():
            onward.wait_recv()

            def add(start, size):
                landed = land[pl.ds(slot + start, size), :].astype(jnp.float32)
                total[pl.ds(start, size), :] += landed

            in_rows(rows, add)

    for base, slot, onward, fed, passes, _ in flows:
        pl.when(passes)(onward.wait_send)


def line_scratch(n_fsdp, rows, width):
    return [
        pltpu.VMEM((2 * (n_fsdp - 1) * rows, width), LOW),
        pltpu.VMEM((2 * (n_fsdp - 1) * rows, width), LOW),
        pltpu.VMEM((rows, width), jnp.float32),
    ]


def communicate(kernel, collective_id, name, operands, in_specs, outs, out_specs, scratch, copies, busy):
    return pl.pallas_call(
        kernel,
        out_shape=outs,
        in_specs=in_specs,
        out_specs=out_specs,
        scratch_shapes=scratch
        + [pltpu.SemaphoreType.DMA((copies,)), pltpu.SemaphoreType.DMA((copies,))],
        compiler_params=pltpu.CompilerParams(
            collective_id=collective_id, has_side_effects=True, vmem_limit_bytes=48 << 20
        ),
        cost_estimate=pl.CostEstimate(flops=0, bytes_accessed=busy * 3_000_000, transcendentals=0),
        name=name,
    )(*operands)


def front_kernel(
    n_ctx,
    n_fsdp,
    own,
    w_query,
    kv,
    w_out,
    gains,
    seq,
    q_all,
    kv_all,
    gains_all,
    cols_all,
    out_rows,
    local_sems,
    send_sems,
    recv_sems,
):
    links = Links(n_ctx, n_fsdp, send_sems, recv_sems)
    rows, weight_rows, query_width = own.shape[0], kv.shape[0], q_all.shape[1]
    head_rows, out_width = out_rows.shape[0], cols_all.shape[1]

    def cut(ref, size):
        return ref.at[:, pl.ds(pl.multiple_of(links.ctx * size, size), size)]

    local = [
        (own, rows_of(seq, links.ctx, rows)),
        (cut(w_query, query_width), rows_of(q_all, links.fsdp, weight_rows)),
        (kv, rows_of(kv_all, links.fsdp, weight_rows)),
        (gains, rows_of(gains_all, links.fsdp, gains.shape[0])),
        (cut(w_out, out_width), rows_of(cols_all, links.fsdp, weight_rows)),
    ]
    local = [pltpu.make_async_copy(a, b, local_sems.at[i]) for i, (a, b) in enumerate(local)]
    for copy in local:
        copy.start()
    links.greet(plane=True, line=True)
    for copy in local:
        copy.wait()
    plane = cube_gather(links, seq, rows)
    line = line_gather(links, [gains_all, q_all, kv_all], [gains.shape[0], weight_rows, weight_rows])
    later = line_gather(links, [cols_all], [weight_rows])
    in_turns(plane, line, later, plane, line, plane, later, line, later)
    finish(later)
    column = cut(out_rows, out_width)
    mine = pltpu.make_async_copy(rows_of(cols_all, links.ctx, head_rows), column, local_sems.at[0])
    mine.start()
    copies = []
    for shift in range(1, n_ctx):
        target = lax.rem(links.ctx + shift, n_ctx)
        copy = links.copy(rows_of(cols_all, target, head_rows), column, target, links.fsdp)
        copy.start()
        copies.append(copy)
    finish(plane, line)
    for copy in copies:
        copy.wait()
    mine.wait()


def front(n_ctx, n_fsdp, own, w_query, kv, w_out, gains):
    rows, width = own.shape
    weight_rows = kv.shape[0]
    total = weight_rows * n_fsdp
    query_width, out_width = w_query.shape[1] // n_ctx, width // n_ctx
    shape = lambda *dims: jax.ShapeDtypeStruct(dims, LOW)
    return communicate(
        functools.partial(front_kernel, n_ctx, n_fsdp),
        1,
        "front",
        (own, w_query, kv, w_out, gains),
        [ANY] * 5,
        [
            shape(rows * n_ctx, width),
            shape(total, query_width),
            shape(total, kv.shape[1]),
            jax.ShapeDtypeStruct((gains.shape[0] * n_fsdp, gains.shape[1]), jnp.float32),
            shape(total, out_width),
            shape(total // n_ctx, width),
        ],
        [ANY] * 6,
        [pltpu.SemaphoreType.DMA((5,))],
        2 * (n_ctx - 1) + 8 * (n_fsdp - 1),
        50,
    )


def middle_kernel(
    n_ctx, n_fsdp, part, own, gain, resid, normed, staged, land, acc, send_sems, recv_sems
):
    links = Links(n_ctx, n_fsdp, send_sems, recv_sems)
    rows = own.shape[0]
    links.greet(cube=True, line=True)
    finish(cube_sum(links, part, staged, land, acc, rows))
    value = acc[pl.ds(0, rows), :] + own[...].astype(jnp.float32)
    resid[...] = value
    scale = lax.rsqrt(jnp.mean(value * value, axis=1, keepdims=True) + EPS)
    block = swap_order((value * scale * gain[...]).astype(LOW), n_fsdp, n_ctx)
    rows_of(normed, links.fsdp, rows)[...] = block
    finish(line_gather(links, [normed], [rows]))


def middle(n_ctx, n_fsdp, part, own, gain):
    rows, width = own.shape
    return communicate(
        functools.partial(middle_kernel, n_ctx, n_fsdp),
        2,
        "middle",
        (part, own, gain),
        [VMEM] * 3,
        [
            jax.ShapeDtypeStruct((rows, width), jnp.float32),
            jax.ShapeDtypeStruct((rows * n_fsdp, width), LOW),
        ],
        [VMEM] * 2,
        cube_scratch(n_ctx, rows, width),
        n_ctx - 1 + 2 * (n_fsdp - 1),
        60,
    )


def turn_kernel(
    n_ctx,
    n_fsdp,
    part,
    down_part,
    upstream,
    resid,
    gain,
    d_resid,
    seq,
    down,
    term,
    line_staged,
    line_land,
    total,
    staged,
    land,
    acc,
    send_sems,
    recv_sems,
):
    links = Links(n_ctx, n_fsdp, send_sems, recv_sems)
    rows, down_rows = upstream.shape[0], down.shape[0]
    links.greet(cube=True, line=True)
    line = line_sum(links, part, line_staged, line_land, total, rows)
    plane = cube_sum(links, down_part, staged, land, acc, down_rows)
    in_turns(line, plane, plane, line, line, plane)
    finish(line)
    d_normed = swap_order(total[...], n_ctx, n_fsdp)
    value = resid[...]
    scale = lax.rsqrt(jnp.mean(value * value, axis=1, keepdims=True) + EPS)
    unit = value * scale
    term[...] = jnp.sum(d_normed * unit, axis=0, keepdims=True)
    value = upstream[...].astype(jnp.float32) + norm_back(d_normed, gain[...], unit, scale)
    d_resid[...] = value
    rows_of(seq, links.ctx, rows)[...] = value.astype(LOW)
    spread_out = cube_gather(links, seq, rows)
    in_turns(spread_out)
    finish(plane)
    down[...] = acc[pl.ds(0, down_rows), :].astype(LOW)
    finish(spread_out)


def turn(n_ctx, n_fsdp, part, down_part, upstream, resid, gain):
    rows, width = upstream.shape
    down_rows = down_part.shape[0] // n_ctx
    return communicate(
        functools.partial(turn_kernel, n_ctx, n_fsdp),
        3,
        "turn",
        (part, down_part, upstream, resid, gain),
        [VMEM] * 5,
        [
            jax.ShapeDtypeStruct((rows, width), jnp.float32),
            jax.ShapeDtypeStruct((rows * n_ctx, width), LOW),
            jax.ShapeDtypeStruct((down_rows, width), LOW),
            jax.ShapeDtypeStruct((1, width), jnp.float32),
        ],
        [VMEM] * 4,
        line_scratch(n_fsdp, rows, width) + cube_scratch(n_ctx, down_rows, width),
        2 * (n_ctx - 1) + 2 * (n_fsdp - 1),
        65,
    )


def last_kernel(
    n_ctx,
    n_fsdp,
    part,
    down_part,
    own,
    resid,
    d_resid,
    gain,
    d_own,
    output,
    term,
    staged,
    land,
    acc,
    down_staged,
    down_land,
    total,
    send_sems,
    recv_sems,
):
    links = Links(n_ctx, n_fsdp, send_sems, recv_sems)
    rows = own.shape[0]
    links.greet(cube=True, line=True)
    line = line_sum(links, down_part, down_staged, down_land, total, rows)
    plane = cube_sum(links, part, staged, land, acc, rows)
    in_turns(plane, line, plane, line, plane)
    finish(plane)
    d_normed = acc[pl.ds(0, rows), :]
    value = own[...].astype(jnp.float32)
    scale = lax.rsqrt(jnp.mean(value * value, axis=1, keepdims=True) + EPS)
    unit = value * scale
    term[...] = jnp.sum(d_normed * unit, axis=0, keepdims=True)
    d_own[...] = (d_resid[...] + norm_back(d_normed, gain[...], unit, scale)).astype(LOW)
    finish(line)
    output[...] = (resid[...] + total[...]).astype(LOW)


def last(n_ctx, n_fsdp, part, down_part, own, resid, d_resid, gain):
    rows, width = own.shape
    return communicate(
        functools.partial(last_kernel, n_ctx, n_fsdp),
        4,
        "last",
        (part, down_part, own, resid, d_resid, gain),
        [VMEM] * 6,
        [
            jax.ShapeDtypeStruct((rows, width), LOW),
            jax.ShapeDtypeStruct((rows, width), LOW),
            jax.ShapeDtypeStruct((1, width), jnp.float32),
        ],
        [VMEM] * 3,
        cube_scratch(n_ctx, rows, width) + line_scratch(n_fsdp, rows, width),
        n_ctx - 1 + 2 * (n_fsdp - 1),
        45,
    )


def tail_kernel(
    n_ctx,
    n_fsdp,
    gate,
    up,
    down,
    joined,
    out_part,
    terms,
    gate_all,
    up_all,
    down_all,
    attn_all,
    attn_part,
    staged,
    land,
    total,
    attn_low,
    local_sems,
    send_sems,
    recv_sems,
):
    links = Links(n_ctx, n_fsdp, send_sems, recv_sems)
    strip, ff_rows = gate.shape[0] // n_fsdp, gate.shape[1]
    down_rows, model_rows = down.shape[0], joined.shape[0] // n_fsdp
    term_rows = terms.shape[0] // n_fsdp
    rows = model_rows + term_rows
    head_rows, joined_width = out_part.shape[0], joined.shape[1]
    out_width = attn_part.shape[1] - joined_width
    heads_in = model_rows // head_rows

    def place(ref, ctx, fsdp):
        return ref.at[
            pl.ds(pl.multiple_of(ctx * strip, strip), strip),
            pl.ds(pl.multiple_of(fsdp * ff_rows, ff_rows), ff_rows),
        ]

    def out_column(ctx):
        return out_part.at[:, pl.ds(pl.multiple_of(ctx * out_width, out_width), out_width)]

    out_from = (links.ctx // heads_in) * rows + lax.rem(links.ctx, heads_in) * head_rows
    out_place = attn_part.at[
        pl.ds(pl.multiple_of(out_from, 16), head_rows), pl.ds(joined_width, out_width)
    ]
    moves = [
        (down, rows_of(down_all, links.ctx, down_rows)),
        (rows_of(gate, links.fsdp, strip), place(gate_all, links.ctx, links.fsdp)),
        (rows_of(up, links.fsdp, strip), place(up_all, links.ctx, links.fsdp)),
        (out_column(links.ctx), out_place),
    ]
    for fsdp in range(n_fsdp):
        moves.append(
            (
                joined.at[pl.ds(fsdp * model_rows, model_rows)],
                attn_part.at[pl.ds(fsdp * rows, model_rows), pl.ds(0, joined_width)],
            )
        )
        moves.append(
            (
                terms.at[pl.ds(fsdp * term_rows, term_rows)],
                attn_part.at[pl.ds(fsdp * rows + model_rows, term_rows)],
            )
        )
    local = [pltpu.make_async_copy(a, b, local_sems.at[i]) for i, (a, b) in enumerate(moves)]
    for copy in local:
        copy.start()
    links.greet(plane=True, line=True, whole_line=True)
    local[0].wait()
    plane_down = cube_gather(links, down_all, down_rows)
    to_shards = []
    for source, goal in ((gate, gate_all), (up, up_all)):
        copies = []
        for shift in range(1, n_fsdp):
            target = lax.rem(links.fsdp + shift, n_fsdp)
            copy = links.copy(
                rows_of(source, target, strip), place(goal, links.ctx, links.fsdp), links.ctx, target
            )
            copy.start()
            copies.append(copy)
        to_shards.append(copies)
    to_plane = []
    for shift in range(1, n_ctx):
        target = lax.rem(links.ctx + shift, n_ctx)
        copy = links.copy(out_column(target), out_place, target, links.fsdp)
        copy.start()
        to_plane.append(copy)
    in_turns(plane_down)
    for copy in local[1:]:
        copy.wait()
    for copy in to_plane:
        copy.wait()
    line = line_sum(links, attn_part, staged, land, total, rows)
    in_turns(plane_down)
    for copy in to_shards[0]:
        copy.wait()
    plane_gate = cube_gather(links, gate_all, strip)
    in_turns(plane_gate, plane_down)
    for copy in to_shards[1]:
        copy.wait()
    plane_up = cube_gather(links, up_all, strip)
    in_turns(line, plane_up, plane_gate, line, line, plane_gate, plane_up, line)
    finish(line)
    attn_low[...] = total[...].astype(LOW)
    mine = pltpu.make_async_copy(attn_low, rows_of(attn_all, links.ctx, rows), local_sems.at[0])
    mine.start()
    mine.wait()
    plane_attn = cube_gather(links, attn_all, rows)
    in_turns(plane_attn, plane_up, plane_attn)
    finish(plane_down, plane_gate, plane_up, plane_attn)


def tail(n_ctx, n_fsdp, gate, up, down, joined, out_part, terms):
    strip, ff_rows = gate.shape[0] // n_fsdp, gate.shape[1]
    rows = (joined.shape[0] + terms.shape[0]) // n_fsdp
    attn_width = joined.shape[1] + out_part.shape[1] // n_ctx
    shape = lambda *dims: jax.ShapeDtypeStruct(dims, LOW)
    return communicate(
        functools.partial(tail_kernel, n_ctx, n_fsdp),
        5,
        "tail",
        (gate, up, down, joined, out_part, terms),
        [ANY] * 6,
        [
            shape(strip * n_ctx, ff_rows * n_fsdp),
            shape(strip * n_ctx, ff_rows * n_fsdp),
            shape(down.shape[0] * n_ctx, down.shape[1]),
            shape(rows * n_ctx, attn_width),
        ],
        [ANY] * 4,
        [pltpu.VMEM((rows * n_fsdp, attn_width), LOW)]
        + line_scratch(n_fsdp, rows, attn_width)
        + [pltpu.VMEM((rows, attn_width), LOW), pltpu.SemaphoreType.DMA((4 + 2 * n_fsdp,))],
        5 * (n_ctx - 1) + 4 * (n_fsdp - 1),
        150,
    )


def spread_kernel(parts, widths, gathered, *outs):
    at = 0
    for out, width, sharers in zip(outs, widths, parts):
        pieces = []
        for i in range(0, gathered.shape[0], sharers):
            piece = gathered[i, :, at : at + width].astype(jnp.float32)
            for j in range(1, sharers):
                piece = piece + gathered[i + j, :, at : at + width].astype(jnp.float32)
            pieces.append(piece)
        out[...] = jnp.concatenate(pieces, axis=1)
        at += width


def spread(gathered, rows, widths, sharers):
    n_ctx, _, joined = gathered.shape
    step = 2 * max(sharers)
    tile = min(rows, 256)
    return pl.pallas_call(
        functools.partial(spread_kernel, sharers, widths),
        grid=(n_ctx // step, rows // tile),
        in_specs=[pl.BlockSpec((step, tile, joined), lambda i, j: (i, j, 0))],
        out_specs=[
            pl.BlockSpec((tile, step // s * w), lambda i, j: (j, i)) for w, s in zip(widths, sharers)
        ],
        out_shape=[
            jax.ShapeDtypeStruct((rows, n_ctx // s * w), jnp.float32) for w, s in zip(widths, sharers)
        ],
        compiler_params=pltpu.CompilerParams(vmem_limit_bytes=32 << 20),
        name="spread",
    )(gathered)


def lanes(shape):
    return lax.broadcasted_iota(jnp.int32, shape, 1)


def halves(tensor, back):
    half = HEAD_DIM // 2
    width = tensor.shape[1]
    later, earlier = pltpu.roll(tensor, width - half, 1), pltpu.roll(tensor, half, 1)
    first = lanes(tensor.shape) % HEAD_DIM < half
    return jnp.where(first, later, -earlier) if back else jnp.where(first, -later, earlier)


def turned(tensor, cosine, sine, back=False):
    parts = []
    for at in range(0, tensor.shape[1], 128):
        piece = tensor[:, at : at + 128]
        if back:
            parts.append(piece * cosine + halves(piece * sine, True))
        else:
            parts.append(piece * cosine + halves(piece, False) * sine)
    return parts[0] if len(parts) == 1 else jnp.concatenate(parts, axis=1)


def dot(left, right):
    return jnp.dot(left, right, preferred_element_type=jnp.float32)


def dot_dims(left, right, left_dim, right_dim):
    dims = (((left_dim,), (right_dim,)), ((), ()))
    return lax.dot_general(left, right, dims, preferred_element_type=jnp.float32)


def pick(ref, order, first, count, block):
    rows = [
        ref[pl.ds(pl.multiple_of(order[first + i] * block, block), block), :] for i in range(count)
    ]
    return rows[0] if count == 1 else jnp.concatenate(rows, axis=0)


def project(seq, order, gain, w_q, w_kv, cosine, sine, normed, q_heads, k_head, v_head, block, tile):
    kv_width = w_kv.shape[1] // 2

    def step(at, carry):
        rows = pl.ds(pl.multiple_of(at * tile, tile), tile)
        wide = pick(seq, order, at * (tile // block), tile // block, block).astype(jnp.float32)
        scale = lax.rsqrt(jnp.mean(wide * wide, axis=1, keepdims=True) + EPS)
        low = (wide * scale * gain[...]).astype(LOW)
        normed[rows, :] = low
        cos, sin = cosine[rows, :], sine[rows, :]
        queries = turned(dot(low, w_q[...]), cos, sin).astype(LOW)
        for head in range(q_heads.shape[0]):
            q_heads[head, rows, :] = queries[:, head * HEAD_DIM : (head + 1) * HEAD_DIM]
        both = dot(low, w_kv[...])
        keys = turned(both, cos, sin).astype(LOW)
        both = both.astype(LOW)
        for head in range(k_head.shape[0]):
            cut = head * HEAD_DIM
            k_head[head, rows, :] = keys[:, cut : cut + HEAD_DIM]
            v_head[head, rows, :] = both[:, kv_width + cut : kv_width + cut + HEAD_DIM]
        return carry

    lax.fori_loop(0, normed.shape[0] // tile, step, 0)


def scores_of(queries, keys, tile):
    logits = dot_dims(queries, keys, 1, 1) * (HEAD_DIM**-0.5)
    last = logits[:, -tile:]
    seen = lax.broadcasted_iota(jnp.int32, last.shape, 0) >= lanes(last.shape)
    last = jnp.where(seen, last, -1e30)
    before = logits.shape[1] - tile
    return last if before == 0 else jnp.concatenate([logits[:, :before], last], axis=1)


def attend(q_heads, k_head, v_head, out_heads, logs, tile, service):
    heads, length, _ = q_heads.shape
    group = heads // k_head.shape[0]
    for tile_at in range(length // tile):
        here, keys = pl.ds(tile_at * tile, tile), (tile_at + 1) * tile
        logs[here, :] = jnp.zeros((tile, logs.shape[1]), jnp.float32)

        def step(head, carry):
            scores = scores_of(q_heads[head, here, :], k_head[head // group, pl.ds(0, keys), :], tile)
            largest = jnp.max(scores, axis=1, keepdims=True)
            expo = jnp.exp(scores - largest)
            total = jnp.sum(expo, axis=1, keepdims=True)
            probs = (expo * (1.0 / total)).astype(LOW)
            out = dot(probs, v_head[head // group, pl.ds(0, keys), :])
            out_heads[head, here, :] = out.astype(LOW)
            log = largest + jnp.log(total)
            logs[here, :] += jnp.where(lanes((tile, logs.shape[1])) == head, log, 0.0)
            return carry

        lax.fori_loop(0, heads, step, 0)
        service()


def attend_back(q_heads, k_head, v_head, d_heads, logs, dq_heads, dk_head, dv_head, tile, service):
    heads, length, _ = q_heads.shape
    group = heads // k_head.shape[0]
    dk_head[...] = jnp.zeros_like(dk_head)
    dv_head[...] = jnp.zeros_like(dv_head)
    for tile_at in range(length // tile):
        here, keys = pl.ds(tile_at * tile, tile), (tile_at + 1) * tile

        def step(head, carry):
            queries, d_out = q_heads[head, here, :], d_heads[head, here, :]
            kept, seen = k_head[head // group, pl.ds(0, keys), :], v_head[head // group, pl.ds(0, keys), :]
            column = lanes((tile, logs.shape[1])) == head
            log = jnp.sum(jnp.where(column, logs[here, :], 0.0), axis=1, keepdims=True)
            probs = jnp.exp(scores_of(queries, kept, tile) - log)
            d_probs = dot_dims(d_out, seen, 1, 1)
            delta = jnp.sum(probs * d_probs, axis=1, keepdims=True)
            d_score = (probs * (d_probs - delta) * (HEAD_DIM**-0.5)).astype(LOW)
            dq_heads[head, here, :] = dot(d_score, kept)
            dk_head[head // group, pl.ds(0, keys), :] += dot_dims(d_score, queries, 0, 0)
            dv_head[head // group, pl.ds(0, keys), :] += dot_dims(probs.astype(LOW), d_out, 0, 0)
            return carry

        lax.fori_loop(0, heads, step, 0)
        service()


def side_by_side(ref, rows):
    return jnp.concatenate([ref[head, rows, :] for head in range(ref.shape[0])], axis=1)


def split_heads(value, ref, rows):
    for head in range(ref.shape[0]):
        ref[head, rows, :] = value[:, head * HEAD_DIM : (head + 1) * HEAD_DIM]


def attention_kernel(
    block,
    tile,
    order,
    place,
    seq,
    gain,
    w_q,
    w_kv,
    w_out,
    cosine,
    sine,
    normed,
    q_heads,
    k_head,
    v_head,
    logs,
    attended,
    part,
    out_heads,
):
    project(seq, order, gain, w_q, w_kv, cosine, sine, normed, q_heads, k_head, v_head, block, tile)
    attend(q_heads, k_head, v_head, out_heads, logs, tile, lambda: None)
    length = normed.shape[0]

    def join(at, carry):
        rows = pl.ds(pl.multiple_of(at * tile, tile), tile)
        attended[rows, :] = side_by_side(out_heads, rows)
        return carry

    lax.fori_loop(0, length // tile, join, 0)

    def out(at, carry):
        rows = pl.ds(pl.multiple_of(at * tile, tile), tile)
        mine = pick(attended, place, at * (tile // block), tile // block, block)
        part[rows, :] = dot(mine, w_out[...]).astype(LOW)
        return carry

    lax.fori_loop(0, length // tile, out, 0)


def attention(block, order, place, seq, gain, w_q, w_kv, w_out, cosine, sine):
    length, width = seq.shape
    heads, kv_heads = w_q.shape[1] // HEAD_DIM, w_kv.shape[1] // (2 * HEAD_DIM)
    tile = 4 * block
    shape = jax.ShapeDtypeStruct
    SMEM = pl.BlockSpec(memory_space=pltpu.SMEM)
    return pl.pallas_call(
        functools.partial(attention_kernel, block, tile),
        in_specs=[SMEM, SMEM] + [VMEM] * 7,
        out_specs=[VMEM] * 7,
        out_shape=[
            shape((length, width), LOW),
            shape((heads, length, HEAD_DIM), LOW),
            shape((kv_heads, length, HEAD_DIM), LOW),
            shape((kv_heads, length, HEAD_DIM), LOW),
            shape((length, 128), jnp.float32),
            shape((length, heads * HEAD_DIM), LOW),
            shape((length, width), LOW),
        ],
        scratch_shapes=[pltpu.VMEM((heads, length, HEAD_DIM), LOW)],
        compiler_params=pltpu.CompilerParams(vmem_limit_bytes=48 << 20),
        cost_estimate=pl.CostEstimate(flops=0, bytes_accessed=90_000_000, transcendentals=0),
        name="attention",
    )(order, place, seq, gain, w_q, w_kv, w_out, cosine, sine)


def back_kernel(
    block,
    tile,
    order,
    place,
    d_seq,
    w_q,
    w_kv,
    w_out,
    cosine,
    sine,
    q_heads,
    k_head,
    v_head,
    logs,
    d_sorted,
    d_joined,
    part,
    d_heads,
    dq_heads,
    dk_head,
    dv_head,
):
    length = d_seq.shape[0]
    query_width = w_q.shape[1]
    kv_width = w_kv.shape[1] // 2

    def begin(at, carry):
        rows = pl.ds(pl.multiple_of(at * tile, tile), tile)
        mine = pick(d_seq, order, at * (tile // block), tile // block, block)
        d_sorted[rows, :] = mine
        split_heads(dot_dims(mine, w_out[...], 1, 1).astype(LOW), d_heads, rows)
        return carry

    lax.fori_loop(0, length // tile, begin, 0)
    attend_back(
        q_heads, k_head, v_head, d_heads, logs, dq_heads, dk_head, dv_head, tile, lambda: None
    )

    def end(at, carry):
        rows = pl.ds(pl.multiple_of(at * tile, tile), tile)
        cos, sin = cosine[rows, :], sine[rows, :]
        d_query = turned(side_by_side(dq_heads, rows), cos, sin, True)
        d_joined[rows, pl.ds(0, query_width)] = d_query.astype(LOW)
        both = jnp.concatenate([side_by_side(dk_head, rows), side_by_side(dv_head, rows)], axis=1)
        keys = lanes(both.shape) < kv_width
        both = jnp.where(keys, turned(both, cos, sin, True), both)
        d_joined[rows, pl.ds(query_width, 2 * kv_width)] = both.astype(LOW)
        return carry

    lax.fori_loop(0, length // tile, end, 0)

    def out(at, carry):
        rows = pl.ds(pl.multiple_of(at * tile, tile), tile)
        mine = pick(d_joined, place, at * (tile // block), tile // block, block)
        total = dot_dims(mine[:, :query_width], w_q[...], 1, 1)
        total += dot_dims(mine[:, query_width:], w_kv[...], 1, 1)
        part[rows, :] = total.astype(LOW)
        return carry

    lax.fori_loop(0, length // tile, out, 0)


def attention_back(block, order, place, d_seq, w_q, w_kv, w_out, cosine, sine, q_heads, k_head, v_head, logs):
    length, width = d_seq.shape
    heads, kv_heads = q_heads.shape[0], k_head.shape[0]
    tile = 4 * block
    shape = jax.ShapeDtypeStruct
    SMEM = pl.BlockSpec(memory_space=pltpu.SMEM)
    return pl.pallas_call(
        functools.partial(back_kernel, block, tile),
        in_specs=[SMEM, SMEM] + [VMEM] * 10,
        out_specs=[VMEM] * 3,
        out_shape=[
            shape((length, width), LOW),
            shape((length, w_q.shape[1] + w_kv.shape[1]), LOW),
            shape((length, width), LOW),
        ],
        scratch_shapes=[
            pltpu.VMEM((heads, length, HEAD_DIM), LOW),
            pltpu.VMEM((heads, length, HEAD_DIM), jnp.float32),
            pltpu.VMEM((kv_heads, length, HEAD_DIM), jnp.float32),
            pltpu.VMEM((kv_heads, length, HEAD_DIM), jnp.float32),
        ],
        compiler_params=pltpu.CompilerParams(vmem_limit_bytes=48 << 20),
        cost_estimate=pl.CostEstimate(flops=0, bytes_accessed=150_000_000, transcendentals=0),
        name="attention_back",
    )(order, place, d_seq, w_q, w_kv, w_out, cosine, sine, q_heads, k_head, v_head, logs)


def on_device(
    tokens,
    cotangent,
    pairing,
    norm_attn,
    w_query,
    w_key,
    w_value,
    w_out,
    norm_mlp,
    w_gate,
    w_up,
    w_down,
):
    n_ctx, n_fsdp = lax.axis_size("ctx"), lax.axis_size("fsdp")
    ctx = lax.axis_index("ctx")
    own_tokens = tokens[0]
    tok_rows, width = own_tokens.shape
    length = tok_rows * n_ctx
    rows_model = w_gate.shape[0]
    low = LOW

    query_width = w_query.shape[1] // n_ctx
    heads_kv = w_key.shape[1] // HEAD_DIM
    kv_here = max(1, heads_kv // n_ctx)
    sharers = max(1, n_ctx // heads_kv)
    kv_width = kv_here * HEAD_DIM
    kv_start = (ctx // sharers) * kv_width

    def columns(matrix, start, size):
        return lax.dynamic_slice_in_dim(matrix, start, size, 1)

    kv = jnp.concatenate([columns(w_key, kv_start, kv_width), columns(w_value, kv_start, kv_width)], axis=1)
    gains = jnp.zeros((8, rows_model), jnp.float32).at[0].set(norm_attn).at[1].set(norm_mlp)
    sequence, w_q, w_kv, gains, _, w_out_rows = front(
        n_ctx, n_fsdp, own_tokens, w_query, kv, w_out, gains
    )
    gains = gains.reshape(n_fsdp, 8, rows_model)
    gain_attn, gain_mlp = gains[:, 0].reshape(1, -1), gains[:, 1].reshape(1, -1)
    out_width = width // n_ctx

    ff_rows = w_down.shape[0]
    strip = rows_model // n_ctx
    upstream = cotangent[0]
    w_gate, w_up, upstream, sequence = lax.optimization_barrier((w_gate, w_up, upstream, sequence))

    def strips(matrix):
        piece = lambda fsdp: lax.dynamic_slice(matrix, (ctx * strip, fsdp * ff_rows), (strip, ff_rows))
        return by_permutes(piece, "fsdp")

    gate_full = gather(strips(w_gate), "ctx")
    up_full = gather(strips(w_up), "ctx")
    upstream_all = by_permutes(lambda fsdp: upstream, "fsdp")

    block = tok_rows // pairing.shape[1]
    place = pairing.reshape(-1)
    blocks = jnp.arange(place.shape[0], dtype=jnp.int32)
    order = jnp.sum(jnp.where(place[None, :] == blocks[:, None], blocks[None, :], 0), axis=1)
    cosine, sine = rotation(jnp.arange(length, dtype=jnp.int32), HEAD_DIM)
    cosine, sine = [jnp.tile(t[:, 0], (1, 128 // HEAD_DIM)) for t in (cosine, sine)]
    normed_attn, q_heads, k_head, v_head, logs, attended_low, part = attention(
        block, order, place, sequence, gain_attn, w_q, w_kv, w_out_rows, cosine, sine
    )
    resid, normed_mlp = middle(n_ctx, n_fsdp, part, own_tokens, gain_mlp)

    gate_pre = product(normed_mlp, gate_full)
    up_pre = product(normed_mlp, up_full)
    sigma = jax.nn.sigmoid(gate_pre)
    swish = gate_pre * sigma
    hidden = (swish * up_pre).astype(low)
    d_hidden = product_t(upstream_all, w_down)
    d_gate = (d_hidden * up_pre * sigma * (1.0 + gate_pre * (1.0 - sigma))).astype(low)
    d_up = (d_hidden * swish).astype(low)
    d_part = (product_t(d_gate, gate_full) + product_t(d_up, up_full)).astype(low)
    grad_gate = tokens_t(normed_mlp, d_gate).astype(low)
    grad_up = tokens_t(normed_mlp, d_up).astype(low)
    d_part, grad_gate, grad_up = lax.optimization_barrier((d_part, grad_gate, grad_up))
    grad_down = tokens_t(hidden, upstream_all).astype(low)
    d_resid, d_resid_low, grad_down, gain_mlp_term = turn(
        n_ctx, n_fsdp, d_part, grad_down, upstream, resid, gain_mlp
    )
    grad_gate, grad_up = scatter_sum(grad_gate, "ctx"), scatter_sum(grad_up, "ctx")

    d_sorted, d_joined, part = attention_back(
        block,
        order,
        place,
        d_resid_low,
        w_q,
        w_kv,
        w_out_rows,
        cosine,
        sine,
        q_heads,
        k_head,
        v_head,
        logs,
    )
    d_inputs, output, gain_attn_term = last(
        n_ctx,
        n_fsdp,
        part,
        product(hidden, w_down).astype(low),
        own_tokens,
        resid,
        d_resid,
        gain_attn,
    )
    grad_out = tokens_t(attended_low, d_sorted).astype(low)
    grad_joined = tokens_t(normed_attn, d_joined).astype(low)
    terms = jnp.concatenate([gain_attn_term, gain_mlp_term]).reshape(2, n_fsdp, rows_model)
    attn_width = query_width + 2 * kv_width + out_width
    pad = ((0, 0), (0, 14), (0, attn_width - rows_model))
    terms = jnp.pad(terms.transpose(1, 0, 2).astype(low), pad).reshape(n_fsdp * 16, attn_width)
    grad_gate, grad_up, grad_down, grad_attn = tail(
        n_ctx, n_fsdp, grad_gate, grad_up, grad_down, grad_joined, grad_out, terms
    )
    grad_attn = grad_attn.reshape(n_ctx, rows_model + 16, attn_width)
    terms = jnp.sum(grad_attn[:, rows_model : rows_model + 2, :rows_model].astype(jnp.float32), axis=0)
    grad_query, grad_key, grad_value, grad_out = spread(
        grad_attn, rows_model, (query_width, kv_width, kv_width, out_width), (1, sharers, sharers, 1)
    )

    return (
        output[None],
        d_inputs[None],
        terms[0],
        grad_query,
        grad_key,
        grad_value,
        grad_out,
        terms[1],
        grad_gate.astype(jnp.float32),
        grad_up.astype(jnp.float32),
        grad_down.astype(jnp.float32),
    )


def solution(mesh):
    return jax.shard_map(
        on_device,
        mesh=mesh,
        in_specs=(
            P("fsdp", "ctx", None),
            P("fsdp", "ctx", None),
            P(),
            P("fsdp"),
            P("fsdp", None),
            P("fsdp", None),
            P("fsdp", None),
            P("fsdp", None),
            P("fsdp"),
            P("fsdp", None),
            P("fsdp", None),
            P("fsdp", None),
        ),
        out_specs=(
            P("fsdp", "ctx", None),
            P("fsdp", "ctx", None),
            P("fsdp"),
            P("fsdp", None),
            P("fsdp", None),
            P("fsdp", None),
            P("fsdp", None),
            P("fsdp"),
            P("fsdp", None),
            P("fsdp", None),
            P("fsdp", None),
        ),
        check_vma=False,
    )
```

```python
import functools
import math

import jax
import jax.numpy as jnp
from jax import lax
from jax.experimental import pallas as pl
from jax.experimental.pallas import tpu as pltpu
from jax.sharding import PartitionSpec as P

HEAD_DIM = 64


EPS = 1e-05
THETA = 500000.0


def frequencies(head_width):
    evens = jnp.arange(0, head_width, 2, dtype=jnp.float32)
    inverse = 1.0 / THETA ** (evens / head_width)
    wavelen = 2.0 * math.pi / inverse
    smooth = (8192.0 / wavelen - 1.0) / 3.0
    middle = (1.0 - smooth) * inverse / 32.0 + smooth * inverse
    return jnp.where(wavelen < 2048.0, inverse, jnp.where(wavelen > 8192.0, inverse / 32.0, middle))


def rotation(positions, head_width):
    angles = positions.astype(jnp.float32)[:, None] * frequencies(head_width)[None, :]
    cosine = jnp.concatenate([jnp.cos(angles), jnp.cos(angles)], axis=1)[:, None, :]
    sine = jnp.concatenate([jnp.sin(angles), jnp.sin(angles)], axis=1)[:, None, :]
    return (cosine, sine)


def rotate(tensor, cosine, sine):
    middle = tensor.shape[-1] // 2
    turned = jnp.concatenate([-tensor[..., middle:], tensor[..., :middle]], axis=-1)
    return tensor * cosine + turned * sine


def unrotate(gradient, cosine, sine):
    middle = gradient.shape[-1] // 2
    moved = gradient * sine
    back_turn = jnp.concatenate([moved[..., middle:], -moved[..., :middle]], axis=-1)
    return gradient * cosine + back_turn


def slot_positions(pairing, seq_length, block_len):
    flattened = pairing.reshape(-1)
    slots = jnp.arange(seq_length, dtype=jnp.int32)
    owning = slots // block_len
    labels = jnp.arange(flattened.shape[0], dtype=jnp.int32)
    anchor = jnp.sum(jnp.where(owning[:, None] == labels[None, :], flattened[None, :], 0), axis=1)
    return anchor * block_len + slots % block_len


def product(left, right):
    return jnp.dot(left, right, preferred_element_type=jnp.float32)


def product_t(left, right):
    return lax.dot_general(
        left, right, (((1,), (1,)), ((), ())), preferred_element_type=jnp.float32
    )


def tokens_t(left, right):
    return lax.dot_general(
        left, right, (((0,), (0,)), ((), ())), preferred_element_type=jnp.float32
    )


LOW = jnp.bfloat16
MESH = pl.DeviceIdType.MESH
ANY = pl.BlockSpec(memory_space=pl.ANY)
VMEM = pl.BlockSpec(memory_space=pltpu.VMEM)


def norm_back(upstream, gain, unit, scale):
    weighted = upstream * gain
    return scale * (weighted - unit * jnp.mean(weighted * unit, axis=1, keepdims=True))


def gather(array, axis):
    return lax.all_gather(array, axis, axis=0, tiled=True)


def scatter_sum(array, axis):
    return lax.psum_scatter(array, axis, scatter_dimension=0, tiled=True)


def einsum(spec, left, right):
    return jnp.einsum(spec, left, right, preferred_element_type=jnp.float32)


def swap_order(array, first, second):
    size = array.shape[1] // (first * second)
    parts = []
    for b in range(second):
        for a in range(first):
            at = (a * second + b) * size
            parts.append(array[:, at : at + size])
    return jnp.concatenate(parts, axis=1)


class Links:
    def __init__(self, n_ctx, n_fsdp, send_sems, recv_sems):
        self.n_ctx, self.n_fsdp = n_ctx, n_fsdp
        self.ctx, self.fsdp = lax.axis_index("ctx"), lax.axis_index("fsdp")
        self.send_sems, self.recv_sems = send_sems, recv_sems
        self.used = 0
        core = self.ctx % 2
        flips = [self.flip(d) for d in range(1, n_ctx.bit_length() - 1)]
        backward = flips[::-1]
        self.order = [(1 - core) * a + core * b for a, b in zip(flips, backward)]
        self.sibling = self.flip(0)

    def flip(self, digit):
        return 2**digit * (1 - 2 * ((self.ctx // 2**digit) % 2))

    def greet(self, cube=False, plane=False, line=False, whole_line=False):
        barrier = pltpu.get_barrier_semaphore()
        count = 0

        def hail(ctx, fsdp):
            pl.semaphore_signal(barrier, inc=1, device_id=(ctx, fsdp), device_id_type=MESH)

        if plane:
            for shift in range(1, self.n_ctx):
                hail(lax.rem(self.ctx + shift, self.n_ctx), self.fsdp)
            count += self.n_ctx - 1
        elif cube:
            for step in self.order + [self.sibling]:
                hail(self.ctx + step, self.fsdp)
            count += len(self.order) + 1
        if whole_line:
            for shift in range(1, self.n_fsdp):
                hail(self.ctx, lax.rem(self.fsdp + shift, self.n_fsdp))
            count += self.n_fsdp - 1
        if line and not whole_line:
            for step in (-1, 1):
                inside = jnp.logical_and(self.fsdp + step >= 0, self.fsdp + step < self.n_fsdp)

                @pl.when(inside)
                def _():
                    hail(self.ctx, self.fsdp + step)

            ends = jnp.logical_or(self.fsdp == 0, self.fsdp == self.n_fsdp - 1)
            pl.when(ends)(lambda: pl.semaphore_wait(barrier, count + 1))
            pl.when(jnp.logical_not(ends))(lambda: pl.semaphore_wait(barrier, count + 2))
        else:
            pl.semaphore_wait(barrier, count)

    def copies(self, sources, target, ctx, fsdp):
        slot = self.used
        self.used += 1
        return [
            pltpu.make_async_remote_copy(
                src_ref=source,
                dst_ref=target,
                send_sem=self.send_sems.at[slot],
                recv_sem=self.recv_sems.at[slot],
                device_id=(ctx, fsdp),
                device_id_type=MESH,
            )
            for source in sources
        ]

    def copy(self, source, target, ctx, fsdp):
        return self.copies((source,), target, ctx, fsdp)[0]


def rows_of(ref, index, rows):
    return ref.at[pl.ds(pl.multiple_of(index * rows, rows), rows)]


def in_turns(*walks):
    for walk in walks:
        next(walk, None)


def finish(*walks):
    for walk in walks:
        for _ in walk:
            pass


def cube_gather(links, ref, rows):
    held, sent, shared = [0], [], []

    def send(offset, step):
        block = rows_of(ref, links.ctx + offset, rows)
        copy = links.copy(block, block, links.ctx + step, links.fsdp)
        copy.start()
        return copy

    fresh = held
    for step in links.order:
        copies = [send(offset, step) for offset in held]
        shared += [send(offset, links.sibling) for offset in fresh]
        yield
        for copy in copies:
            copy.wait_recv()
        sent += copies
        fresh = [offset + step for offset in held]
        held = held + fresh
    shared += [send(offset, links.sibling) for offset in fresh]
    yield
    for copy in shared:
        copy.wait_recv()
    for copy in sent + shared:
        copy.wait_send()


def in_rows(rows, body):
    size = math.gcd(rows, 64)

    def step(at, carry):
        body(pl.multiple_of(at * size, size), size)
        return carry

    lax.fori_loop(0, rows // size, step, 0)


def cube_sum(links, part, land, acc, rows):
    offsets, theirs = [0], [0]
    for step, other in zip(links.order, links.order[::-1]):
        offsets = offsets + [offset + step for offset in offsets]
        theirs = theirs + [offset + other for offset in theirs]
    wide = jnp.float32
    sent, pending = [], []
    for at, offset in enumerate(theirs):
        source = rows_of(part, links.ctx + links.sibling + offset, rows)
        target = land.at[pl.ds(at * rows, rows)]
        copy = links.copy(source, target, links.ctx + links.sibling, links.fsdp)
        copy.start()
        pending.append(copy)
    yield
    land_from, land_at = 0, len(offsets)
    for level in range(len(links.order) + 1):
        count = len(offsets)
        half = count // 2
        onward = []
        for at in list(range(half, count)) + list(range(half)):
            pending[at].wait_recv()
            first, place = level == 0, (land_from + at) * rows
            goes = at >= half and count > 1

            def add(start, size, at=at, place=place, first=first, goes=goes):
                landed = land[pl.ds(place + start, size), :].astype(wide)
                if first:
                    base = (links.ctx + offsets[at]) * rows
                    mine = part[pl.ds(pl.multiple_of(base + start, size), size), :].astype(wide)
                else:
                    mine = acc[pl.ds(at * rows + start, size), :]
                if goes:
                    land[pl.ds(place + start, size), :] = (mine + landed).astype(LOW)
                else:
                    acc[pl.ds(at * rows + start, size), :] = mine + landed

            in_rows(rows, add)
            if goes:
                source = land.at[pl.ds(place, rows)]
                target = land.at[pl.ds((land_at + at - half) * rows, rows)]
                step = links.order[len(links.order) - 1 - level]
                copy = links.copy(source, target, links.ctx + step, links.fsdp)
                copy.start()
                onward.append(copy)
        sent += pending
        pending, land_from = onward, land_at
        land_at += half
        offsets = offsets[: max(half, 1)]
        if level < len(links.order):
            yield
    for copy in sent:
        copy.wait_send()


def cube_scratch(n_ctx, rows, width):
    return [
        pltpu.VMEM(((n_ctx - 1) * rows, width), LOW),
        pltpu.VMEM((max(1, n_ctx // 4) * rows, width), jnp.float32),
    ]


def line_gather(links, refs, rows):
    count, me = links.n_fsdp, links.fsdp
    sends = []
    for hop in range(count - 1):
        receives = []
        for ref, size in zip(refs, rows):
            up_block = rows_of(ref, me - hop, size)
            down_block = rows_of(ref, me + hop, size)
            up = links.copy(up_block, up_block, links.ctx, me + 1)
            down = links.copy(down_block, down_block, links.ctx, me - 1)
            up_ok = jnp.logical_and(me >= hop, me < count - 1)
            down_ok = jnp.logical_and(me <= count - 1 - hop, me > 0)
            pl.when(up_ok)(up.start)
            pl.when(down_ok)(down.start)
            sends += [(up_ok, up), (down_ok, down)]
            receives += [(me >= hop + 1, up), (me <= count - 2 - hop, down)]
        yield
        for ok, copy in receives:
            pl.when(ok)(copy.wait_recv)
    for ok, copy in sends:
        pl.when(ok)(copy.wait_send)


def line_sum(links, part, land, total, rows):
    count, me = links.n_fsdp, links.fsdp
    flows = []
    for hop in range(count - 1):
        for side in (0, 1):
            goal = count - 1 - hop if side == 0 else hop
            slot = (side * (count - 1) + hop) * rows
            landing = land.at[pl.ds(slot, rows)]
            fed = me > 0 if side == 0 else me < count - 1
            passes = me < goal if side == 0 else me > goal
            peer = me + 1 if side == 0 else me - 1
            first, onward = links.copies((part.at[pl.ds(goal * rows, rows)], landing), landing, links.ctx, peer)
            flows.append((goal * rows, slot, onward, fed, passes, me == goal))
            pl.when(jnp.logical_and(passes, jnp.logical_not(fed)))(first.start)

    total[...] = rows_of(part, me, rows)[...].astype(jnp.float32)
    lower = me < count // 2
    for hop in range(count - 1):
        yield
        for near in (0, 1):

            @pl.when(lower if near == 0 else jnp.logical_not(lower))
            def _():
                for way in (near, 1 - near):
                    base, slot, onward, fed, passes, _ = flows[2 * hop + way]

                    @pl.when(jnp.logical_and(passes, fed))
                    def _():
                        onward.wait_recv()

                        def add(start, size):
                            own = part[pl.ds(base + start, size), :].astype(jnp.float32)
                            landed = land[pl.ds(slot + start, size), :].astype(jnp.float32)
                            land[pl.ds(slot + start, size), :] = (own + landed).astype(LOW)

                        in_rows(rows, add)
                        onward.start()

    yield
    for base, slot, onward, fed, passes, mine in flows:

        @pl.when(jnp.logical_and(mine, fed))
        def _():
            onward.wait_recv()

            def add(start, size):
                landed = land[pl.ds(slot + start, size), :].astype(jnp.float32)
                total[pl.ds(start, size), :] += landed

            in_rows(rows, add)

    for base, slot, onward, fed, passes, _ in flows:
        pl.when(passes)(onward.wait_send)


def line_scratch(n_fsdp, rows, width):
    return [
        pltpu.VMEM((2 * (n_fsdp - 1) * rows, width), LOW),
        pltpu.VMEM((rows, width), jnp.float32),
    ]


def communicate(kernel, collective_id, name, operands, in_specs, outs, out_specs, scratch, copies, busy):
    return pl.pallas_call(
        kernel,
        out_shape=outs,
        in_specs=in_specs,
        out_specs=out_specs,
        scratch_shapes=scratch
        + [pltpu.SemaphoreType.DMA((copies,)), pltpu.SemaphoreType.DMA((copies,))],
        compiler_params=pltpu.CompilerParams(
            collective_id=collective_id, has_side_effects=True, vmem_limit_bytes=62 << 20
        ),
        cost_estimate=pl.CostEstimate(flops=0, bytes_accessed=busy * 3_000_000, transcendentals=0),
        name=name,
    )(*operands)


def tail_kernel(
    n_ctx,
    n_fsdp,
    pair,
    joined,
    out_part,
    terms,
    gate_all,
    up_all,
    attn_all,
    attn_part,
    land,
    total,
    attn_low,
    local_sems,
    send_sems,
    recv_sems,
):
    links = Links(n_ctx, n_fsdp, send_sems, recv_sems)
    strip, ff_rows = pair.shape[1] // n_fsdp, pair.shape[2]
    model_rows, term_rows = joined.shape[0] // n_fsdp, terms.shape[0] // n_fsdp
    rows = model_rows + term_rows
    head_rows, joined_width = out_part.shape[0], joined.shape[1]
    out_width = attn_part.shape[1] - joined_width
    heads_in = model_rows // head_rows

    def place(ref, ctx, fsdp):
        return ref.at[
            pl.ds(pl.multiple_of(ctx * strip, strip), strip),
            pl.ds(pl.multiple_of(fsdp * ff_rows, ff_rows), ff_rows),
        ]

    def strip_of(part, fsdp):
        return pair.at[part, pl.ds(pl.multiple_of(fsdp * strip, strip), strip)]

    def out_column(ctx):
        return out_part.at[:, pl.ds(pl.multiple_of(ctx * out_width, out_width), out_width)]

    out_from = (links.ctx // heads_in) * rows + lax.rem(links.ctx, heads_in) * head_rows
    out_place = attn_part.at[
        pl.ds(pl.multiple_of(out_from, 16), head_rows), pl.ds(joined_width, out_width)
    ]
    moves = [
        (strip_of(0, links.fsdp), place(gate_all, links.ctx, links.fsdp)),
        (strip_of(1, links.fsdp), place(up_all, links.ctx, links.fsdp)),
        (out_column(links.ctx), out_place),
    ]
    for fsdp in range(n_fsdp):
        moves.append(
            (
                joined.at[pl.ds(fsdp * model_rows, model_rows)],
                attn_part.at[pl.ds(fsdp * rows, model_rows), pl.ds(0, joined_width)],
            )
        )
        moves.append(
            (
                terms.at[pl.ds(fsdp * term_rows, term_rows)],
                attn_part.at[pl.ds(fsdp * rows + model_rows, term_rows)],
            )
        )
    local = [pltpu.make_async_copy(a, b, local_sems.at[i]) for i, (a, b) in enumerate(moves)]
    for copy in local:
        copy.start()
    links.greet(plane=True, line=True, whole_line=True)
    to_shards = []
    for part, goal in enumerate((gate_all, up_all)):
        copies = []
        for shift in range(1, n_fsdp):
            target = lax.rem(links.fsdp + shift, n_fsdp)
            copy = links.copy(
                strip_of(part, target), place(goal, links.ctx, links.fsdp), links.ctx, target
            )
            copy.start()
            copies.append(copy)
        to_shards.append(copies)
    to_plane = []
    for shift in range(1, n_ctx):
        target = lax.rem(links.ctx + shift, n_ctx)
        copy = links.copy(out_column(target), out_place, target, links.fsdp)
        copy.start()
        to_plane.append(copy)
    for copy in local:
        copy.wait()
    for copy in to_plane:
        copy.wait()
    for copy in to_shards[0]:
        copy.wait()
    plane_gate = cube_gather(links, gate_all, strip)
    in_turns(plane_gate)
    line = line_sum(links, attn_part, land, total, rows)
    in_turns(line)
    for copy in to_shards[1]:
        copy.wait()
    plane_up = cube_gather(links, up_all, strip)
    in_turns(plane_gate, plane_up, line, plane_gate, line, plane_up, line)
    finish(line)
    attn_low[...] = total[...].astype(LOW)
    mine = pltpu.make_async_copy(attn_low, rows_of(attn_all, links.ctx, rows), local_sems.at[0])
    mine.start()
    mine.wait()
    plane_attn = cube_gather(links, attn_all, rows)
    in_turns(plane_attn, plane_up, plane_attn)
    finish(plane_gate, plane_up, plane_attn)


def tail(n_ctx, n_fsdp, pair, joined, out_part, terms):
    strip, ff_rows = pair.shape[1] // n_fsdp, pair.shape[2]
    rows = (joined.shape[0] + terms.shape[0]) // n_fsdp
    attn_width = joined.shape[1] + out_part.shape[1] // n_ctx
    shape = lambda *dims: jax.ShapeDtypeStruct(dims, LOW)
    return communicate(
        functools.partial(tail_kernel, n_ctx, n_fsdp),
        5,
        "tail",
        (pair, joined, out_part, terms),
        [ANY] * 4,
        [
            shape(strip * n_ctx, ff_rows * n_fsdp),
            shape(strip * n_ctx, ff_rows * n_fsdp),
            shape(rows * n_ctx, attn_width),
        ],
        [ANY] * 3,
        [pltpu.VMEM((rows * n_fsdp, attn_width), LOW)]
        + line_scratch(n_fsdp, rows, attn_width)
        + [pltpu.VMEM((rows, attn_width), LOW), pltpu.SemaphoreType.DMA((3 + 2 * n_fsdp,))],
        4 * (n_ctx - 1) + 4 * (n_fsdp - 1),
        130,
    )


def widen_kernel(*refs):
    count = len(refs) // 2
    for source, goal in zip(refs[:count], refs[count:]):
        goal[...] = source[...].astype(jnp.float32)


def widen(*arrays):
    steps = max(4, arrays[0].shape[0] // 128)
    specs = [pl.BlockSpec((a.shape[0] // steps, a.shape[1]), lambda i: (i, 0)) for a in arrays]
    return pl.pallas_call(
        widen_kernel,
        grid=(steps,),
        in_specs=specs,
        out_specs=specs,
        out_shape=[jax.ShapeDtypeStruct(a.shape, jnp.float32) for a in arrays],
        compiler_params=pltpu.CompilerParams(vmem_limit_bytes=60 << 20),
        name="widen",
    )(*arrays)


def spread_kernel(parts, widths, gathered, *outs):
    at = 0
    for out, width, sharers in zip(outs, widths, parts):
        pieces = []
        for i in range(0, gathered.shape[0], sharers):
            piece = gathered[i, :, at : at + width].astype(jnp.float32)
            for j in range(1, sharers):
                piece = piece + gathered[i + j, :, at : at + width].astype(jnp.float32)
            pieces.append(piece)
        out[...] = jnp.concatenate(pieces, axis=1)
        at += width


def spread(gathered, rows, widths, sharers):
    n_ctx, _, joined = gathered.shape
    step = 2 * max(sharers)
    tile = min(rows, 256)
    return pl.pallas_call(
        functools.partial(spread_kernel, sharers, widths),
        grid=(n_ctx // step, rows // tile),
        in_specs=[pl.BlockSpec((step, tile, joined), lambda i, j: (i, j, 0))],
        out_specs=[
            pl.BlockSpec((tile, step // s * w), lambda i, j: (j, i)) for w, s in zip(widths, sharers)
        ],
        out_shape=[
            jax.ShapeDtypeStruct((rows, n_ctx // s * w), jnp.float32) for w, s in zip(widths, sharers)
        ],
        compiler_params=pltpu.CompilerParams(vmem_limit_bytes=32 << 20),
        name="spread",
    )(gathered)


def lanes(shape):
    return lax.broadcasted_iota(jnp.int32, shape, 1)


def halves(tensor, back):
    half = HEAD_DIM // 2
    width = tensor.shape[1]
    later, earlier = pltpu.roll(tensor, width - half, 1), pltpu.roll(tensor, half, 1)
    first = lanes(tensor.shape) % HEAD_DIM < half
    return jnp.where(first, later, -earlier) if back else jnp.where(first, -later, earlier)


def turned(tensor, cosine, sine, back=False):
    parts = []
    for at in range(0, tensor.shape[1], 128):
        piece = tensor[:, at : at + 128]
        if back:
            parts.append(piece * cosine + halves(piece * sine, True))
        else:
            parts.append(piece * cosine + halves(piece, False) * sine)
    return parts[0] if len(parts) == 1 else jnp.concatenate(parts, axis=1)


def dot(left, right):
    return jnp.dot(left, right, preferred_element_type=jnp.float32)


def dot_dims(left, right, left_dim, right_dim):
    dims = (((left_dim,), (right_dim,)), ((), ()))
    return lax.dot_general(left, right, dims, preferred_element_type=jnp.float32)


def to_positions(pos_row, at, tile):
    shape = (tile, pos_row.shape[1])
    here = lax.broadcasted_iota(jnp.int32, shape, 0) + at * tile
    return jnp.where(here == pos_row[...], 1.0, 0.0).astype(LOW)


def to_slots(pos_column, rows, tile):
    shape = (tile, pos_column.shape[0])
    return jnp.where(lanes(shape) == pos_column[rows, :], 1.0, 0.0).astype(LOW)


def project(seq, gain, w_q, w_kv, cosine, sine, normed, joined, tile, start, stop):
    query_width, kv_width = w_q.shape[1], w_kv.shape[1] // 2

    def step(at, carry):
        rows = pl.ds(pl.multiple_of(at * tile, tile), tile)
        wide = seq[rows, :].astype(jnp.float32)
        scale = lax.rsqrt(jnp.mean(wide * wide, axis=1, keepdims=True) + EPS)
        low = (wide * scale * gain).astype(LOW)
        normed[rows, :] = low
        cos, sin = cosine[rows, :], sine[rows, :]
        joined[rows, pl.ds(0, query_width)] = turned(dot(low, w_q[...]), cos, sin).astype(LOW)
        both = dot(low, w_kv[...])
        both = jnp.where(lanes(both.shape) < kv_width, turned(both, cos, sin), both)
        joined[rows, pl.ds(query_width, 2 * kv_width)] = both.astype(LOW)
        return carry

    lax.fori_loop(start, stop, step, 0)


def in_order(pos_row, joined, q_heads, k_head, v_head, tile):
    query_width = q_heads.shape[0] * HEAD_DIM
    kv_width = k_head.shape[0] * HEAD_DIM

    def step(at, carry):
        rows = pl.ds(pl.multiple_of(at * tile, tile), tile)
        moved = dot(to_positions(pos_row, at, tile), joined[...]).astype(LOW)
        split_heads(moved[:, :query_width], q_heads, rows)
        split_heads(moved[:, query_width : query_width + kv_width], k_head, rows)
        split_heads(moved[:, query_width + kv_width :], v_head, rows)
        return carry

    lax.fori_loop(0, joined.shape[0] // tile, step, 0)


def scores_of(queries, keys, tile):
    logits = dot_dims(queries, keys, 1, 1) * (HEAD_DIM**-0.5)
    last = logits[:, -tile:]
    seen = lax.broadcasted_iota(jnp.int32, last.shape, 0) >= lanes(last.shape)
    last = jnp.where(seen, last, -1e30)
    before = logits.shape[1] - tile
    return last if before == 0 else jnp.concatenate([logits[:, :before], last], axis=1)


def attend(q_heads, k_head, v_head, out_heads, logs, tile, service):
    heads, length, _ = q_heads.shape
    group = heads // k_head.shape[0]
    for tile_at in range(length // tile):
        here, keys = pl.ds(tile_at * tile, tile), (tile_at + 1) * tile
        logs[here, :] = jnp.zeros((tile, logs.shape[1]), jnp.float32)

        def step(head, carry):
            scores = scores_of(q_heads[head, here, :], k_head[head // group, pl.ds(0, keys), :], tile)
            largest = jnp.max(scores, axis=1, keepdims=True)
            expo = jnp.exp(scores - largest)
            total = jnp.sum(expo, axis=1, keepdims=True)
            probs = (expo * (1.0 / total)).astype(LOW)
            out = dot(probs, v_head[head // group, pl.ds(0, keys), :])
            out_heads[head, here, :] = out.astype(LOW)
            log = largest + jnp.log(total)
            logs[here, :] += jnp.where(lanes((tile, logs.shape[1])) == head, log, 0.0)
            return carry

        lax.fori_loop(0, heads, step, 0)
        service()


def attend_back(q_heads, k_head, v_head, d_heads, logs, dq_heads, dk_head, dv_head, tile, service):
    heads, length, _ = q_heads.shape
    group = heads // k_head.shape[0]
    dk_head[...] = jnp.zeros_like(dk_head)
    dv_head[...] = jnp.zeros_like(dv_head)
    for tile_at in range(length // tile):
        here, keys = pl.ds(tile_at * tile, tile), (tile_at + 1) * tile

        def step(head, carry):
            queries, d_out = q_heads[head, here, :], d_heads[head, here, :]
            kept, seen = k_head[head // group, pl.ds(0, keys), :], v_head[head // group, pl.ds(0, keys), :]
            column = lanes((tile, logs.shape[1])) == head
            log = jnp.sum(jnp.where(column, logs[here, :], 0.0), axis=1, keepdims=True)
            probs = jnp.exp(scores_of(queries, kept, tile) - log)
            d_probs = dot_dims(d_out, seen, 1, 1)
            delta = jnp.sum(probs * d_probs, axis=1, keepdims=True)
            d_score = (probs * (d_probs - delta) * (HEAD_DIM**-0.5)).astype(LOW)
            dq_heads[head, here, :] = dot(d_score, kept)
            dk_head[head // group, pl.ds(0, keys), :] += dot_dims(d_score, queries, 0, 0)
            dv_head[head // group, pl.ds(0, keys), :] += dot_dims(probs.astype(LOW), d_out, 0, 0)
            return carry

        lax.fori_loop(0, heads, step, 0)
        service()


def side_by_side(ref, rows):
    return jnp.concatenate([ref[head, rows, :] for head in range(ref.shape[0])], axis=1)


def split_heads(value, ref, rows):
    for head in range(ref.shape[0]):
        ref[head, rows, :] = value[:, head * HEAD_DIM : (head + 1) * HEAD_DIM]


def forward_kernel(
    n_ctx,
    n_fsdp,
    tile,
    pos_row,
    pos_column,
    own,
    w_query,
    kv,
    w_out,
    gains,
    w_gate,
    w_up,
    upstream,
    cosine,
    sine,
    gate_all,
    up_all,
    upstream_all,
    q_all,
    kv_all,
    gains_all,
    out_rows,
    normed,
    q_heads,
    k_head,
    v_head,
    logs,
    attended,
    resid,
    normed_mlp,
    seq,
    cols_all,
    out_heads,
    joined,
    part,
    land,
    acc,
    local_sems,
    send_sems,
    recv_sems,
):
    links = Links(n_ctx, n_fsdp, send_sems, recv_sems)
    rows, weight_rows, query_width = own.shape[0], kv.shape[0], q_all.shape[1]
    head_rows, out_width = out_rows.shape[0], cols_all.shape[1]
    strip, ff_rows = weight_rows // n_ctx, gate_all.shape[1]
    length = normed.shape[0]

    def cut(ref, size):
        return ref.at[:, pl.ds(pl.multiple_of(links.ctx * size, size), size)]

    def strip_from(ref, fsdp):
        return ref.at[
            pl.ds(pl.multiple_of(links.ctx * strip, strip), strip),
            pl.ds(pl.multiple_of(fsdp * ff_rows, ff_rows), ff_rows),
        ]

    def strip_to(ref):
        return rows_of(ref, links.ctx * n_fsdp + links.fsdp, strip)

    moves = [
        (own, rows_of(seq, links.ctx, rows)),
        (cut(w_query, query_width), rows_of(q_all, links.fsdp, weight_rows)),
        (kv, rows_of(kv_all, links.fsdp, weight_rows)),
        (gains, rows_of(gains_all, links.fsdp, gains.shape[0])),
        (cut(w_out, out_width), rows_of(cols_all, links.fsdp, weight_rows)),
        (strip_from(w_gate, links.fsdp), strip_to(gate_all)),
        (strip_from(w_up, links.fsdp), strip_to(up_all)),
        (upstream, rows_of(upstream_all, links.fsdp, rows)),
    ]
    local = [pltpu.make_async_copy(a, b, local_sems.at[i]) for i, (a, b) in enumerate(moves)]
    for copy in local:
        copy.start()
    links.greet(plane=True, line=True, whole_line=True)
    for copy in local[:5]:
        copy.wait()
    plane = cube_gather(links, seq, rows)
    line = line_gather(links, [gains_all, q_all, kv_all], [gains.shape[0], weight_rows, weight_rows])
    cols = line_gather(links, [cols_all], [weight_rows])
    in_turns(plane, line, plane, line, plane, line)
    finish(line, plane)
    in_turns(cols)
    for copy in local[5:]:
        copy.wait()

    def gain_row(row):
        first = [gains_all[pl.ds(z * gains.shape[0] + row, 1), :] for z in range(n_fsdp)]
        return jnp.concatenate(first, axis=1)

    gain = gain_row(0)
    tiles = length // tile
    half = max(1, tiles // 2)
    slots = (seq, gain, q_all, kv_all, cosine, sine, normed, joined, tile)
    project(*slots, 0, half)
    in_turns(cols)
    project(*slots, half, tiles)
    in_order(pos_row, joined, q_heads, k_head, v_head, tile)

    to_plane, gate_strips, up_strips = [], [], []
    column = cut(out_rows, out_width)
    mine = pltpu.make_async_copy(rows_of(cols_all, links.ctx, head_rows), column, local_sems.at[0])

    def hand_out():
        finish(cols)
        mine.start()
        for shift in range(1, n_ctx):
            target = lax.rem(links.ctx + shift, n_ctx)
            copy = links.copy(rows_of(cols_all, target, head_rows), column, target, links.fsdp)
            copy.start()
            to_plane.append(copy)
        for source, goal, copies in ((w_gate, gate_all, gate_strips), (w_up, up_all, up_strips)):
            for shift in range(1, n_fsdp):
                target = lax.rem(links.fsdp + shift, n_fsdp)
                copy = links.copy(strip_from(source, target), strip_to(goal), links.ctx, target)
                copy.start()
                copies.append(copy)

    services = [lambda: in_turns(cols), lambda: in_turns(cols), hand_out]

    def service():
        if services:
            services.pop(0)()

    attend(q_heads, k_head, v_head, out_heads, logs, tile, service)
    while services:
        service()

    def join(at, carry):
        here = pl.ds(pl.multiple_of(at * tile, tile), tile)
        joined[here, pl.ds(0, query_width)] = side_by_side(out_heads, here)
        return carry

    lax.fori_loop(0, tiles, join, 0)
    mine.wait()
    for copy in to_plane:
        copy.wait()

    def out(at, carry):
        here = pl.ds(pl.multiple_of(at * tile, tile), tile)
        moved = dot(to_slots(pos_column, here, tile), joined[:, pl.ds(0, query_width)]).astype(LOW)
        attended[here, :] = moved
        part[here, :] = dot(moved, out_rows[...]).astype(LOW)
        return carry

    lax.fori_loop(0, tiles, out, 0)
    finish(cube_sum(links, part, land, acc, rows))
    value = acc[pl.ds(0, rows), :] + rows_of(seq, links.ctx, rows)[...].astype(jnp.float32)
    resid[...] = value
    scale = lax.rsqrt(jnp.mean(value * value, axis=1, keepdims=True) + EPS)
    low = swap_order((value * scale * gain_row(1)).astype(LOW), n_fsdp, n_ctx)
    rows_of(normed_mlp, links.fsdp, rows)[...] = low
    line_normed = line_gather(links, [normed_mlp], [rows])
    in_turns(line_normed)
    for copy in gate_strips:
        copy.wait()
    plane_gate = cube_gather(links, gate_all, strip * n_fsdp)
    in_turns(plane_gate, line_normed)
    for copy in up_strips:
        copy.wait()
    plane_up = cube_gather(links, up_all, strip * n_fsdp)
    line_upstream = line_gather(links, [upstream_all], [rows])
    in_turns(plane_gate, plane_up, line_normed, line_upstream)
    in_turns(plane_gate, plane_up, line_normed, line_upstream, plane_up, line_upstream)
    finish(plane_gate, line_normed, plane_up, line_upstream)


def forward(n_ctx, n_fsdp, block, positions, own, w_query, kv, w_out, gains, w_gate, w_up, upstream, tables):
    rows, width = own.shape
    length = rows * n_ctx
    weight_rows = kv.shape[0]
    total = weight_rows * n_fsdp
    query_width, out_width = w_query.shape[1] // n_ctx, width // n_ctx
    ff_rows = w_gate.shape[1] // n_fsdp
    heads, kv_heads = query_width // HEAD_DIM, kv.shape[1] // (2 * HEAD_DIM)
    tile = block * (4 if length <= 1024 else 2)
    shape = jax.ShapeDtypeStruct
    return communicate(
        functools.partial(forward_kernel, n_ctx, n_fsdp, tile),
        1,
        "forward",
        (*positions, own, w_query, kv, w_out, gains, w_gate, w_up, upstream, *tables),
        [VMEM] * 2 + [ANY] * 8 + [VMEM] * 2,
        [
            shape((total, ff_rows), LOW),
            shape((total, ff_rows), LOW),
            shape((rows * n_fsdp, width), LOW),
            shape((total, query_width), LOW),
            shape((total, kv.shape[1]), LOW),
            shape((gains.shape[0] * n_fsdp, gains.shape[1]), jnp.float32),
            shape((total // n_ctx, width), LOW),
            shape((length, width), LOW),
            shape((heads, length, HEAD_DIM), LOW),
            shape((kv_heads, length, HEAD_DIM), LOW),
            shape((kv_heads, length, HEAD_DIM), LOW),
            shape((length, 128), jnp.float32),
            shape((length, query_width), LOW),
            shape((rows, width), jnp.float32),
            shape((rows * n_fsdp, width), LOW),
        ],
        [ANY] * 3 + [VMEM] * 12,
        [
            pltpu.VMEM((length, width), LOW),
            pltpu.VMEM((total, out_width), LOW),
            pltpu.VMEM((heads, length, HEAD_DIM), LOW),
            pltpu.VMEM((length, query_width + kv.shape[1]), LOW),
            pltpu.VMEM((length, width), LOW),
        ]
        + cube_scratch(n_ctx, rows, width)
        + [pltpu.SemaphoreType.DMA((8,))],
        5 * (n_ctx - 1) + 14 * (n_fsdp - 1) + 2 * (n_fsdp - 1),
        160,
    )


def backward_kernel(
    n_ctx,
    n_fsdp,
    tile,
    pos_row,
    pos_column,
    mlp_part,
    down_part,
    out_part,
    own,
    upstream,
    resid,
    gain_mlp,
    gain_attn,
    w_q,
    w_kv,
    w_out,
    cosine,
    sine,
    q_heads,
    k_head,
    v_head,
    logs,
    attended,
    down_all,
    grad_out,
    d_joined,
    d_own,
    output,
    terms,
    seq,
    d_resid,
    line_land,
    total,
    out_land,
    out_total,
    down_land,
    land,
    acc,
    joined,
    d_heads,
    dq_heads,
    dk_head,
    dv_head,
    local_sem,
    send_sems,
    recv_sems,
):
    links = Links(n_ctx, n_fsdp, send_sems, recv_sems)
    rows, down_rows = own.shape[0], down_all.shape[0] // n_ctx
    length, query_width, kv_width = seq.shape[0], w_q.shape[1], w_kv.shape[1] // 2
    tiles = length // tile
    links.greet(cube=True, line=True)
    line = line_sum(links, mlp_part, line_land, total, rows)
    summed_here = out_part.shape[0] > rows
    line_out = line_sum(links, out_part, out_land, out_total, rows) if summed_here else iter(())
    down_here = down_part.shape[0] > down_rows
    plane_down = cube_sum(links, down_part, down_land, acc, down_rows) if down_here else iter(())
    in_turns(line, plane_down, plane_down, line, line, plane_down)
    finish(line)
    d_normed = swap_order(total[...], n_ctx, n_fsdp)
    value = resid[...]
    scale = lax.rsqrt(jnp.mean(value * value, axis=1, keepdims=True) + EPS)
    unit = value * scale
    terms[1:2, :] = jnp.sum(d_normed * unit, axis=0, keepdims=True)
    value = upstream[...].astype(jnp.float32) + norm_back(d_normed, gain_mlp[...], unit, scale)
    d_resid[...] = value
    rows_of(seq, links.ctx, rows)[...] = value.astype(LOW)
    plane = cube_gather(links, seq, rows)
    in_turns(plane, line_out)
    finish(plane_down)
    if down_here:
        down_land[pl.ds(0, down_rows), :] = acc[pl.ds(0, down_rows), :].astype(LOW)
    down_low = down_land.at[pl.ds(0, down_rows)] if down_here else down_part
    mine = pltpu.make_async_copy(down_low, rows_of(down_all, links.ctx, down_rows), local_sem)
    mine.start()
    finish(plane)
    mine.wait()
    plane_all = cube_gather(links, down_all, down_rows)
    in_turns(plane_all, line_out)
    grad_rows = pl.ds(0, query_width)
    acc[grad_rows, :] = jnp.zeros((query_width, acc.shape[1]), jnp.float32)

    def begin(at, carry):
        here = pl.ds(pl.multiple_of(at * tile, tile), tile)
        mine = seq[here, :]
        acc[grad_rows, :] += dot_dims(attended[here, :], mine, 0, 0)
        joined[here, pl.ds(0, query_width)] = dot_dims(mine, w_out[...], 1, 1).astype(LOW)
        return carry

    lax.fori_loop(0, tiles, begin, 0)

    def sort(at, carry):
        here = pl.ds(pl.multiple_of(at * tile, tile), tile)
        moved = dot(to_positions(pos_row, at, tile), joined[:, pl.ds(0, query_width)]).astype(LOW)
        split_heads(moved, d_heads, here)
        return carry

    lax.fori_loop(0, tiles, sort, 0)
    grad_out[...] = acc[grad_rows, :].astype(LOW)
    services = [
        lambda: in_turns(line_out),
        lambda: in_turns(plane_all, line_out),
        lambda: in_turns(plane_all),
    ]

    def service():
        if services:
            services.pop(0)()

    attend_back(q_heads, k_head, v_head, d_heads, logs, dq_heads, dk_head, dv_head, tile, service)
    while services:
        service()

    def end(at, carry):
        here = pl.ds(pl.multiple_of(at * tile, tile), tile)
        cos, sin = cosine[here, :], sine[here, :]
        d_query = turned(side_by_side(dq_heads, here), cos, sin, True)
        joined[here, pl.ds(0, query_width)] = d_query.astype(LOW)
        both = jnp.concatenate([side_by_side(dk_head, here), side_by_side(dv_head, here)], axis=1)
        keys = lanes(both.shape) < kv_width
        both = jnp.where(keys, turned(both, cos, sin, True), both)
        joined[here, pl.ds(query_width, 2 * kv_width)] = both.astype(LOW)
        return carry

    lax.fori_loop(0, tiles, end, 0)

    def out(at, carry):
        here = pl.ds(pl.multiple_of(at * tile, tile), tile)
        moved = dot(to_slots(pos_column, here, tile), joined[...]).astype(LOW)
        d_joined[here, :] = moved
        both = dot_dims(moved[:, :query_width], w_q[...], 1, 1)
        both += dot_dims(moved[:, query_width:], w_kv[...], 1, 1)
        seq[here, :] = both.astype(LOW)
        return carry

    lax.fori_loop(0, tiles, out, 0)
    plane = cube_sum(links, seq, land, acc, rows)
    in_turns(plane)
    finish(line_out)
    out_sum = out_total[...] if summed_here else out_part[...].astype(jnp.float32)
    output[...] = (resid[...] + out_sum).astype(LOW)
    in_turns(plane, plane)
    finish(plane)
    d_normed = acc[pl.ds(0, rows), :]
    value = own[...].astype(jnp.float32)
    scale = lax.rsqrt(jnp.mean(value * value, axis=1, keepdims=True) + EPS)
    unit = value * scale
    terms[0:1, :] = jnp.sum(d_normed * unit, axis=0, keepdims=True)
    d_own[...] = (d_resid[...] + norm_back(d_normed, gain_attn[...], unit, scale)).astype(LOW)
    finish(plane_all)


def backward(
    n_ctx, n_fsdp, block, positions, parts, own, upstream, resid, gains, weights, tables, saved
):
    rows, width = own.shape
    length = rows * n_ctx
    down_here = length <= 1024
    down_rows = parts[1].shape[0] // (n_ctx if down_here else 1)
    q_heads, k_head = saved[0], saved[1]
    joined_width = weights[0].shape[1] + weights[1].shape[1]
    tile = block * (4 if length <= 1024 else 2)
    shape = jax.ShapeDtypeStruct
    wide = jnp.float32
    return communicate(
        functools.partial(backward_kernel, n_ctx, n_fsdp, tile),
        3,
        "backward",
        (*positions, *parts, own, upstream, resid, *gains, *weights, *tables, *saved),
        [VMEM] * 20,
        [
            shape((down_rows * n_ctx, width), LOW),
            shape((weights[0].shape[1], width), LOW),
            shape((length, joined_width), LOW),
            shape((rows, width), LOW),
            shape((rows, width), LOW),
            shape((2, width), wide),
        ],
        [ANY] + [VMEM] * 5,
        [pltpu.VMEM((length, width), LOW), pltpu.VMEM((rows, width), wide)]
        + line_scratch(n_fsdp, rows, width)
        + (line_scratch(n_fsdp, rows, width) if parts[2].shape[0] > rows else line_scratch(2, 8, 128))
        + (cube_scratch(n_ctx, down_rows, width)[:1] if down_here else cube_scratch(2, 16, 128)[:1])
        + cube_scratch(n_ctx, rows, width)[:1]
        + [
            pltpu.VMEM((max(max(1, n_ctx // 4) * max(rows, down_rows), weights[0].shape[1]), width), wide),
            pltpu.VMEM((length, joined_width), LOW),
            pltpu.VMEM(q_heads.shape, LOW),
            pltpu.VMEM(q_heads.shape, wide),
            pltpu.VMEM(k_head.shape, wide),
            pltpu.VMEM(k_head.shape, wide),
            pltpu.SemaphoreType.DMA(()),
        ],
        4 * (n_ctx - 1) + 4 * (n_fsdp - 1),
        160,
    )


def feed_forward_kernel(
    normed, upstream, w_gate, w_up, w_down, d_part, out_part, down, pair, flipped, d_acc, out_acc, held, sems
):
    at, steps = pl.program_id(0), pl.num_programs(0)
    chunk, ff_rows = w_gate.shape[1], pair.shape[1] // 2
    slot = lax.rem(at, 2)

    def leave(which, part, step):
        column = pl.multiple_of(part * ff_rows + step * chunk, chunk)
        return pltpu.make_async_copy(
            held.at[which, part], pair.at[:, pl.ds(column, chunk)], sems.at[which, part]
        )

    @pl.when(at == 0)
    def _():
        flipped[...] = normed[...].T
        d_acc[...] = jnp.zeros_like(d_acc)
        out_acc[...] = jnp.zeros_like(out_acc)

    gate_pre, up_pre = dot(normed[...], w_gate[...]), dot(normed[...], w_up[...])
    sigma = 1.0 / (1.0 + jnp.exp(-gate_pre))
    swish = gate_pre * sigma
    hidden = (swish * up_pre).astype(LOW)
    d_hidden = dot_dims(upstream[...], w_down[...], 1, 1)
    d_gate = (d_hidden * up_pre * sigma * (1.0 + gate_pre * (1.0 - sigma))).astype(LOW)
    d_up = (d_hidden * swish).astype(LOW)
    down[...] = dot_dims(hidden, upstream[...], 0, 0).astype(LOW)

    @pl.when(at >= 2)
    def _():
        for part in (0, 1):
            leave(slot, part, at - 2).wait()

    held[slot, 0] = dot(flipped[...], d_gate).astype(LOW)
    held[slot, 1] = dot(flipped[...], d_up).astype(LOW)
    for part in (0, 1):
        leave(slot, part, at).start()
    d_acc[...] += dot_dims(d_gate, w_gate[...], 1, 1) + dot_dims(d_up, w_up[...], 1, 1)
    out_acc[...] += dot(hidden, w_down[...])

    @pl.when(at == steps - 1)
    def _():
        d_part[...] = d_acc[...].astype(LOW)
        out_part[...] = out_acc[...].astype(LOW)

        @pl.when(steps > 1)
        def _():
            for part in (0, 1):
                leave(1 - slot, part, at - 1).wait()

        for part in (0, 1):
            leave(slot, part, at).wait()


def feed_forward(normed, upstream, w_gate, w_up, w_down):
    count, width = normed.shape
    ff_rows = w_down.shape[0]
    chunk = min(ff_rows, 512 if count <= 512 else 256)
    whole = pl.BlockSpec((count, width), lambda f: (0, 0), pipeline_mode=pl.Buffered(1))
    tall = pl.BlockSpec((width, chunk), lambda f: (0, f))
    flat = pl.BlockSpec((chunk, width), lambda f: (f, 0))
    shape = jax.ShapeDtypeStruct
    return pl.pallas_call(
        feed_forward_kernel,
        grid=(ff_rows // chunk,),
        in_specs=[whole, whole, tall, tall, flat],
        out_specs=[whole, whole, flat, ANY],
        out_shape=[
            shape((count, width), LOW),
            shape((count, width), LOW),
            shape((ff_rows, width), LOW),
            shape((width, 2 * ff_rows), LOW),
        ],
        scratch_shapes=[
            pltpu.VMEM((width, count), LOW),
            pltpu.VMEM((count, width), jnp.float32),
            pltpu.VMEM((count, width), jnp.float32),
            pltpu.VMEM((2, 2, width, chunk), LOW),
            pltpu.SemaphoreType.DMA((2, 2)),
        ],
        compiler_params=pltpu.CompilerParams(vmem_limit_bytes=60 << 20),
        cost_estimate=pl.CostEstimate(flops=0, bytes_accessed=150_000_000, transcendentals=0),
        name="feed_forward",
    )(normed, upstream, w_gate, w_up, w_down)


class ChunkSum:
    def __init__(self, links, land, rows):
        self.links, self.land, self.rows = links, land, rows
        self.count = links.n_ctx // 2
        self.levels = len(links.order) + 1
        self.offsets, self.theirs = [0], [0]
        for step, other in zip(links.order, links.order[::-1]):
            self.offsets = self.offsets + [offset + step for offset in self.offsets]
            self.theirs = self.theirs + [offset + other for offset in self.theirs]

    def first(self, level):
        return sum(self.count >> done for done in range(level))

    def spot(self, chunk, at):
        return pl.multiple_of((chunk * (self.links.n_ctx - 1) + at) * self.rows, self.rows)

    def transfer(self, part, chunk, level, at):
        links = self.links
        target = self.land.at[pl.ds(self.spot(chunk, self.first(level) + at), self.rows)]
        if level == 0:
            source = rows_of(part, links.ctx + links.sibling + self.theirs[at], self.rows)
            step = links.sibling
        else:
            source = self.land.at[pl.ds(self.spot(chunk, at + (self.count >> level)), self.rows)]
            step = links.order[len(links.order) - level]
        links.used = chunk * (links.n_ctx - 1) + self.first(level) + at
        return links.copy(source, target, links.ctx + step, links.fsdp)

    def start(self, part, chunk):
        for at in range(self.count):
            self.transfer(part, chunk, 0, at).start()

    def sent(self, part, chunk, level):
        for at in range(self.count >> level):
            self.transfer(part, chunk, level, at).wait_send()

    def meet(self, part, chunk, level, leave):
        count = self.count >> level
        half = count // 2
        wide = jnp.float32
        for at in list(range(half, count)) + list(range(half)):
            self.transfer(part, chunk, level, at).wait_recv()
            kept, landing = self.spot(chunk, at), self.spot(chunk, self.first(level) + at)

            def add(start, size):
                landed = self.land[pl.ds(pl.multiple_of(landing + start, size), size), :].astype(wide)
                place = pl.ds(pl.multiple_of(kept + start, size), size)
                if level == 0:
                    base = (self.links.ctx + self.offsets[at]) * self.rows
                    mine = part[pl.ds(pl.multiple_of(base + start, size), size), :]
                else:
                    mine = self.land[place, :]
                total = mine.astype(wide) + landed
                if count == 1:
                    leave(start, size, total)
                else:
                    self.land[place, :] = total.astype(LOW)

            in_rows(self.rows, add)
            if count > 1 and at >= half:
                self.transfer(part, chunk, level + 1, at - half).start()


def feed_forward_sum_kernel(
    n_ctx,
    n_fsdp,
    normed,
    upstream,
    w_gate,
    w_up,
    w_down,
    d_part,
    out_part,
    down,
    pair,
    flipped,
    d_acc,
    out_acc,
    held,
    land,
    local_sems,
    send_sems,
    recv_sems,
):
    at, steps = pl.program_id(0), w_down.shape[0]
    chunk, ff_rows, width = w_gate.shape[1], pair.shape[2], normed.shape[1]
    count, steps = normed.shape[0], pair.shape[2] // w_gate.shape[1]
    links = Links(n_ctx, n_fsdp, send_sems, recv_sems)
    sums = ChunkSum(links, land, width // n_ctx)
    slot, other = lax.rem(at, 2), lax.rem(at + 1, 2)
    last = sums.levels - 1

    def meet(step, level):
        part = held.at[lax.rem(step, 2)]
        column = pl.multiple_of(step * chunk, chunk)

        def leave(start, size, total):
            low = total.astype(LOW)
            for which in (0, 1):
                pair[which, pl.ds(start, size), pl.ds(column, chunk)] = low[:, which * chunk : (which + 1) * chunk]

        sums.meet(part, step, level, leave)

    @pl.when(at == 0)
    def _():
        links.greet(cube=True)
        flipped[...] = normed[...].T
        d_acc[...] = jnp.zeros_like(d_acc)
        out_acc[...] = jnp.zeros_like(out_acc)

    gate_pre, up_pre = dot(normed[...], w_gate[...]), dot(normed[...], w_up[...])
    sigma = 1.0 / (1.0 + jnp.exp(-gate_pre))
    swish = gate_pre * sigma
    hidden = (swish * up_pre).astype(LOW)
    d_hidden = dot_dims(upstream[...], w_down[...], 1, 1)
    d_gate = (d_hidden * up_pre * sigma * (1.0 + gate_pre * (1.0 - sigma))).astype(LOW)
    d_up = (d_hidden * swish).astype(LOW)

    @pl.when(at >= 1)
    def _():
        meet(at - 1, 0)

    @pl.when(at >= 2)
    def _():
        meet(at - 2, 1)
        sums.sent(held.at[slot], at - 2, 0)

    held[slot, :, pl.ds(0, chunk)] = dot(flipped[...], d_gate).astype(LOW)
    held[slot, :, pl.ds(chunk, chunk)] = dot(flipped[...], d_up).astype(LOW)
    sums.start(held.at[slot], at)
    down[...] = dot_dims(hidden, upstream[...], 0, 0).astype(LOW)
    d_acc[...] += dot_dims(d_gate, w_gate[...], 1, 1) + dot_dims(d_up, w_up[...], 1, 1)
    out_acc[...] += dot(hidden, w_down[...])
    for level in range(2, last + 1):

        @pl.when(at >= 2)
        def _():
            meet(at - 2, level)

    @pl.when(at == steps - 1)
    def _():
        meet(at, 0)
        meet(at - 1, 1)
        sums.sent(held.at[other], at - 1, 0)
        leaving = []
        for which, (acc, goal) in enumerate(((d_acc, d_part), (out_acc, out_part))):
            for piece in range(width // (2 * chunk)):
                spot = pl.ds((which * (width // (2 * chunk)) + piece) * count, count)
                columns = pl.ds(piece * 2 * chunk, 2 * chunk)
                held[other, spot, :] = acc[:, columns].astype(LOW)
                copy = pltpu.make_async_copy(
                    held.at[other, spot], goal.at[:, columns], local_sems.at[len(leaving)]
                )
                copy.start()
                leaving.append(copy)
        for level in range(2, last + 1):
            meet(at - 1, level)
        meet(at, 1)
        for level in range(2, last + 1):
            meet(at, level)
        sums.sent(held.at[slot], at, 0)
        for copy in leaving:
            copy.wait()
        for step in range(steps):
            for level in range(1, last + 1):
                sums.sent(held.at[0], step, level)


def feed_forward_sum(n_ctx, n_fsdp, normed, upstream, w_gate, w_up, w_down):
    count, width = normed.shape
    ff_rows = w_down.shape[0]
    chunk = 512
    steps, rows = ff_rows // chunk, width // n_ctx
    whole = pl.BlockSpec((count, width), lambda f: (0, 0), pipeline_mode=pl.Buffered(1))
    tall = pl.BlockSpec((width, chunk), lambda f: (0, f))
    flat = pl.BlockSpec((chunk, width), lambda f: (f, 0))
    both = pl.BlockSpec((2, rows, ff_rows), lambda f: (0, 0, 0), pipeline_mode=pl.Buffered(1))
    shape = jax.ShapeDtypeStruct
    copies = steps * (n_ctx - 1)
    return pl.pallas_call(
        functools.partial(feed_forward_sum_kernel, n_ctx, n_fsdp),
        grid=(steps,),
        in_specs=[whole, whole, tall, tall, flat],
        out_specs=[ANY, ANY, flat, both],
        out_shape=[
            shape((count, width), LOW),
            shape((count, width), LOW),
            shape((ff_rows, width), LOW),
            shape((2, rows, ff_rows), LOW),
        ],
        scratch_shapes=[
            pltpu.VMEM((width, count), LOW),
            pltpu.VMEM((count, width), jnp.float32),
            pltpu.VMEM((count, width), jnp.float32),
            pltpu.VMEM((2, width, 2 * chunk), LOW),
            pltpu.VMEM((copies * rows, 2 * chunk), LOW),
            pltpu.SemaphoreType.DMA((2 * width // (2 * chunk),)),
            pltpu.SemaphoreType.DMA((copies,)),
            pltpu.SemaphoreType.DMA((copies,)),
        ],
        compiler_params=pltpu.CompilerParams(
            collective_id=2, has_side_effects=True, vmem_limit_bytes=62 << 20
        ),
        name="feed_forward_sum",
    )(normed, upstream, w_gate, w_up, w_down)


def on_device(
    tokens,
    cotangent,
    pairing,
    norm_attn,
    w_query,
    w_key,
    w_value,
    w_out,
    norm_mlp,
    w_gate,
    w_up,
    w_down,
):
    n_ctx, n_fsdp = lax.axis_size("ctx"), lax.axis_size("fsdp")
    ctx = lax.axis_index("ctx")
    own_tokens = tokens[0]
    tok_rows, width = own_tokens.shape
    length = tok_rows * n_ctx
    rows_model = w_gate.shape[0]
    low = LOW

    query_width = w_query.shape[1] // n_ctx
    heads_kv = w_key.shape[1] // HEAD_DIM
    kv_here = max(1, heads_kv // n_ctx)
    sharers = max(1, n_ctx // heads_kv)
    kv_width = kv_here * HEAD_DIM
    kv_start = (ctx // sharers) * kv_width

    def columns(matrix, start, size):
        return lax.dynamic_slice_in_dim(matrix, start, size, 1)

    kv = jnp.concatenate([columns(w_key, kv_start, kv_width), columns(w_value, kv_start, kv_width)], axis=1)
    gains = jnp.zeros((8, rows_model), jnp.float32).at[0].set(norm_attn).at[1].set(norm_mlp)
    upstream = cotangent[0]
    block = tok_rows // pairing.shape[1]
    all_pos = slot_positions(pairing, length, block)
    positions = (all_pos[None, :], all_pos[:, None])

    def tables_at(places):
        return [jnp.tile(t[:, 0], (1, 128 // HEAD_DIM)) for t in rotation(places, HEAD_DIM)]

    (
        gate_full,
        up_full,
        upstream_all,
        w_q,
        w_kv,
        gains,
        w_out_rows,
        normed_attn,
        q_heads,
        k_head,
        v_head,
        logs,
        attended_low,
        resid,
        normed_mlp,
    ) = forward(
        n_ctx,
        n_fsdp,
        block,
        positions,
        own_tokens,
        w_query,
        kv,
        w_out,
        gains,
        w_gate,
        w_up,
        upstream,
        tables_at(all_pos),
    )
    gains = gains.reshape(n_fsdp, 8, rows_model)
    gain_attn, gain_mlp = gains[:, 0].reshape(1, -1), gains[:, 1].reshape(1, -1)
    out_width = width // n_ctx
    ff_rows = w_down.shape[0]
    strip = rows_model // n_ctx

    if length <= 1024:
        mlp_part, out_part, down_part, pair = feed_forward_sum(
            n_ctx, n_fsdp, normed_mlp, upstream_all, gate_full, up_full, w_down
        )
    else:
        mlp_part, out_part, down_part, pair = feed_forward(
            normed_mlp, upstream_all, gate_full, up_full, w_down
        )
        pair, down_part = scatter_sum(pair, "ctx"), scatter_sum(down_part, "ctx")
        pair = jnp.stack([pair[:, :ff_rows], pair[:, ff_rows:]])
        out_part = scatter_sum(out_part, "fsdp")

    grad_down, grad_out, d_joined, d_inputs, output, terms = backward(
        n_ctx,
        n_fsdp,
        block,
        positions,
        (mlp_part, down_part, out_part),
        own_tokens,
        upstream,
        resid,
        (gain_mlp, gain_attn),
        (w_q, w_kv, w_out_rows),
        tables_at(jnp.arange(length, dtype=jnp.int32)),
        (q_heads, k_head, v_head, logs, attended_low),
    )
    grad_joined = tokens_t(normed_attn, d_joined).astype(low)
    terms = terms.reshape(2, n_fsdp, rows_model)
    attn_width = query_width + 2 * kv_width + out_width
    pad = ((0, 0), (0, 14), (0, attn_width - rows_model))
    terms = jnp.pad(terms.transpose(1, 0, 2).astype(low), pad).reshape(n_fsdp * 16, attn_width)
    grad_gate, grad_up, grad_attn = tail(n_ctx, n_fsdp, pair, grad_joined, grad_out, terms)
    grad_gate, grad_up, grad_down = widen(grad_gate, grad_up, grad_down)
    grad_attn = grad_attn.reshape(n_ctx, rows_model + 16, attn_width)
    terms = jnp.sum(grad_attn[:, rows_model : rows_model + 2, :rows_model].astype(jnp.float32), axis=0)
    grad_query, grad_key, grad_value, grad_out = spread(
        grad_attn, rows_model, (query_width, kv_width, kv_width, out_width), (1, sharers, sharers, 1)
    )

    return (
        output[None],
        d_inputs[None],
        terms[0],
        grad_query,
        grad_key,
        grad_value,
        grad_out,
        terms[1],
        grad_gate,
        grad_up,
        grad_down,
    )


def solution(mesh):
    return jax.shard_map(
        on_device,
        mesh=mesh,
        in_specs=(
            P("fsdp", "ctx", None),
            P("fsdp", "ctx", None),
            P(),
            P("fsdp"),
            P("fsdp", None),
            P("fsdp", None),
            P("fsdp", None),
            P("fsdp", None),
            P("fsdp"),
            P("fsdp", None),
            P("fsdp", None),
            P("fsdp", None),
        ),
        out_specs=(
            P("fsdp", "ctx", None),
            P("fsdp", "ctx", None),
            P("fsdp"),
            P("fsdp", None),
            P("fsdp", None),
            P("fsdp", None),
            P("fsdp", None),
            P("fsdp"),
            P("fsdp", None),
            P("fsdp", None),
            P("fsdp", None),
        ),
        check_vma=False,
    )
```

```python
import functools
import math

import jax
import jax.numpy as jnp
from jax import lax
from jax.experimental import pallas as pl
from jax.experimental.pallas import tpu as pltpu
from jax.sharding import PartitionSpec as P

HEAD_DIM = 64


EPS = 1e-05
THETA = 500000.0


def frequencies(head_width):
    evens = jnp.arange(0, head_width, 2, dtype=jnp.float32)
    inverse = 1.0 / THETA ** (evens / head_width)
    wavelen = 2.0 * math.pi / inverse
    smooth = (8192.0 / wavelen - 1.0) / 3.0
    middle = (1.0 - smooth) * inverse / 32.0 + smooth * inverse
    return jnp.where(wavelen < 2048.0, inverse, jnp.where(wavelen > 8192.0, inverse / 32.0, middle))


def rotation(positions, head_width):
    angles = positions.astype(jnp.float32)[:, None] * frequencies(head_width)[None, :]
    cosine = jnp.concatenate([jnp.cos(angles), jnp.cos(angles)], axis=1)[:, None, :]
    sine = jnp.concatenate([jnp.sin(angles), jnp.sin(angles)], axis=1)[:, None, :]
    return (cosine, sine)


def rotate(tensor, cosine, sine):
    middle = tensor.shape[-1] // 2
    turned = jnp.concatenate([-tensor[..., middle:], tensor[..., :middle]], axis=-1)
    return tensor * cosine + turned * sine


def unrotate(gradient, cosine, sine):
    middle = gradient.shape[-1] // 2
    moved = gradient * sine
    back_turn = jnp.concatenate([moved[..., middle:], -moved[..., :middle]], axis=-1)
    return gradient * cosine + back_turn


def slot_positions(pairing, seq_length, block_len):
    flattened = pairing.reshape(-1)
    slots = jnp.arange(seq_length, dtype=jnp.int32)
    owning = slots // block_len
    labels = jnp.arange(flattened.shape[0], dtype=jnp.int32)
    anchor = jnp.sum(jnp.where(owning[:, None] == labels[None, :], flattened[None, :], 0), axis=1)
    return anchor * block_len + slots % block_len


def product(left, right):
    return jnp.dot(left, right, preferred_element_type=jnp.float32)


def product_t(left, right):
    return lax.dot_general(
        left, right, (((1,), (1,)), ((), ())), preferred_element_type=jnp.float32
    )


def tokens_t(left, right):
    return lax.dot_general(
        left, right, (((0,), (0,)), ((), ())), preferred_element_type=jnp.float32
    )


LOW = jnp.bfloat16
MESH = pl.DeviceIdType.MESH
ANY = pl.BlockSpec(memory_space=pl.ANY)
VMEM = pl.BlockSpec(memory_space=pltpu.VMEM)


def norm_back(upstream, gain, unit, scale):
    weighted = upstream * gain
    return scale * (weighted - unit * jnp.mean(weighted * unit, axis=1, keepdims=True))


def gather(array, axis):
    return lax.all_gather(array, axis, axis=0, tiled=True)


def scatter_sum(array, axis):
    return lax.psum_scatter(array, axis, scatter_dimension=0, tiled=True)


def einsum(spec, left, right):
    return jnp.einsum(spec, left, right, preferred_element_type=jnp.float32)


def swap_order(array, first, second):
    size = array.shape[1] // (first * second)
    parts = []
    for b in range(second):
        for a in range(first):
            at = (a * second + b) * size
            parts.append(array[:, at : at + size])
    return jnp.concatenate(parts, axis=1)


class Links:
    def __init__(self, n_ctx, n_fsdp, send_sems, recv_sems):
        self.n_ctx, self.n_fsdp = n_ctx, n_fsdp
        self.ctx, self.fsdp = lax.axis_index("ctx"), lax.axis_index("fsdp")
        self.send_sems, self.recv_sems = send_sems, recv_sems
        self.used = 0
        core = self.ctx % 2
        flips = [self.flip(d) for d in range(1, n_ctx.bit_length() - 1)]
        backward = flips[::-1]
        self.order = [(1 - core) * a + core * b for a, b in zip(flips, backward)]
        self.sibling = self.flip(0)

    def flip(self, digit):
        return 2**digit * (1 - 2 * ((self.ctx // 2**digit) % 2))

    def greet(self, cube=False, plane=False, line=False, whole_line=False):
        barrier = pltpu.get_barrier_semaphore()
        count = 0

        def hail(ctx, fsdp):
            pl.semaphore_signal(barrier, inc=1, device_id=(ctx, fsdp), device_id_type=MESH)

        if plane:
            for shift in range(1, self.n_ctx):
                hail(lax.rem(self.ctx + shift, self.n_ctx), self.fsdp)
            count += self.n_ctx - 1
        elif cube:
            for step in self.order + [self.sibling]:
                hail(self.ctx + step, self.fsdp)
            count += len(self.order) + 1
        if whole_line:
            for shift in range(1, self.n_fsdp):
                hail(self.ctx, lax.rem(self.fsdp + shift, self.n_fsdp))
            count += self.n_fsdp - 1
        if line and not whole_line:
            for step in (-1, 1):
                inside = jnp.logical_and(self.fsdp + step >= 0, self.fsdp + step < self.n_fsdp)

                @pl.when(inside)
                def _():
                    hail(self.ctx, self.fsdp + step)

            ends = jnp.logical_or(self.fsdp == 0, self.fsdp == self.n_fsdp - 1)
            pl.when(ends)(lambda: pl.semaphore_wait(barrier, count + 1))
            pl.when(jnp.logical_not(ends))(lambda: pl.semaphore_wait(barrier, count + 2))
        else:
            pl.semaphore_wait(barrier, count)

    def copies(self, sources, target, ctx, fsdp):
        slot = self.used
        self.used += 1
        return [
            pltpu.make_async_remote_copy(
                src_ref=source,
                dst_ref=target,
                send_sem=self.send_sems.at[slot],
                recv_sem=self.recv_sems.at[slot],
                device_id=(ctx, fsdp),
                device_id_type=MESH,
            )
            for source in sources
        ]

    def copy(self, source, target, ctx, fsdp):
        return self.copies((source,), target, ctx, fsdp)[0]


def rows_of(ref, index, rows):
    return ref.at[pl.ds(pl.multiple_of(index * rows, rows), rows)]


def in_turns(*walks):
    for walk in walks:
        next(walk, None)


def finish(*walks):
    for walk in walks:
        for _ in walk:
            pass


def cube_gather(links, ref, rows):
    held, sent, shared = [0], [], []

    def send(offset, step):
        block = rows_of(ref, links.ctx + offset, rows)
        copy = links.copy(block, block, links.ctx + step, links.fsdp)
        copy.start()
        return copy

    fresh = held
    for step in links.order:
        copies = [send(offset, step) for offset in held]
        shared += [send(offset, links.sibling) for offset in fresh]
        yield
        for copy in copies:
            copy.wait_recv()
        sent += copies
        fresh = [offset + step for offset in held]
        held = held + fresh
    shared += [send(offset, links.sibling) for offset in fresh]
    yield
    for copy in shared:
        copy.wait_recv()
    for copy in sent + shared:
        copy.wait_send()


def in_rows(rows, body):
    size = math.gcd(rows, 64)

    def step(at, carry):
        body(pl.multiple_of(at * size, size), size)
        return carry

    lax.fori_loop(0, rows // size, step, 0)


def cube_sum(links, part, land, acc, rows):
    offsets, theirs = [0], [0]
    for step, other in zip(links.order, links.order[::-1]):
        offsets = offsets + [offset + step for offset in offsets]
        theirs = theirs + [offset + other for offset in theirs]
    wide = jnp.float32
    sent, pending = [], []
    for at, offset in enumerate(theirs):
        source = rows_of(part, links.ctx + links.sibling + offset, rows)
        target = land.at[pl.ds(at * rows, rows)]
        copy = links.copy(source, target, links.ctx + links.sibling, links.fsdp)
        copy.start()
        pending.append(copy)
    yield
    land_from, land_at = 0, len(offsets)
    for level in range(len(links.order) + 1):
        count = len(offsets)
        half = count // 2
        onward = []
        for at in list(range(half, count)) + list(range(half)):
            pending[at].wait_recv()
            first, place = level == 0, (land_from + at) * rows
            goes = at >= half and count > 1

            def add(start, size, at=at, place=place, first=first, goes=goes):
                landed = land[pl.ds(place + start, size), :].astype(wide)
                if first:
                    base = (links.ctx + offsets[at]) * rows
                    mine = part[pl.ds(pl.multiple_of(base + start, size), size), :].astype(wide)
                else:
                    mine = acc[pl.ds(at * rows + start, size), :]
                if goes:
                    land[pl.ds(place + start, size), :] = (mine + landed).astype(LOW)
                else:
                    acc[pl.ds(at * rows + start, size), :] = mine + landed

            in_rows(rows, add)
            if goes:
                source = land.at[pl.ds(place, rows)]
                target = land.at[pl.ds((land_at + at - half) * rows, rows)]
                step = links.order[len(links.order) - 1 - level]
                copy = links.copy(source, target, links.ctx + step, links.fsdp)
                copy.start()
                onward.append(copy)
        sent += pending
        pending, land_from = onward, land_at
        land_at += half
        offsets = offsets[: max(half, 1)]
        if level < len(links.order):
            yield
    for copy in sent:
        copy.wait_send()


def cube_scratch(n_ctx, rows, width):
    return [
        pltpu.VMEM(((n_ctx - 1) * rows, width), LOW),
        pltpu.VMEM((max(1, n_ctx // 4) * rows, width), jnp.float32),
    ]


def line_gather(links, refs, rows):
    count, me = links.n_fsdp, links.fsdp
    sends = []
    for hop in range(count - 1):
        receives = []
        for ref, size in zip(refs, rows):
            up_block = rows_of(ref, me - hop, size)
            down_block = rows_of(ref, me + hop, size)
            up = links.copy(up_block, up_block, links.ctx, me + 1)
            down = links.copy(down_block, down_block, links.ctx, me - 1)
            up_ok = jnp.logical_and(me >= hop, me < count - 1)
            down_ok = jnp.logical_and(me <= count - 1 - hop, me > 0)
            pl.when(up_ok)(up.start)
            pl.when(down_ok)(down.start)
            sends += [(up_ok, up), (down_ok, down)]
            receives += [(me >= hop + 1, up), (me <= count - 2 - hop, down)]
        yield
        for ok, copy in receives:
            pl.when(ok)(copy.wait_recv)
    for ok, copy in sends:
        pl.when(ok)(copy.wait_send)


def line_sum(links, part, land, total, rows):
    count, me = links.n_fsdp, links.fsdp
    flows = []
    for hop in range(count - 1):
        for side in (0, 1):
            goal = count - 1 - hop if side == 0 else hop
            slot = (side * (count - 1) + hop) * rows
            landing = land.at[pl.ds(slot, rows)]
            fed = me > 0 if side == 0 else me < count - 1
            passes = me < goal if side == 0 else me > goal
            peer = me + 1 if side == 0 else me - 1
            first, onward = links.copies((part.at[pl.ds(goal * rows, rows)], landing), landing, links.ctx, peer)
            flows.append((goal * rows, slot, onward, fed, passes, me == goal))
            pl.when(jnp.logical_and(passes, jnp.logical_not(fed)))(first.start)

    total[...] = rows_of(part, me, rows)[...].astype(jnp.float32)
    lower = me < count // 2
    for hop in range(count - 1):
        yield
        for near in (0, 1):

            @pl.when(lower if near == 0 else jnp.logical_not(lower))
            def _():
                for way in (near, 1 - near):
                    base, slot, onward, fed, passes, _ = flows[2 * hop + way]

                    @pl.when(jnp.logical_and(passes, fed))
                    def _():
                        onward.wait_recv()

                        def add(start, size):
                            own = part[pl.ds(base + start, size), :].astype(jnp.float32)
                            landed = land[pl.ds(slot + start, size), :].astype(jnp.float32)
                            land[pl.ds(slot + start, size), :] = (own + landed).astype(LOW)

                        in_rows(rows, add)
                        onward.start()

    yield
    for base, slot, onward, fed, passes, mine in flows:

        @pl.when(jnp.logical_and(mine, fed))
        def _():
            onward.wait_recv()

            def add(start, size):
                landed = land[pl.ds(slot + start, size), :].astype(jnp.float32)
                total[pl.ds(start, size), :] += landed

            in_rows(rows, add)

    for base, slot, onward, fed, passes, _ in flows:
        pl.when(passes)(onward.wait_send)


def line_scratch(n_fsdp, rows, width):
    return [
        pltpu.VMEM((2 * (n_fsdp - 1) * rows, width), LOW),
        pltpu.VMEM((rows, width), jnp.float32),
    ]


def communicate(kernel, collective_id, name, operands, in_specs, outs, out_specs, scratch, copies, busy):
    return pl.pallas_call(
        kernel,
        out_shape=outs,
        in_specs=in_specs,
        out_specs=out_specs,
        scratch_shapes=scratch
        + [pltpu.SemaphoreType.DMA((copies,)), pltpu.SemaphoreType.DMA((copies,))],
        compiler_params=pltpu.CompilerParams(
            collective_id=collective_id, has_side_effects=True, vmem_limit_bytes=62 << 20
        ),
        cost_estimate=pl.CostEstimate(flops=0, bytes_accessed=busy * 3_000_000, transcendentals=0),
        name=name,
    )(*operands)


def tail_kernel(
    n_ctx,
    n_fsdp,
    pair,
    joined,
    out_part,
    terms,
    gate_all,
    up_all,
    attn_all,
    attn_part,
    land,
    total,
    attn_low,
    local_sems,
    send_sems,
    recv_sems,
):
    links = Links(n_ctx, n_fsdp, send_sems, recv_sems)
    strip, ff_rows = pair.shape[1] // n_fsdp, pair.shape[2]
    model_rows, term_rows = joined.shape[0] // n_fsdp, terms.shape[0] // n_fsdp
    rows = model_rows + term_rows
    head_rows, joined_width = out_part.shape[0], joined.shape[1]
    out_width = attn_part.shape[1] - joined_width
    heads_in = model_rows // head_rows

    def place(ref, ctx, fsdp):
        return ref.at[
            pl.ds(pl.multiple_of(ctx * strip, strip), strip),
            pl.ds(pl.multiple_of(fsdp * ff_rows, ff_rows), ff_rows),
        ]

    def strip_of(part, fsdp):
        return pair.at[part, pl.ds(pl.multiple_of(fsdp * strip, strip), strip)]

    def out_column(ctx):
        return out_part.at[:, pl.ds(pl.multiple_of(ctx * out_width, out_width), out_width)]

    out_from = (links.ctx // heads_in) * rows + lax.rem(links.ctx, heads_in) * head_rows
    out_place = attn_part.at[
        pl.ds(pl.multiple_of(out_from, 16), head_rows), pl.ds(joined_width, out_width)
    ]
    moves = [
        (strip_of(0, links.fsdp), place(gate_all, links.ctx, links.fsdp)),
        (strip_of(1, links.fsdp), place(up_all, links.ctx, links.fsdp)),
        (out_column(links.ctx), out_place),
    ]
    for fsdp in range(n_fsdp):
        moves.append(
            (
                joined.at[pl.ds(fsdp * model_rows, model_rows)],
                attn_part.at[pl.ds(fsdp * rows, model_rows), pl.ds(0, joined_width)],
            )
        )
        moves.append(
            (
                terms.at[pl.ds(fsdp * term_rows, term_rows)],
                attn_part.at[pl.ds(fsdp * rows + model_rows, term_rows)],
            )
        )
    local = [pltpu.make_async_copy(a, b, local_sems.at[i]) for i, (a, b) in enumerate(moves)]
    for copy in local:
        copy.start()
    links.greet(plane=True, line=True, whole_line=True)
    to_shards = []
    for part, goal in enumerate((gate_all, up_all)):
        copies = []
        for shift in range(1, n_fsdp):
            target = lax.rem(links.fsdp + shift, n_fsdp)
            copy = links.copy(
                strip_of(part, target), place(goal, links.ctx, links.fsdp), links.ctx, target
            )
            copy.start()
            copies.append(copy)
        to_shards.append(copies)
    to_plane = []
    for shift in range(1, n_ctx):
        target = lax.rem(links.ctx + shift, n_ctx)
        copy = links.copy(out_column(target), out_place, target, links.fsdp)
        copy.start()
        to_plane.append(copy)
    for copy in local:
        copy.wait()
    for copy in to_plane:
        copy.wait()
    for copy in to_shards[0]:
        copy.wait()
    plane_gate = cube_gather(links, gate_all, strip)
    in_turns(plane_gate)
    line = line_sum(links, attn_part, land, total, rows)
    in_turns(line)
    for copy in to_shards[1]:
        copy.wait()
    plane_up = cube_gather(links, up_all, strip)
    in_turns(plane_up, plane_gate, line, line, plane_gate, plane_up, line)
    finish(line)
    attn_low[...] = total[...].astype(LOW)
    mine = pltpu.make_async_copy(attn_low, rows_of(attn_all, links.ctx, rows), local_sems.at[0])
    mine.start()
    mine.wait()
    plane_attn = cube_gather(links, attn_all, rows)
    in_turns(plane_attn, plane_up, plane_attn)
    finish(plane_gate, plane_up, plane_attn)


def tail(n_ctx, n_fsdp, pair, joined, out_part, terms):
    strip, ff_rows = pair.shape[1] // n_fsdp, pair.shape[2]
    rows = (joined.shape[0] + terms.shape[0]) // n_fsdp
    attn_width = joined.shape[1] + out_part.shape[1] // n_ctx
    shape = lambda *dims: jax.ShapeDtypeStruct(dims, LOW)
    return communicate(
        functools.partial(tail_kernel, n_ctx, n_fsdp),
        5,
        "tail",
        (pair, joined, out_part, terms),
        [ANY] * 4,
        [
            shape(strip * n_ctx, ff_rows * n_fsdp),
            shape(strip * n_ctx, ff_rows * n_fsdp),
            shape(rows * n_ctx, attn_width),
        ],
        [ANY] * 3,
        [pltpu.VMEM((rows * n_fsdp, attn_width), LOW)]
        + line_scratch(n_fsdp, rows, attn_width)
        + [pltpu.VMEM((rows, attn_width), LOW), pltpu.SemaphoreType.DMA((3 + 2 * n_fsdp,))],
        4 * (n_ctx - 1) + 4 * (n_fsdp - 1),
        130,
    )


def widen_kernel(widths, sharers, gathered, *refs):
    count = (len(refs) - len(widths)) // 2
    for source, goal in zip(refs[:count], refs[count : 2 * count]):
        goal[...] = source[...].astype(jnp.float32)
    at = 0
    for out, width, group in zip(refs[2 * count :], widths, sharers):
        pieces = []
        for i in range(0, gathered.shape[0], group):
            piece = gathered[i, :, at : at + width].astype(jnp.float32)
            for j in range(1, group):
                piece = piece + gathered[i + j, :, at : at + width].astype(jnp.float32)
            pieces.append(piece)
        out[...] = jnp.concatenate(pieces, axis=1)
        at += width


def widen(gathered, rows, widths, sharers, *arrays):
    n_ctx, _, joined = gathered.shape
    step = 2 * max(sharers)
    steps = n_ctx // step
    specs = [pl.BlockSpec((a.shape[0] // steps, a.shape[1]), lambda i: (i, 0)) for a in arrays]
    shape = lambda *dims: jax.ShapeDtypeStruct(dims, jnp.float32)
    return pl.pallas_call(
        functools.partial(widen_kernel, widths, sharers),
        grid=(steps,),
        in_specs=[pl.BlockSpec((step, rows, joined), lambda i: (i, 0, 0))] + specs,
        out_specs=specs
        + [pl.BlockSpec((rows, step // s * w), lambda i: (0, i)) for w, s in zip(widths, sharers)],
        out_shape=[shape(*a.shape) for a in arrays]
        + [shape(rows, n_ctx // s * w) for w, s in zip(widths, sharers)],
        compiler_params=pltpu.CompilerParams(vmem_limit_bytes=60 << 20),
        name="widen",
    )(gathered, *arrays)


def lanes(shape):
    return lax.broadcasted_iota(jnp.int32, shape, 1)


def halves(tensor, back):
    half = HEAD_DIM // 2
    width = tensor.shape[1]
    later, earlier = pltpu.roll(tensor, width - half, 1), pltpu.roll(tensor, half, 1)
    first = lanes(tensor.shape) % HEAD_DIM < half
    return jnp.where(first, later, -earlier) if back else jnp.where(first, -later, earlier)


def turned(tensor, cosine, sine, back=False):
    parts = []
    for at in range(0, tensor.shape[1], 128):
        piece = tensor[:, at : at + 128]
        if back:
            parts.append(piece * cosine + halves(piece * sine, True))
        else:
            parts.append(piece * cosine + halves(piece, False) * sine)
    return parts[0] if len(parts) == 1 else jnp.concatenate(parts, axis=1)


def dot(left, right):
    return jnp.dot(left, right, preferred_element_type=jnp.float32)


def dot_dims(left, right, left_dim, right_dim):
    dims = (((left_dim,), (right_dim,)), ((), ()))
    return lax.dot_general(left, right, dims, preferred_element_type=jnp.float32)


def to_positions(pos_row, at, tile):
    shape = (tile, pos_row.shape[1])
    here = lax.broadcasted_iota(jnp.int32, shape, 0) + at * tile
    return jnp.where(here == pos_row[...], 1.0, 0.0).astype(LOW)


def to_slots(pos_column, rows, tile):
    shape = (tile, pos_column.shape[0])
    return jnp.where(lanes(shape) == pos_column[rows, :], 1.0, 0.0).astype(LOW)


def project(seq, gain, w_q, w_kv, cosine, sine, normed, joined, tile, start, stop):
    query_width, kv_width = w_q.shape[1], w_kv.shape[1] // 2

    def step(at, carry):
        rows = pl.ds(pl.multiple_of(at * tile, tile), tile)
        wide = seq[rows, :].astype(jnp.float32)
        scale = lax.rsqrt(jnp.mean(wide * wide, axis=1, keepdims=True) + EPS)
        low = (wide * scale * gain).astype(LOW)
        normed[rows, :] = low
        cos, sin = cosine[rows, :], sine[rows, :]
        joined[rows, pl.ds(0, query_width)] = turned(dot(low, w_q[...]), cos, sin).astype(LOW)
        both = dot(low, w_kv[...])
        both = jnp.where(lanes(both.shape) < kv_width, turned(both, cos, sin), both)
        joined[rows, pl.ds(query_width, 2 * kv_width)] = both.astype(LOW)
        return carry

    lax.fori_loop(start, stop, step, 0)


def in_order(pos_row, joined, q_heads, k_head, v_head, tile):
    query_width = q_heads.shape[0] * HEAD_DIM
    kv_width = k_head.shape[0] * HEAD_DIM

    def step(at, carry):
        rows = pl.ds(pl.multiple_of(at * tile, tile), tile)
        moved = dot(to_positions(pos_row, at, tile), joined[...]).astype(LOW)
        split_heads(moved[:, :query_width], q_heads, rows)
        split_heads(moved[:, query_width : query_width + kv_width], k_head, rows)
        split_heads(moved[:, query_width + kv_width :], v_head, rows)
        return carry

    lax.fori_loop(0, joined.shape[0] // tile, step, 0)


def scores_of(queries, keys, tile):
    logits = dot_dims(queries, keys, 1, 1) * (HEAD_DIM**-0.5)
    last = logits[:, -tile:]
    seen = lax.broadcasted_iota(jnp.int32, last.shape, 0) >= lanes(last.shape)
    last = jnp.where(seen, last, -1e30)
    before = logits.shape[1] - tile
    return last if before == 0 else jnp.concatenate([logits[:, :before], last], axis=1)


def attend(q_heads, k_head, v_head, out_heads, logs, tile, service):
    heads, length, _ = q_heads.shape
    group = heads // k_head.shape[0]
    for tile_at in range(length // tile):
        here, keys = pl.ds(tile_at * tile, tile), (tile_at + 1) * tile
        logs[here, :] = jnp.zeros((tile, logs.shape[1]), jnp.float32)

        def step(head, carry):
            scores = scores_of(q_heads[head, here, :], k_head[head // group, pl.ds(0, keys), :], tile)
            largest = jnp.max(scores, axis=1, keepdims=True)
            expo = jnp.exp(scores - largest)
            total = jnp.sum(expo, axis=1, keepdims=True)
            probs = (expo * (1.0 / total)).astype(LOW)
            out = dot(probs, v_head[head // group, pl.ds(0, keys), :])
            out_heads[head, here, :] = out.astype(LOW)
            log = largest + jnp.log(total)
            logs[here, :] += jnp.where(lanes((tile, logs.shape[1])) == head, log, 0.0)
            return carry

        lax.fori_loop(0, heads, step, 0)
        service()


def attend_back(q_heads, k_head, v_head, d_heads, logs, dq_heads, dk_head, dv_head, tile, service):
    heads, length, _ = q_heads.shape
    group = heads // k_head.shape[0]
    dk_head[...] = jnp.zeros_like(dk_head)
    dv_head[...] = jnp.zeros_like(dv_head)
    for tile_at in range(length // tile):
        here, keys = pl.ds(tile_at * tile, tile), (tile_at + 1) * tile

        def step(head, carry):
            queries, d_out = q_heads[head, here, :], d_heads[head, here, :]
            kept, seen = k_head[head // group, pl.ds(0, keys), :], v_head[head // group, pl.ds(0, keys), :]
            column = lanes((tile, logs.shape[1])) == head
            log = jnp.sum(jnp.where(column, logs[here, :], 0.0), axis=1, keepdims=True)
            probs = jnp.exp(scores_of(queries, kept, tile) - log)
            d_probs = dot_dims(d_out, seen, 1, 1)
            delta = jnp.sum(probs * d_probs, axis=1, keepdims=True)
            d_score = (probs * (d_probs - delta) * (HEAD_DIM**-0.5)).astype(LOW)
            dq_heads[head, here, :] = dot(d_score, kept)
            dk_head[head // group, pl.ds(0, keys), :] += dot_dims(d_score, queries, 0, 0)
            dv_head[head // group, pl.ds(0, keys), :] += dot_dims(probs.astype(LOW), d_out, 0, 0)
            return carry

        lax.fori_loop(0, heads, step, 0)
        service()


def side_by_side(ref, rows):
    return jnp.concatenate([ref[head, rows, :] for head in range(ref.shape[0])], axis=1)


def split_heads(value, ref, rows):
    for head in range(ref.shape[0]):
        ref[head, rows, :] = value[:, head * HEAD_DIM : (head + 1) * HEAD_DIM]


def forward_kernel(
    n_ctx,
    n_fsdp,
    tile,
    pos_row,
    pos_column,
    own,
    w_query,
    kv,
    w_out,
    gains,
    w_gate,
    w_up,
    upstream,
    cosine,
    sine,
    gate_all,
    up_all,
    upstream_all,
    q_all,
    kv_all,
    gains_all,
    out_rows,
    normed,
    q_heads,
    k_head,
    v_head,
    logs,
    attended,
    resid,
    normed_mlp,
    seq,
    cols_all,
    out_heads,
    joined,
    part,
    land,
    acc,
    local_sems,
    send_sems,
    recv_sems,
):
    links = Links(n_ctx, n_fsdp, send_sems, recv_sems)
    rows, weight_rows, query_width = own.shape[0], kv.shape[0], q_all.shape[1]
    head_rows, out_width = out_rows.shape[0], cols_all.shape[1]
    strip, ff_rows = weight_rows // n_ctx, gate_all.shape[1]
    length = normed.shape[0]

    def cut(ref, size):
        return ref.at[:, pl.ds(pl.multiple_of(links.ctx * size, size), size)]

    def strip_from(ref, fsdp):
        return ref.at[
            pl.ds(pl.multiple_of(links.ctx * strip, strip), strip),
            pl.ds(pl.multiple_of(fsdp * ff_rows, ff_rows), ff_rows),
        ]

    def strip_to(ref):
        return rows_of(ref, links.ctx * n_fsdp + links.fsdp, strip)

    moves = [
        (own, rows_of(seq, links.ctx, rows)),
        (cut(w_query, query_width), rows_of(q_all, links.fsdp, weight_rows)),
        (kv, rows_of(kv_all, links.fsdp, weight_rows)),
        (gains, rows_of(gains_all, links.fsdp, gains.shape[0])),
        (cut(w_out, out_width), rows_of(cols_all, links.fsdp, weight_rows)),
        (strip_from(w_gate, links.fsdp), strip_to(gate_all)),
        (strip_from(w_up, links.fsdp), strip_to(up_all)),
        (upstream, rows_of(upstream_all, links.fsdp, rows)),
    ]
    local = [pltpu.make_async_copy(a, b, local_sems.at[i]) for i, (a, b) in enumerate(moves)]
    for copy in local:
        copy.start()
    links.greet(plane=True, line=True, whole_line=True)
    for copy in local[:5]:
        copy.wait()
    plane = cube_gather(links, seq, rows)
    line = line_gather(links, [gains_all, q_all, kv_all], [gains.shape[0], weight_rows, weight_rows])
    cols = line_gather(links, [cols_all], [weight_rows])
    in_turns(plane, line, plane, line, plane, line)
    finish(line, plane)
    in_turns(cols)
    for copy in local[5:]:
        copy.wait()

    def gain_row(row):
        first = [gains_all[pl.ds(z * gains.shape[0] + row, 1), :] for z in range(n_fsdp)]
        return jnp.concatenate(first, axis=1)

    gain = gain_row(0)
    tiles = length // tile
    half = max(1, tiles // 2)
    slots = (seq, gain, q_all, kv_all, cosine, sine, normed, joined, tile)
    project(*slots, 0, half)
    in_turns(cols)
    project(*slots, half, tiles)
    in_order(pos_row, joined, q_heads, k_head, v_head, tile)

    to_plane, gate_strips, up_strips = [], [], []
    column = cut(out_rows, out_width)
    mine = pltpu.make_async_copy(rows_of(cols_all, links.ctx, head_rows), column, local_sems.at[0])

    def hand_out():
        finish(cols)
        mine.start()
        for shift in range(1, n_ctx):
            target = lax.rem(links.ctx + shift, n_ctx)
            copy = links.copy(rows_of(cols_all, target, head_rows), column, target, links.fsdp)
            copy.start()
            to_plane.append(copy)
        for source, goal, copies in ((w_gate, gate_all, gate_strips), (w_up, up_all, up_strips)):
            for shift in range(1, n_fsdp):
                target = lax.rem(links.fsdp + shift, n_fsdp)
                copy = links.copy(strip_from(source, target), strip_to(goal), links.ctx, target)
                copy.start()
                copies.append(copy)

    services = [lambda: in_turns(cols), lambda: in_turns(cols), hand_out]

    def service():
        if services:
            services.pop(0)()

    attend(q_heads, k_head, v_head, out_heads, logs, tile, service)
    while services:
        service()

    def join(at, carry):
        here = pl.ds(pl.multiple_of(at * tile, tile), tile)
        joined[here, pl.ds(0, query_width)] = side_by_side(out_heads, here)
        return carry

    lax.fori_loop(0, tiles, join, 0)
    mine.wait()
    for copy in to_plane:
        copy.wait()

    def out(at, carry):
        here = pl.ds(pl.multiple_of(at * tile, tile), tile)
        moved = dot(to_slots(pos_column, here, tile), joined[:, pl.ds(0, query_width)]).astype(LOW)
        attended[here, :] = moved
        part[here, :] = dot(moved, out_rows[...]).astype(LOW)
        return carry

    lax.fori_loop(0, tiles, out, 0)
    finish(cube_sum(links, part, land, acc, rows))
    value = acc[pl.ds(0, rows), :] + rows_of(seq, links.ctx, rows)[...].astype(jnp.float32)
    resid[...] = value
    scale = lax.rsqrt(jnp.mean(value * value, axis=1, keepdims=True) + EPS)
    low = swap_order((value * scale * gain_row(1)).astype(LOW), n_fsdp, n_ctx)
    rows_of(normed_mlp, links.fsdp, rows)[...] = low
    line_normed = line_gather(links, [normed_mlp], [rows])
    in_turns(line_normed)
    for copy in gate_strips:
        copy.wait()
    plane_gate = cube_gather(links, gate_all, strip * n_fsdp)
    in_turns(plane_gate, line_normed)
    for copy in up_strips:
        copy.wait()
    plane_up = cube_gather(links, up_all, strip * n_fsdp)
    line_upstream = line_gather(links, [upstream_all], [rows])
    in_turns(plane_gate, plane_up, line_normed, line_upstream, line_normed, line_upstream)
    in_turns(plane_up, plane_gate, line_upstream, plane_up, line_upstream)
    finish(plane_gate, line_normed, plane_up, line_upstream)


def forward(n_ctx, n_fsdp, block, positions, own, w_query, kv, w_out, gains, w_gate, w_up, upstream, tables):
    rows, width = own.shape
    length = rows * n_ctx
    weight_rows = kv.shape[0]
    total = weight_rows * n_fsdp
    query_width, out_width = w_query.shape[1] // n_ctx, width // n_ctx
    ff_rows = w_gate.shape[1] // n_fsdp
    heads, kv_heads = query_width // HEAD_DIM, kv.shape[1] // (2 * HEAD_DIM)
    tile = block * (4 if length <= 1024 else 2)
    shape = jax.ShapeDtypeStruct
    return communicate(
        functools.partial(forward_kernel, n_ctx, n_fsdp, tile),
        1,
        "forward",
        (*positions, own, w_query, kv, w_out, gains, w_gate, w_up, upstream, *tables),
        [VMEM] * 2 + [ANY] * 8 + [VMEM] * 2,
        [
            shape((total, ff_rows), LOW),
            shape((total, ff_rows), LOW),
            shape((rows * n_fsdp, width), LOW),
            shape((total, query_width), LOW),
            shape((total, kv.shape[1]), LOW),
            shape((gains.shape[0] * n_fsdp, gains.shape[1]), jnp.float32),
            shape((total // n_ctx, width), LOW),
            shape((length, width), LOW),
            shape((heads, length, HEAD_DIM), LOW),
            shape((kv_heads, length, HEAD_DIM), LOW),
            shape((kv_heads, length, HEAD_DIM), LOW),
            shape((length, 128), jnp.float32),
            shape((length, query_width), LOW),
            shape((rows, width), jnp.float32),
            shape((rows * n_fsdp, width), LOW),
        ],
        [ANY] * 3 + [VMEM] * 12,
        [
            pltpu.VMEM((length, width), LOW),
            pltpu.VMEM((total, out_width), LOW),
            pltpu.VMEM((heads, length, HEAD_DIM), LOW),
            pltpu.VMEM((length, query_width + kv.shape[1]), LOW),
            pltpu.VMEM((length, width), LOW),
        ]
        + cube_scratch(n_ctx, rows, width)
        + [pltpu.SemaphoreType.DMA((8,))],
        5 * (n_ctx - 1) + 14 * (n_fsdp - 1) + 2 * (n_fsdp - 1),
        160,
    )


def backward_kernel(
    n_ctx,
    n_fsdp,
    tile,
    pos_row,
    pos_column,
    mlp_part,
    down_part,
    out_part,
    own,
    upstream,
    resid,
    gain_mlp,
    gain_attn,
    w_q,
    w_kv,
    w_out,
    cosine,
    sine,
    q_heads,
    k_head,
    v_head,
    logs,
    attended,
    down_all,
    grad_out,
    d_joined,
    d_own,
    output,
    terms,
    seq,
    d_resid,
    line_land,
    total,
    out_land,
    out_total,
    down_land,
    land,
    acc,
    joined,
    d_heads,
    dq_heads,
    dk_head,
    dv_head,
    local_sem,
    send_sems,
    recv_sems,
):
    links = Links(n_ctx, n_fsdp, send_sems, recv_sems)
    rows, down_rows = own.shape[0], down_all.shape[0] // n_ctx
    length, query_width, kv_width = seq.shape[0], w_q.shape[1], w_kv.shape[1] // 2
    tiles = length // tile
    links.greet(cube=True, line=True)
    line = line_sum(links, mlp_part, line_land, total, rows)
    summed_here = out_part.shape[0] > rows
    line_out = line_sum(links, out_part, out_land, out_total, rows) if summed_here else iter(())
    down_here = down_part.shape[0] > down_rows
    plane_down = cube_sum(links, down_part, down_land, acc, down_rows) if down_here else iter(())
    in_turns(line, plane_down, plane_down, line, line, plane_down)
    finish(line)
    d_normed = swap_order(total[...], n_ctx, n_fsdp)
    value = resid[...]
    scale = lax.rsqrt(jnp.mean(value * value, axis=1, keepdims=True) + EPS)
    unit = value * scale
    terms[1:2, :] = jnp.sum(d_normed * unit, axis=0, keepdims=True)
    value = upstream[...].astype(jnp.float32) + norm_back(d_normed, gain_mlp[...], unit, scale)
    d_resid[...] = value
    rows_of(seq, links.ctx, rows)[...] = value.astype(LOW)
    plane = cube_gather(links, seq, rows)
    in_turns(plane, line_out)
    finish(plane_down)
    if down_here:
        down_land[pl.ds(0, down_rows), :] = acc[pl.ds(0, down_rows), :].astype(LOW)
    down_low = down_land.at[pl.ds(0, down_rows)] if down_here else down_part
    mine = pltpu.make_async_copy(down_low, rows_of(down_all, links.ctx, down_rows), local_sem)
    mine.start()
    finish(plane)
    mine.wait()
    plane_all = cube_gather(links, down_all, down_rows)
    in_turns(plane_all, line_out)
    grad_rows = pl.ds(0, query_width)
    acc[grad_rows, :] = jnp.zeros((query_width, acc.shape[1]), jnp.float32)

    def begin(at, carry):
        here = pl.ds(pl.multiple_of(at * tile, tile), tile)
        mine = seq[here, :]
        acc[grad_rows, :] += dot_dims(attended[here, :], mine, 0, 0)
        joined[here, pl.ds(0, query_width)] = dot_dims(mine, w_out[...], 1, 1).astype(LOW)
        return carry

    lax.fori_loop(0, tiles, begin, 0)

    def sort(at, carry):
        here = pl.ds(pl.multiple_of(at * tile, tile), tile)
        moved = dot(to_positions(pos_row, at, tile), joined[:, pl.ds(0, query_width)]).astype(LOW)
        split_heads(moved, d_heads, here)
        return carry

    lax.fori_loop(0, tiles, sort, 0)
    grad_out[...] = acc[grad_rows, :].astype(LOW)
    services = [
        lambda: in_turns(line_out),
        lambda: in_turns(plane_all, line_out),
        lambda: in_turns(plane_all),
    ]

    def service():
        if services:
            services.pop(0)()

    attend_back(q_heads, k_head, v_head, d_heads, logs, dq_heads, dk_head, dv_head, tile, service)
    while services:
        service()

    def end(at, carry):
        here = pl.ds(pl.multiple_of(at * tile, tile), tile)
        cos, sin = cosine[here, :], sine[here, :]
        d_query = turned(side_by_side(dq_heads, here), cos, sin, True)
        joined[here, pl.ds(0, query_width)] = d_query.astype(LOW)
        both = jnp.concatenate([side_by_side(dk_head, here), side_by_side(dv_head, here)], axis=1)
        keys = lanes(both.shape) < kv_width
        both = jnp.where(keys, turned(both, cos, sin, True), both)
        joined[here, pl.ds(query_width, 2 * kv_width)] = both.astype(LOW)
        return carry

    lax.fori_loop(0, tiles, end, 0)

    def out(at, carry):
        here = pl.ds(pl.multiple_of(at * tile, tile), tile)
        moved = dot(to_slots(pos_column, here, tile), joined[...]).astype(LOW)
        d_joined[here, :] = moved
        both = dot_dims(moved[:, :query_width], w_q[...], 1, 1)
        both += dot_dims(moved[:, query_width:], w_kv[...], 1, 1)
        seq[here, :] = both.astype(LOW)
        return carry

    lax.fori_loop(0, tiles, out, 0)
    plane = cube_sum(links, seq, land, acc, rows)
    in_turns(plane)
    finish(line_out)
    out_sum = out_total[...] if summed_here else out_part[...].astype(jnp.float32)
    output[...] = (resid[...] + out_sum).astype(LOW)
    in_turns(plane, plane)
    finish(plane)
    d_normed = acc[pl.ds(0, rows), :]
    value = own[...].astype(jnp.float32)
    scale = lax.rsqrt(jnp.mean(value * value, axis=1, keepdims=True) + EPS)
    unit = value * scale
    terms[0:1, :] = jnp.sum(d_normed * unit, axis=0, keepdims=True)
    d_own[...] = (d_resid[...] + norm_back(d_normed, gain_attn[...], unit, scale)).astype(LOW)
    finish(plane_all)


def backward(
    n_ctx, n_fsdp, block, positions, parts, own, upstream, resid, gains, weights, tables, saved
):
    rows, width = own.shape
    length = rows * n_ctx
    down_here = length <= 1024
    down_rows = parts[1].shape[0] // (n_ctx if down_here else 1)
    q_heads, k_head = saved[0], saved[1]
    joined_width = weights[0].shape[1] + weights[1].shape[1]
    tile = block * (4 if length <= 1024 else 2)
    shape = jax.ShapeDtypeStruct
    wide = jnp.float32
    return communicate(
        functools.partial(backward_kernel, n_ctx, n_fsdp, tile),
        3,
        "backward",
        (*positions, *parts, own, upstream, resid, *gains, *weights, *tables, *saved),
        [VMEM] * 20,
        [
            shape((down_rows * n_ctx, width), LOW),
            shape((weights[0].shape[1], width), LOW),
            shape((length, joined_width), LOW),
            shape((rows, width), LOW),
            shape((rows, width), LOW),
            shape((2, width), wide),
        ],
        [ANY] + [VMEM] * 5,
        [pltpu.VMEM((length, width), LOW), pltpu.VMEM((rows, width), wide)]
        + line_scratch(n_fsdp, rows, width)
        + (line_scratch(n_fsdp, rows, width) if parts[2].shape[0] > rows else line_scratch(2, 8, 128))
        + (cube_scratch(n_ctx, down_rows, width)[:1] if down_here else cube_scratch(2, 16, 128)[:1])
        + cube_scratch(n_ctx, rows, width)[:1]
        + [
            pltpu.VMEM((max(max(1, n_ctx // 4) * max(rows, down_rows), weights[0].shape[1]), width), wide),
            pltpu.VMEM((length, joined_width), LOW),
            pltpu.VMEM(q_heads.shape, LOW),
            pltpu.VMEM(q_heads.shape, wide),
            pltpu.VMEM(k_head.shape, wide),
            pltpu.VMEM(k_head.shape, wide),
            pltpu.SemaphoreType.DMA(()),
        ],
        4 * (n_ctx - 1) + 4 * (n_fsdp - 1),
        160,
    )


def feed_forward_kernel(
    normed, upstream, w_gate, w_up, w_down, d_part, out_part, down, pair, flipped, d_acc, out_acc, held, sems
):
    at, steps = pl.program_id(0), pl.num_programs(0)
    chunk, ff_rows = w_gate.shape[1], pair.shape[1] // 2
    slot = lax.rem(at, 2)

    def leave(which, part, step):
        column = pl.multiple_of(part * ff_rows + step * chunk, chunk)
        return pltpu.make_async_copy(
            held.at[which, part], pair.at[:, pl.ds(column, chunk)], sems.at[which, part]
        )

    @pl.when(at == 0)
    def _():
        flipped[...] = normed[...].T
        d_acc[...] = jnp.zeros_like(d_acc)
        out_acc[...] = jnp.zeros_like(out_acc)

    gate_pre, up_pre = dot(normed[...], w_gate[...]), dot(normed[...], w_up[...])
    sigma = 1.0 / (1.0 + jnp.exp(-gate_pre))
    swish = gate_pre * sigma
    hidden = (swish * up_pre).astype(LOW)
    d_hidden = dot_dims(upstream[...], w_down[...], 1, 1)
    d_gate = (d_hidden * up_pre * sigma * (1.0 + gate_pre * (1.0 - sigma))).astype(LOW)
    d_up = (d_hidden * swish).astype(LOW)
    down[...] = dot_dims(hidden, upstream[...], 0, 0).astype(LOW)

    @pl.when(at >= 2)
    def _():
        for part in (0, 1):
            leave(slot, part, at - 2).wait()

    held[slot, 0] = dot(flipped[...], d_gate).astype(LOW)
    held[slot, 1] = dot(flipped[...], d_up).astype(LOW)
    for part in (0, 1):
        leave(slot, part, at).start()
    d_acc[...] += dot_dims(d_gate, w_gate[...], 1, 1) + dot_dims(d_up, w_up[...], 1, 1)
    out_acc[...] += dot(hidden, w_down[...])

    @pl.when(at == steps - 1)
    def _():
        d_part[...] = d_acc[...].astype(LOW)
        out_part[...] = out_acc[...].astype(LOW)

        @pl.when(steps > 1)
        def _():
            for part in (0, 1):
                leave(1 - slot, part, at - 1).wait()

        for part in (0, 1):
            leave(slot, part, at).wait()


def feed_forward(normed, upstream, w_gate, w_up, w_down):
    count, width = normed.shape
    ff_rows = w_down.shape[0]
    chunk = min(ff_rows, 512 if count <= 512 else 256)
    whole = pl.BlockSpec((count, width), lambda f: (0, 0), pipeline_mode=pl.Buffered(1))
    tall = pl.BlockSpec((width, chunk), lambda f: (0, f))
    flat = pl.BlockSpec((chunk, width), lambda f: (f, 0))
    shape = jax.ShapeDtypeStruct
    return pl.pallas_call(
        feed_forward_kernel,
        grid=(ff_rows // chunk,),
        in_specs=[whole, whole, tall, tall, flat],
        out_specs=[whole, whole, flat, ANY],
        out_shape=[
            shape((count, width), LOW),
            shape((count, width), LOW),
            shape((ff_rows, width), LOW),
            shape((width, 2 * ff_rows), LOW),
        ],
        scratch_shapes=[
            pltpu.VMEM((width, count), LOW),
            pltpu.VMEM((count, width), jnp.float32),
            pltpu.VMEM((count, width), jnp.float32),
            pltpu.VMEM((2, 2, width, chunk), LOW),
            pltpu.SemaphoreType.DMA((2, 2)),
        ],
        compiler_params=pltpu.CompilerParams(vmem_limit_bytes=60 << 20),
        cost_estimate=pl.CostEstimate(flops=0, bytes_accessed=150_000_000, transcendentals=0),
        name="feed_forward",
    )(normed, upstream, w_gate, w_up, w_down)


class ChunkSum:
    def __init__(self, links, land, rows):
        self.links, self.land, self.rows = links, land, rows
        self.count = links.n_ctx // 2
        self.levels = len(links.order) + 1
        self.offsets, self.theirs = [0], [0]
        for step, other in zip(links.order, links.order[::-1]):
            self.offsets = self.offsets + [offset + step for offset in self.offsets]
            self.theirs = self.theirs + [offset + other for offset in self.theirs]

    def first(self, level):
        return sum(self.count >> done for done in range(level))

    def spot(self, chunk, at):
        return pl.multiple_of((chunk * (self.links.n_ctx - 1) + at) * self.rows, self.rows)

    def transfer(self, part, chunk, level, at):
        links = self.links
        target = self.land.at[pl.ds(self.spot(chunk, self.first(level) + at), self.rows)]
        if level == 0:
            source = rows_of(part, links.ctx + links.sibling + self.theirs[at], self.rows)
            step = links.sibling
        else:
            source = self.land.at[pl.ds(self.spot(chunk, at + (self.count >> level)), self.rows)]
            step = links.order[len(links.order) - level]
        links.used = chunk * (links.n_ctx - 1) + self.first(level) + at
        return links.copy(source, target, links.ctx + step, links.fsdp)

    def start(self, part, chunk):
        for at in range(self.count):
            self.transfer(part, chunk, 0, at).start()

    def sent(self, part, chunk, level):
        for at in range(self.count >> level):
            self.transfer(part, chunk, level, at).wait_send()

    def meet(self, part, chunk, level, leave):
        count = self.count >> level
        half = count // 2
        wide = jnp.float32
        for at in list(range(half, count)) + list(range(half)):
            self.transfer(part, chunk, level, at).wait_recv()
            kept, landing = self.spot(chunk, at), self.spot(chunk, self.first(level) + at)

            def add(start, size):
                landed = self.land[pl.ds(pl.multiple_of(landing + start, size), size), :].astype(wide)
                place = pl.ds(pl.multiple_of(kept + start, size), size)
                if level == 0:
                    base = (self.links.ctx + self.offsets[at]) * self.rows
                    mine = part[pl.ds(pl.multiple_of(base + start, size), size), :]
                else:
                    mine = self.land[place, :]
                total = mine.astype(wide) + landed
                if count == 1:
                    leave(start, size, total)
                else:
                    self.land[place, :] = total.astype(LOW)

            in_rows(self.rows, add)
            if count > 1 and at >= half:
                self.transfer(part, chunk, level + 1, at - half).start()


def feed_forward_sum_kernel(
    n_ctx,
    n_fsdp,
    normed,
    upstream,
    w_gate,
    w_up,
    w_down,
    d_part,
    out_part,
    down,
    pair,
    flipped,
    d_acc,
    out_acc,
    held,
    land,
    local_sems,
    send_sems,
    recv_sems,
):
    at, steps = pl.program_id(0), w_down.shape[0]
    chunk, ff_rows, width = w_gate.shape[1], pair.shape[2], normed.shape[1]
    count, steps = normed.shape[0], pair.shape[2] // w_gate.shape[1]
    links = Links(n_ctx, n_fsdp, send_sems, recv_sems)
    sums = ChunkSum(links, land, width // n_ctx)
    slot, other = lax.rem(at, 2), lax.rem(at + 1, 2)
    last = sums.levels - 1

    def meet(step, level):
        part = held.at[lax.rem(step, 2)]
        column = pl.multiple_of(step * chunk, chunk)

        def leave(start, size, total):
            low = total.astype(LOW)
            for which in (0, 1):
                pair[which, pl.ds(start, size), pl.ds(column, chunk)] = low[:, which * chunk : (which + 1) * chunk]

        sums.meet(part, step, level, leave)

    @pl.when(at == 0)
    def _():
        links.greet(cube=True)
        flipped[...] = normed[...].T
        d_acc[...] = jnp.zeros_like(d_acc)
        out_acc[...] = jnp.zeros_like(out_acc)

    gate_pre, up_pre = dot(normed[...], w_gate[...]), dot(normed[...], w_up[...])
    sigma = 1.0 / (1.0 + jnp.exp(-gate_pre))
    swish = gate_pre * sigma
    hidden = (swish * up_pre).astype(LOW)
    d_hidden = dot_dims(upstream[...], w_down[...], 1, 1)
    d_gate = (d_hidden * up_pre * sigma * (1.0 + gate_pre * (1.0 - sigma))).astype(LOW)
    d_up = (d_hidden * swish).astype(LOW)

    @pl.when(at >= 1)
    def _():
        meet(at - 1, 0)

    @pl.when(at >= 2)
    def _():
        meet(at - 2, 1)
        sums.sent(held.at[slot], at - 2, 0)

    held[slot, :, pl.ds(0, chunk)] = dot(flipped[...], d_gate).astype(LOW)
    held[slot, :, pl.ds(chunk, chunk)] = dot(flipped[...], d_up).astype(LOW)
    sums.start(held.at[slot], at)
    down[...] = dot_dims(hidden, upstream[...], 0, 0).astype(LOW)
    d_acc[...] += dot_dims(d_gate, w_gate[...], 1, 1) + dot_dims(d_up, w_up[...], 1, 1)
    out_acc[...] += dot(hidden, w_down[...])
    for level in range(2, last + 1):

        @pl.when(at >= 2)
        def _():
            meet(at - 2, level)

    @pl.when(at == steps - 1)
    def _():
        meet(at, 0)
        meet(at - 1, 1)
        sums.sent(held.at[other], at - 1, 0)
        leaving = []
        for which, (acc, goal) in enumerate(((d_acc, d_part), (out_acc, out_part))):
            for piece in range(width // (2 * chunk)):
                spot = pl.ds((which * (width // (2 * chunk)) + piece) * count, count)
                columns = pl.ds(piece * 2 * chunk, 2 * chunk)
                held[other, spot, :] = acc[:, columns].astype(LOW)
                copy = pltpu.make_async_copy(
                    held.at[other, spot], goal.at[:, columns], local_sems.at[len(leaving)]
                )
                copy.start()
                leaving.append(copy)
        for level in range(2, last + 1):
            meet(at - 1, level)
        meet(at, 1)
        for level in range(2, last + 1):
            meet(at, level)
        sums.sent(held.at[slot], at, 0)
        for copy in leaving:
            copy.wait()
        for step in range(steps):
            for level in range(1, last + 1):
                sums.sent(held.at[0], step, level)


def feed_forward_sum(n_ctx, n_fsdp, normed, upstream, w_gate, w_up, w_down):
    count, width = normed.shape
    ff_rows = w_down.shape[0]
    chunk = 512
    steps, rows = ff_rows // chunk, width // n_ctx
    whole = pl.BlockSpec((count, width), lambda f: (0, 0), pipeline_mode=pl.Buffered(1))
    tall = pl.BlockSpec((width, chunk), lambda f: (0, f))
    flat = pl.BlockSpec((chunk, width), lambda f: (f, 0))
    both = pl.BlockSpec((2, rows, ff_rows), lambda f: (0, 0, 0), pipeline_mode=pl.Buffered(1))
    shape = jax.ShapeDtypeStruct
    copies = steps * (n_ctx - 1)
    return pl.pallas_call(
        functools.partial(feed_forward_sum_kernel, n_ctx, n_fsdp),
        grid=(steps,),
        in_specs=[whole, whole, tall, tall, flat],
        out_specs=[ANY, ANY, flat, both],
        out_shape=[
            shape((count, width), LOW),
            shape((count, width), LOW),
            shape((ff_rows, width), LOW),
            shape((2, rows, ff_rows), LOW),
        ],
        scratch_shapes=[
            pltpu.VMEM((width, count), LOW),
            pltpu.VMEM((count, width), jnp.float32),
            pltpu.VMEM((count, width), jnp.float32),
            pltpu.VMEM((2, width, 2 * chunk), LOW),
            pltpu.VMEM((copies * rows, 2 * chunk), LOW),
            pltpu.SemaphoreType.DMA((2 * width // (2 * chunk),)),
            pltpu.SemaphoreType.DMA((copies,)),
            pltpu.SemaphoreType.DMA((copies,)),
        ],
        compiler_params=pltpu.CompilerParams(
            collective_id=2, has_side_effects=True, vmem_limit_bytes=62 << 20
        ),
        name="feed_forward_sum",
    )(normed, upstream, w_gate, w_up, w_down)


def on_device(
    tokens,
    cotangent,
    pairing,
    norm_attn,
    w_query,
    w_key,
    w_value,
    w_out,
    norm_mlp,
    w_gate,
    w_up,
    w_down,
):
    n_ctx, n_fsdp = lax.axis_size("ctx"), lax.axis_size("fsdp")
    ctx = lax.axis_index("ctx")
    own_tokens = tokens[0]
    tok_rows, width = own_tokens.shape
    length = tok_rows * n_ctx
    rows_model = w_gate.shape[0]
    low = LOW

    query_width = w_query.shape[1] // n_ctx
    heads_kv = w_key.shape[1] // HEAD_DIM
    kv_here = max(1, heads_kv // n_ctx)
    sharers = max(1, n_ctx // heads_kv)
    kv_width = kv_here * HEAD_DIM
    kv_start = (ctx // sharers) * kv_width

    def columns(matrix, start, size):
        return lax.dynamic_slice_in_dim(matrix, start, size, 1)

    kv = jnp.concatenate([columns(w_key, kv_start, kv_width), columns(w_value, kv_start, kv_width)], axis=1)
    gains = jnp.zeros((8, rows_model), jnp.float32).at[0].set(norm_attn).at[1].set(norm_mlp)
    upstream = cotangent[0]
    block = tok_rows // pairing.shape[1]
    all_pos = slot_positions(pairing, length, block)
    positions = (all_pos[None, :], all_pos[:, None])

    def tables_at(places):
        return [jnp.tile(t[:, 0], (1, 128 // HEAD_DIM)) for t in rotation(places, HEAD_DIM)]

    (
        gate_full,
        up_full,
        upstream_all,
        w_q,
        w_kv,
        gains,
        w_out_rows,
        normed_attn,
        q_heads,
        k_head,
        v_head,
        logs,
        attended_low,
        resid,
        normed_mlp,
    ) = forward(
        n_ctx,
        n_fsdp,
        block,
        positions,
        own_tokens,
        w_query,
        kv,
        w_out,
        gains,
        w_gate,
        w_up,
        upstream,
        tables_at(all_pos),
    )
    gains = gains.reshape(n_fsdp, 8, rows_model)
    gain_attn, gain_mlp = gains[:, 0].reshape(1, -1), gains[:, 1].reshape(1, -1)
    out_width = width // n_ctx
    ff_rows = w_down.shape[0]
    strip = rows_model // n_ctx

    if length <= 1024:
        mlp_part, out_part, down_part, pair = feed_forward_sum(
            n_ctx, n_fsdp, normed_mlp, upstream_all, gate_full, up_full, w_down
        )
    else:
        mlp_part, out_part, down_part, pair = feed_forward(
            normed_mlp, upstream_all, gate_full, up_full, w_down
        )
        pair, down_part = scatter_sum(pair, "ctx"), scatter_sum(down_part, "ctx")
        pair = jnp.stack([pair[:, :ff_rows], pair[:, ff_rows:]])
        out_part = scatter_sum(out_part, "fsdp")

    grad_down, grad_out, d_joined, d_inputs, output, terms = backward(
        n_ctx,
        n_fsdp,
        block,
        positions,
        (mlp_part, down_part, out_part),
        own_tokens,
        upstream,
        resid,
        (gain_mlp, gain_attn),
        (w_q, w_kv, w_out_rows),
        tables_at(jnp.arange(length, dtype=jnp.int32)),
        (q_heads, k_head, v_head, logs, attended_low),
    )
    grad_joined = tokens_t(normed_attn, d_joined).astype(low)
    terms = terms.reshape(2, n_fsdp, rows_model)
    attn_width = query_width + 2 * kv_width + out_width
    pad = ((0, 0), (0, 14), (0, attn_width - rows_model))
    terms = jnp.pad(terms.transpose(1, 0, 2).astype(low), pad).reshape(n_fsdp * 16, attn_width)
    grad_gate, grad_up, grad_attn = tail(n_ctx, n_fsdp, pair, grad_joined, grad_out, terms)
    grad_attn = grad_attn.reshape(n_ctx, rows_model + 16, attn_width)
    terms = jnp.sum(grad_attn[:, rows_model : rows_model + 2, :rows_model].astype(jnp.float32), axis=0)
    grad_gate, grad_up, grad_down, grad_query, grad_key, grad_value, grad_out = widen(
        grad_attn,
        rows_model,
        (query_width, kv_width, kv_width, out_width),
        (1, sharers, sharers, 1),
        grad_gate,
        grad_up,
        grad_down,
    )
    return (
        output[None],
        d_inputs[None],
        terms[0],
        grad_query,
        grad_key,
        grad_value,
        grad_out,
        terms[1],
        grad_gate,
        grad_up,
        grad_down,
    )


def solution(mesh):
    return jax.shard_map(
        on_device,
        mesh=mesh,
        in_specs=(
            P("fsdp", "ctx", None),
            P("fsdp", "ctx", None),
            P(),
            P("fsdp"),
            P("fsdp", None),
            P("fsdp", None),
            P("fsdp", None),
            P("fsdp", None),
            P("fsdp"),
            P("fsdp", None),
            P("fsdp", None),
            P("fsdp", None),
        ),
        out_specs=(
            P("fsdp", "ctx", None),
            P("fsdp", "ctx", None),
            P("fsdp"),
            P("fsdp", None),
            P("fsdp", None),
            P("fsdp", None),
            P("fsdp", None),
            P("fsdp"),
            P("fsdp", None),
            P("fsdp", None),
            P("fsdp", None),
        ),
        check_vma=False,
    )
```
